32 devices in a mesh: grp: 4 (over x, core), loop: 8 (over z, y).
Axes of the slice: x: 2, y: 2, z: 4, core: 2. Of those that a mesh axis runs over, the one named last changes fastest.
Arguments:
- solid_temp: float32 [12, 256, 2048], P(None, 'grp', 'loop'), may hold values from -3 to 3
- kappa: float32 [12, 256, 2048], P(None, 'grp', 'loop'), may hold values from 0.5 to 1.5
- slope: float32 [12, 256, 2048], P(None, 'grp', 'loop'), may hold values from 0.02 to 0.25
- power: float32 [12, 256, 2048], P(None, 'grp', 'loop'), may hold values from 0.2 to 5
- coolant_temp: float32 [256, 2048], P('grp', 'loop'), may hold values from -4 to 4
- wall_coeff: float32 [256, 2048], P('grp', 'loop'), may hold values from 0.25 to 1
- channel_map: int32 [8, 256], P('loop'), may hold values from 0 to 255, each once within a row
- flow_dir: int32 [256], P('grp'), may hold values 0 or 1
- loop_link: int32 [256], replicated, may hold values from 0 to 255, each once
Outputs:
- solid_out: float32 [12, 256, 2048], P(None, 'grp', 'loop')
- coolant_out: float32 [256, 2048], P('grp', 'loop')
The draws below stay inside these ranges and needn't reach their ends.
Inputs may be any that keep to these rules, and one draw needn't show every extreme that they name: Each row of channel_map is a permutation of 0 to 255. loop_link is a permutation of 0 to 255.
All inputs are finite; a program needn't handle non-finite values. No bound on the sum of `flow_dir` on one device may be relied on, other than what follows from the above.
Results may differ from the reference program's by a relative error of at most 0.0001.
Values sent between devices are 32-bit elements; how exact they have to be, the bound alone decides.
No kernel may reach another device: no remote copies, remote signals or barrier semaphores. Data moves between devices by JAX's collectives and lax.ppermute only.
A program may use at most 64 MiB of HBM per device.

```python
import math
import jax
import jax.numpy as jnp
from jax import lax

DIE_X = 256
DIE_Y = 256
LAYERS = 12
STEPS = 2
NDIES = 8
NX = 2048


def plant(array, own_key, least, high):
    longest = array.shape.index(max(array.shape))
    spots = []
    for shift in (0, 1):
        where = [jax.random.randint(jax.random.fold_in(own_key, axis), (), 0, length) for axis, length in enumerate(array.shape)]
        where[longest] = (where[longest] + shift) % array.shape[longest]
        spots.append(tuple(where))
    return array.at[spots[0]].set(least).at[spots[1]].set(high)


def level_of(rng, dims, split, smallest, high):
    factor_of, own = 1.0, jax.random.fold_in(rng, 6)
    for axis_at, shards_of in split:
        draws = jnp.exp(jax.random.uniform(jax.random.fold_in(own, axis_at), (shards_of,), jnp.float32, smallest / len(split), high / len(split)))
        factor_of = factor_of * jnp.repeat(draws, dims[axis_at] // shards_of).reshape([-1 if axis == axis_at else 1 for axis in range(len(dims))])
    return factor_of


def normal_values(key, dims, width, most, pieces=(), kind=jnp.bfloat16):
    entries = width * jax.random.normal(key, dims, jnp.float32)
    if pieces:
        entries = entries * level_of(key, dims, pieces, -0.22, 0.18)
    return jnp.clip(entries, -most, most).astype(kind)


def setup_inputs(seed: int = 0) -> dict:
    splits = jax.random.split(jax.random.key(seed), 10)
    return {
        "solid_temp": normal_values(splits[0], (LAYERS, DIE_Y, NX), 1.0, 3.0, ((1, 4), (2, 8)), jnp.float32),
        "kappa": jnp.clip(jnp.exp(math.log(1.5) - 1.0986123 * jax.random.uniform(splits[1], (LAYERS, DIE_Y, NX), jnp.float32) ** level_of(splits[1], (LAYERS, DIE_Y, NX), ((1, 4), (2, 8)), -0.2, 0.2)), 0.5, 1.5),
        "slope": jnp.clip(0.02 + 0.23 * jax.random.uniform(splits[2], (LAYERS, DIE_Y, NX), jnp.float32) ** level_of(splits[2], (LAYERS, DIE_Y, NX), ((1, 4), (2, 8)), -0.2, 0.2), 0.02, 0.25),
        "power": jnp.clip(jnp.exp(math.log(5.0) - 3.218876 * jax.random.uniform(splits[3], (LAYERS, DIE_Y, NX), jnp.float32) ** level_of(splits[3], (LAYERS, DIE_Y, NX), ((1, 4), (2, 8)), -0.2, 0.2)), 0.2, 5.0),
        "coolant_temp": normal_values(splits[4], (DIE_Y, NX), 1.0, 4.0, ((0, 4), (1, 8)), jnp.float32),
        "wall_coeff": jnp.clip(jnp.exp(math.log(1.0) - 1.3862944 * jax.random.uniform(splits[5], (DIE_Y, NX), jnp.float32) ** level_of(splits[5], (DIE_Y, NX), ((0, 4), (1, 8)), -0.2, 0.2)), 0.25, 1.0),
        "channel_map": jax.vmap(lambda own: jax.random.permutation(own, DIE_Y))(jax.random.split(splits[6], NDIES)).reshape((NDIES, DIE_Y)).astype(jnp.int32),
        "flow_dir": plant((jax.random.randint(splits[7], (DIE_Y,), 0, 2) < 1).astype(jnp.int32), jax.random.fold_in(splits[7], 1), 0, 1),
        "loop_link": jax.random.permutation(splits[8], DIE_Y).astype(jnp.int32),
    }


time_step = 0.06
courant = 0.5
heat_gain = 0.5


def face_heat(temp, cond):
    flux_z = 0.5 * (cond[1:] + cond[:-1]) * (temp[1:] - temp[:-1])
    heat = jnp.pad(flux_z, ((0, 1), (0, 0), (0, 0))) - jnp.pad(flux_z, ((1, 0), (0, 0), (0, 0)))
    temp_next = jnp.roll(temp, -1, 2)
    cond_next = jnp.roll(cond, -1, 2)
    flux_x = 0.5 * (cond + cond_next) * (temp_next - temp)
    heat = heat + flux_x - jnp.roll(flux_x, 1, 2)
    flux_y = 0.5 * (cond[:, 1:, :] + cond[:, :-1, :]) * (temp[:, 1:, :] - temp[:, :-1, :])
    heat = heat + jnp.pad(flux_y, ((0, 0), (0, 1), (0, 0))) - jnp.pad(flux_y, ((0, 0), (1, 0), (0, 0)))
    return heat


def reference(solid_temp, kappa, slope, power, coolant_temp, wall_coeff, channel_map, flow_dir, loop_link):
    highest = lax.Precision.HIGHEST
    die_count = channel_map.shape[0]
    select = (channel_map[:, :, None] == jnp.arange(DIE_Y, dtype=jnp.int32)[None, None, :]).astype(jnp.float32)
    temp = solid_temp
    flow = coolant_temp
    for step_index in range(STEPS):
        top_plane = temp[0].reshape(DIE_Y, die_count, DIE_X)
        wall_temp = jnp.einsum("dcy,ydx->cdx", select, top_plane, precision=highest).reshape(DIE_Y, NX)
        flux = wall_coeff * (wall_temp - flow)
        sink = jnp.einsum("cdx,dcy->ydx", flux.reshape(DIE_Y, die_count, DIE_X), select, precision=highest).reshape(DIE_Y, NX)
        before = jnp.roll(flow, 1, 1).at[:, 0].set(flow[loop_link, NX - 1])
        after = jnp.roll(flow, -1, 1).at[:, NX - 1].set(flow[loop_link, 0])
        upstream = jnp.where(flow_dir[:, None] == 1, before, after)
        new_flow = flow - courant * (flow - upstream) + heat_gain * flux
        cond = kappa * (1.0 + slope * temp)
        heat = face_heat(temp, cond)
        temp = temp + time_step * (heat + power)
        temp = temp.at[0].add(-time_step * sink)
        flow = new_flow
    return temp, flow
```

```python
import jax
import jax.numpy as jnp
from jax import lax
from jax.experimental import pallas as pl
from jax.experimental.pallas import tpu as pltpu
from jax.sharding import PartitionSpec as P

time_step = 0.06
courant = 0.5
heat_gain = 0.5
TILE = 128
F32 = jnp.float32
BF16 = jnp.bfloat16


def split3(value):
    high = value.astype(BF16)
    rest = value - high.astype(F32)
    middle = rest.astype(BF16)
    low = (rest - middle.astype(F32)).astype(BF16)
    return high, middle, low


def pick(chooser, value, dims):
    total = None
    for part in split3(value):
        term = lax.dot_general(chooser, part, (dims, ((), ())), preferred_element_type=F32)
        total = term if total is None else total + term
    return total


def pick_rows(value, chooser):
    total = None
    for part in split3(value):
        term = lax.dot_general(part, chooser, (((1,), (0,)), ((), ())), preferred_element_type=F32)
        total = term if total is None else total + term
    return total


def one_hot(index_row, first, count):
    shape = (count, index_row.shape[1])
    here = lax.broadcasted_iota(jnp.int32, shape, 0) + first
    return jnp.where(index_row == here, 1.0, 0.0).astype(BF16)


def face(cond_a, cond_b, temp_a, temp_b):
    return 0.5 * (cond_a + cond_b) * (temp_b - temp_a)


def closed_heat(temp_ref, kappa_ref, slope_ref, emit):
    layers, rows, cols = temp_ref.shape
    lane = lax.broadcasted_iota(jnp.int32, (rows, cols), 1)
    row = lax.broadcasted_iota(jnp.int32, (rows, cols), 0)
    temp = temp_ref[0]
    cond = kappa_ref[0] * (1.0 + slope_ref[0] * temp)
    flux_below = None
    for z in range(layers):
        flux_x = face(cond, pltpu.roll(cond, cols - 1, 1), temp, pltpu.roll(temp, cols - 1, 1))
        flux_x = jnp.where(lane == cols - 1, 0.0, flux_x)
        heat = flux_x - pltpu.roll(flux_x, 1, 1)
        flux_y = face(cond, pltpu.roll(cond, rows - 1, 0), temp, pltpu.roll(temp, rows - 1, 0))
        flux_y = jnp.where(row == rows - 1, 0.0, flux_y)
        heat = heat + flux_y - pltpu.roll(flux_y, 1, 0)
        if flux_below is not None:
            heat = heat - flux_below
        if z + 1 < layers:
            temp_up = temp_ref[z + 1]
            cond_up = kappa_ref[z + 1] * (1.0 + slope_ref[z + 1] * temp_up)
            flux_below = face(cond, cond_up, temp, temp_up)
            heat = heat + flux_below
        emit(z, temp, cond, heat)
        if z + 1 < layers:
            temp, cond = temp_up, cond_up


def open_kernel(
    temp_ref, kappa_ref, slope_ref, power_ref, flow_ref, wall_ref, dir_ref,
    next_ref, ya_ref, yb_ref, share_ref, tmp_ref, row_ref,
):
    layers, rows, cols = temp_ref.shape
    group = lax.axis_index("grp")
    even = lax.rem(group, 2) == 0

    def emit(z, temp, cond, heat):
        next_ref[z] = temp + time_step * (heat + power_ref[z])

    closed_heat(temp_ref, kappa_ref, slope_ref, emit)
    for q, ref in enumerate((next_ref, temp_ref, kappa_ref, slope_ref)):
        for z in range(layers):
            first = ref[z, 0:1, :]
            last = ref[z, rows - 1 : rows, :]
            at = q * layers + z
            ya_ref[at : at + 1, :] = jnp.where(even, last, first)
            yb_ref[at : at + 1, :] = jnp.where(even, first, last)
    share_ref[0:rows, :] = flow_ref[...]
    share_ref[rows : 2 * rows, :] = wall_ref[...]
    lane = lax.broadcasted_iota(jnp.int32, (rows, TILE), 1)
    left = temp_ref[0, :, 0:TILE]
    right = temp_ref[0, :, cols - TILE : cols]
    tmp_ref[...] = jnp.zeros_like(tmp_ref)
    tmp_ref[0:rows, :] = jnp.where(lane == 0, left, pltpu.roll(right, 2, 1))
    turned = tmp_ref[...].T
    row_ref[...] = jnp.zeros_like(row_ref)
    row_ref[0:8, 0:TILE] = turned[0:8, :]
    row_ref[2:3, 0:rows] = dir_ref[...].astype(F32)
    share_ref[2 * rows :, :] = pltpu.roll(row_ref[...], group * rows, 1)


def edge_kernel(
    first_ref, temp_ref, kappa_ref, slope_ref, ya_ref, yb_ref, share_ref, map_ref,
    next_ref, yo_ref, sa_ref, sb_ref, fw_ref, crow_ref, strip_ref, small_ref,
):
    layers, rows, cols = temp_ref.shape
    span = 2 * rows + 8
    groups = share_ref.shape[0] // span
    group = lax.axis_index("grp")
    even = lax.rem(group, 2) == 0
    place_even = lax.rem(lax.axis_index("loop"), 2) == 0
    ya, yb = ya_ref[...], yb_ref[...]
    low, high = jnp.where(even, yb, ya), jnp.where(even, ya, yb)
    yo_ref[0 : 4 * layers, :] = low
    yo_ref[4 * layers :, :] = high
    low_open = jnp.where(group == 0, 0.0, 1.0)
    high_open = jnp.where(group == groups - 1, 0.0, 1.0)

    flow_all = jnp.concatenate([share_ref[i * span : i * span + rows, :] for i in range(groups)], 0)
    wall_all = jnp.concatenate(
        [share_ref[i * span + rows : i * span + 2 * rows, :] for i in range(groups)], 0
    )
    extra = share_ref[2 * rows : span, :]
    for i in range(1, groups):
        extra = extra + share_ref[i * span + 2 * rows : (i + 1) * span, :]
    chooser = one_hot(map_ref[...], group * rows - 8, rows + 16)
    both = pick(chooser, jnp.concatenate([flow_all, wall_all], 1), ((1,), (0,)))
    flow_y, wall_y = both[:, :cols], both[:, cols:]
    fw_ref[0:rows, :] = flow_y[8 : 8 + rows]
    fw_ref[rows:, :] = wall_y[8 : 8 + rows]
    sink = wall_y[8 : 8 + rows] * (temp_ref[0] - flow_y[8 : 8 + rows])
    temp_low, temp_high = yo_ref[layers : layers + 1, :], yo_ref[5 * layers : 5 * layers + 1, :]
    sink_low = wall_y[7:8] * (temp_low - flow_y[7:8])
    sink_high = wall_y[8 + rows : 9 + rows] * (temp_high - flow_y[8 + rows : 9 + rows])

    row = lax.broadcasted_iota(jnp.int32, (rows, cols), 0)
    lane = lax.broadcasted_iota(jnp.int32, (rows, TILE), 1)
    small_ref[...] = jnp.zeros_like(small_ref)
    lane1 = lax.broadcasted_iota(jnp.int32, (1, TILE), 1)
    for z in range(layers):
        temp, kappa, slope = temp_ref[z], kappa_ref[z], slope_ref[z]
        after = first_ref[z]
        edges = []
        for side, base, at, opened, sunk in (
            (0, 0, 0, low_open, sink_low),
            (1, 4 * layers, rows - 1, high_open, sink_high),
        ):
            temp_h = yo_ref[base + layers + z : base + layers + z + 1, :]
            cond_h = yo_ref[base + 2 * layers + z : base + 2 * layers + z + 1, :] * (
                1.0 + yo_ref[base + 3 * layers + z : base + 3 * layers + z + 1, :] * temp_h
            )
            temp_e = temp[at : at + 1]
            cond_e = kappa[at : at + 1] * (1.0 + slope[at : at + 1] * temp_e)
            flux = opened * face(cond_e, cond_h, temp_e, temp_h)
            halo = yo_ref[base + z : base + z + 1, :] - time_step * flux
            if z == 0:
                halo = halo - time_step * sunk
            yo_ref[base + z : base + z + 1, :] = halo
            edges.append(time_step * flux)
            corner = jnp.where(
                lane1 == 0,
                temp_h[:, 0:TILE],
                jnp.where(
                    lane1 == 1,
                    pltpu.roll(cond_h[:, 0:TILE], 1, 1),
                    jnp.where(
                        lane1 == 4,
                        pltpu.roll(temp_h[:, cols - TILE :], 5, 1),
                        pltpu.roll(cond_h[:, cols - TILE :], 6, 1),
                    ),
                ),
            )
            small_ref[16 * side + z : 16 * side + z + 1, :] = corner
        after = after + jnp.where(row == 0, edges[0], jnp.where(row == rows - 1, edges[1], 0.0))
        if z == 0:
            after = after - time_step * sink
        next_ref[z] = after
        packed = None
        for n, value in enumerate((after, temp, kappa, slope)):
            left = value[:, 0:TILE]
            right = pltpu.roll(value[:, cols - TILE :], n + 5, 1)
            left = pltpu.roll(left, n, 1) if n else left
            packed = left if packed is None else jnp.where(lane == n, left, packed)
            packed = jnp.where(lane == n + 4, right, packed)
        strip_ref[z * rows : (z + 1) * rows, :] = packed
    strips = strip_ref[...].T[0:8, :]
    corners = small_ref[...].T[0:8, :]

    lane_c = lax.broadcasted_iota(jnp.int32, (groups * rows, TILE), 1)
    right_flow = flow_all[:, cols - TILE :]
    pack = jnp.where(lane_c < 2, flow_all[:, 0:TILE], pltpu.roll(right_flow, 4, 1))
    pack = jnp.where(lane_c == 4, pltpu.roll(wall_all[:, 0:TILE], 4, 1), pack)
    pack = jnp.where(lane_c == 5, pltpu.roll(wall_all[:, cols - TILE :], 6, 1), pack)
    turned = pack.T
    flow_0, flow_1 = turned[0:1], turned[1:2]
    flow_m, flow_e = turned[2:3], turned[3:4]
    wall_0, wall_e = turned[4:5], turned[5:6]
    top = pick_rows(extra, one_hot(map_ref[...], 0, groups * rows))
    toward = extra[2:3]
    flux_0 = wall_0 * (top[0:1] - flow_0)
    flux_e = wall_e * (top[1:2] - flow_e)
    part_0 = (1.0 - courant) * flow_0 + courant * (1.0 - toward) * flow_1 + heat_gain * flux_0
    part_e = (1.0 - courant) * flow_e + courant * toward * flow_m + heat_gain * flux_e
    crow_ref[...] = jnp.zeros_like(crow_ref)
    crow_ref[0:1, :] = toward
    crow_ref[1:2, :] = flow_0
    crow_ref[2:3, :] = flow_e
    width = sa_ref.shape[1]
    channels = groups * rows
    for ref, pick_right in ((sa_ref, place_even), (sb_ref, jnp.logical_not(place_even))):
        ref[...] = jnp.zeros_like(ref)
        ref[0:4, :] = jnp.where(pick_right, strips[4:8], strips[0:4])
        ref[4:6, 0:TILE] = jnp.where(pick_right, corners[4:6], corners[0:2])
        ref[6:7, 0:channels] = jnp.where(pick_right, flow_e, flow_0)
        ref[7:8, 0:channels] = jnp.where(pick_right, part_e, part_0)


def close_kernel(
    temp_ref, kappa_ref, slope_ref, power_ref, top_ref, yo_ref, ra_ref, rb_ref, sa_ref, sb_ref,
    fw_ref, crow_ref, map_ref, link_ref,
    out_ref, flow_ref, wide_ref, xt_ref, xc_ref, xf_ref, full_ref,
):
    layers, rows, cols = temp_ref.shape
    group, groups = lax.axis_index("grp"), lax.axis_size("grp")
    place, places = lax.axis_index("loop"), lax.axis_size("loop")
    even = lax.rem(place, 2) == 0
    channels = crow_ref.shape[1]
    low_open = jnp.where(group == 0, 0.0, 1.0)
    high_open = jnp.where(group == groups - 1, 0.0, 1.0)
    got_a, got_b, own_a, own_b = ra_ref[...], rb_ref[...], sa_ref[...], sb_ref[...]
    got = (jnp.where(even, got_b, got_a), jnp.where(even, got_a, got_b))
    own = (jnp.where(even, own_b, own_a), jnp.where(even, own_a, own_b))

    def turn(first, last, ref):
        wide_ref[0:1, 0 : first.shape[1]] = first
        wide_ref[TILE - 1 : TILE, 0 : last.shape[1]] = last
        ref[...] = wide_ref[:, 0 : ref.shape[0]].T

    wide_ref[...] = jnp.zeros_like(wide_ref)
    temps, conds, fluxes = [], [], []
    for side in range(2):
        temp_n, temp_o = got[side][1:2], own[side][1:2]
        cond_n = got[side][2:3] * (1.0 + got[side][3:4] * temp_n)
        cond_o = own[side][2:3] * (1.0 + own[side][3:4] * temp_o)
        flux = time_step * face(cond_o, cond_n, temp_o, temp_n)
        after = got[side][0:1] - flux
        temps.append(after)
        conds.append(got[side][2:3] * (1.0 + got[side][3:4] * after))
        fluxes.append(flux)
    turn(temps[0], temps[1], xt_ref)
    turn(conds[0], conds[1], xc_ref)
    turn(fluxes[0], fluxes[1], xf_ref)

    wide_ref[0:1, 0:TILE] = got[0][4:5, 0:TILE]
    wide_ref[TILE - 1 : TILE, 0:TILE] = got[1][4:5, 0:TILE]
    corner_t = wide_ref[:, 0:TILE].T
    wide_ref[0:1, 0:TILE] = got[0][5:6, 0:TILE]
    wide_ref[TILE - 1 : TILE, 0:TILE] = got[1][5:6, 0:TILE]
    corner_c = wide_ref[:, 0:TILE].T
    lane_l = lax.broadcasted_iota(jnp.int32, (layers, TILE), 1)
    halo = []
    for side in range(2):
        base = 4 * layers * side
        after = yo_ref[base : base + layers, :]
        before = yo_ref[base + layers : base + 2 * layers, :]
        kappa = yo_ref[base + 2 * layers : base + 3 * layers, :]
        slope = yo_ref[base + 3 * layers : base + 4 * layers, :]
        cond = kappa * (1.0 + slope * before)
        c_t, c_c = corner_t[16 * side : 16 * side + layers], corner_c[16 * side : 16 * side + layers]
        tiles = []
        for start, at in ((0, 0), (cols - TILE, TILE - 1)):
            flux = time_step * face(
                cond[:, start : start + TILE], c_c, before[:, start : start + TILE], c_t
            )
            tiles.append(after[:, start : start + TILE] + jnp.where(lane_l == at, flux, 0.0))
        after = jnp.concatenate([tiles[0], after[:, TILE : cols - TILE], tiles[1]], 1) if (
            cols > 2 * TILE
        ) else jnp.concatenate(tiles, 1)
        halo.append((after, kappa * (1.0 + slope * after)))

    lane = lax.broadcasted_iota(jnp.int32, (rows, TILE), 1)
    for z in range(layers):
        add = xf_ref[z * rows : (z + 1) * rows, :]
        full_ref[z] = temp_ref[z]
        full_ref[z, :, 0:TILE] = temp_ref[z, :, 0:TILE] + jnp.where(lane == 0, add, 0.0)
        full_ref[z, :, cols - TILE :] = temp_ref[z, :, cols - TILE :] + jnp.where(
            lane == TILE - 1, add, 0.0
        )

    toward_c = crow_ref[0:1, :]
    first_place = place == 0
    last_place = place == places - 1
    link = one_hot(link_ref[...], 0, channels)
    stack = jnp.concatenate(
        [got[0][6:7, 0:channels], got[1][6:7, 0:channels], crow_ref[1:3, :], crow_ref[4:8, :]], 0
    )
    moved = pick_rows(stack, link)
    own_0 = jnp.where(first_place, moved[2:3], stack[2:3])
    own_e = jnp.where(last_place, moved[3:4], stack[3:4])
    late_l = got[0][7:8, 0:channels] + courant * (1.0 - toward_c) * own_0
    late_r = got[1][7:8, 0:channels] + courant * toward_c * own_e
    late = jnp.concatenate([late_l, late_r, crow_ref[2:8, :]], 0)
    late_moved = pick_rows(late, link)
    edge_rows = (
        (jnp.where(first_place, moved[0:1], stack[0:1]), jnp.where(last_place, moved[1:2], stack[1:2])),
        (jnp.where(first_place, late_moved[0:1], late_l), jnp.where(last_place, late_moved[1:2], late_r)),
    )
    chooser = one_hot(map_ref[...], group * rows, rows)
    wide_row = lax.broadcasted_iota(jnp.int32, (TILE, channels), 0)
    edge_y = [
        pick(chooser, jnp.where(wide_row == 0, pair[0], pair[1]), ((1,), (1,))) for pair in edge_rows
    ]
    toward = pick(chooser, jnp.broadcast_to(toward_c, (TILE, channels)), ((1,), (1,)))
    toward = jnp.concatenate([toward] * (cols // TILE), 1) > 0.5
    lane_w = lax.broadcasted_iota(jnp.int32, (rows, cols), 1)

    def upstream(flow, edge):
        edges = jnp.concatenate([edge] * (cols // TILE), 1)
        before = jnp.where(lane_w == 0, edges, pltpu.roll(flow, 1, 1))
        after = jnp.where(lane_w == cols - 1, edges, pltpu.roll(flow, cols - 1, 1))
        return jnp.where(toward, before, after)

    flow, wall = fw_ref[0:rows, :], fw_ref[rows:, :]
    flux = wall * (top_ref[0] - flow)
    flow = flow - courant * (flow - upstream(flow, edge_y[0])) + heat_gain * flux
    flux = wall * (full_ref[0] - flow)
    flow_ref[...] = flow - courant * (flow - upstream(flow, edge_y[1])) + heat_gain * flux

    row8 = lax.broadcasted_iota(jnp.int32, (8, cols), 0)

    def emit(z, temp, cond, heat):
        result = temp + time_step * (heat + power_ref[z])
        if z == 0:
            result = result - time_step * flux
        halo_t = xt_ref[z * rows : (z + 1) * rows, :]
        halo_c = xc_ref[z * rows : (z + 1) * rows, :]
        sides = []
        for start, at in ((0, 0), (cols - TILE, TILE - 1)):
            part = slice(start, start + TILE)
            extra = time_step * face(cond[:, part], halo_c, temp[:, part], halo_t)
            sides.append(jnp.where(lane == at, extra, 0.0))
        middle = [jnp.zeros((rows, cols - 2 * TILE), F32)] if cols > 2 * TILE else []
        result = result + jnp.concatenate([sides[0]] + middle + [sides[1]], 1)
        out_ref[z] = result
        for side, opened, start, at in ((0, low_open, 0, 0), (1, high_open, rows - 8, 7)):
            part = slice(start, start + 8)
            extra = (time_step * opened) * face(
                cond[part], halo[side][1][z : z + 1], temp[part], halo[side][0][z : z + 1]
            )
            out_ref[z, part, :] = result[part] + jnp.where(row8 == at, extra, 0.0)

    closed_heat(full_ref, kappa_ref, slope_ref, emit)


def return_kernel(flow_ref, map_ref, out_ref, tmp_ref):
    rows = out_ref.shape[0]
    group = lax.axis_index("grp")
    chooser = one_hot(map_ref[...], 0, flow_ref.shape[0])
    tmp_ref[...] = pick(chooser, flow_ref[...], ((0,), (0,)))
    out_ref[...] = tmp_ref[pl.ds(pl.multiple_of(group * rows, 8), rows), :]


def pairs(count, first, closed):
    swaps = []
    for low in range(first, count, 2):
        high = low + 1
        if high == count:
            if not closed:
                continue
            high = 0
        swaps += [(low, high), (high, low)]
    return swaps


def shards(
    solid_temp, kappa, slope, power, coolant_temp, wall_coeff, channel_map, flow_dir, loop_link
):
    groups, places = lax.axis_size("grp"), lax.axis_size("loop")
    layers, rows, cols = solid_temp.shape
    channels = groups * rows
    strip = layers * rows
    params = pltpu.CompilerParams(vmem_limit_bytes=48 * 1024 * 1024)

    def shape(*dims):
        return jax.ShapeDtypeStruct(dims, F32)

    def call(body, outs, scratch, *args):
        return pl.pallas_call(
            body,
            out_shape=outs,
            scratch_shapes=[pltpu.VMEM(dims, F32) for dims in scratch],
            compiler_params=params,
        )(*args)

    link = loop_link.reshape(1, channels)
    first, ya, yb, share = call(
        open_kernel,
        (shape(layers, rows, cols), shape(4 * layers, cols), shape(4 * layers, cols), shape(2 * rows + 8, cols)),
        [(TILE, TILE), (8, cols)],
        solid_temp, kappa, slope, power, coolant_temp, wall_coeff, flow_dir.reshape(1, rows),
    )
    ya = lax.ppermute(ya, "grp", pairs(groups, 0, False))
    yb = lax.ppermute(yb, "grp", pairs(groups, 1, False))
    share = lax.all_gather(share, "grp", axis=0, tiled=True)
    after, yo, sa, sb, fw, crow = call(
        edge_kernel,
        (
            shape(layers, rows, cols), shape(8 * layers, cols), shape(8, strip), shape(8, strip),
            shape(2 * rows, cols), shape(8, channels),
        ),
        [(strip, TILE), (TILE, TILE)],
        first, solid_temp, kappa, slope, ya, yb, share, channel_map,
    )
    ra = lax.ppermute(sa, "loop", pairs(places, 0, True))
    rb = lax.ppermute(sb, "loop", pairs(places, 1, True))
    temp, flow = call(
        close_kernel,
        (shape(layers, rows, cols), shape(rows, cols)),
        [(TILE, strip), (strip, TILE), (strip, TILE), (strip, TILE), (layers, rows, cols)],
        after, kappa, slope, power, solid_temp[0:1], yo, ra, rb, sa, sb, fw, crow, channel_map, link,
    )
    flow = lax.all_gather(flow, "grp", axis=0, tiled=True)
    flow = call(return_kernel, shape(rows, cols), [(channels, cols)], flow, channel_map)
    return (temp, flow)


def solution(mesh):
    block = P(None, "grp", "loop")
    plane = P("grp", "loop")
    return jax.shard_map(
        shards,
        mesh=mesh,
        in_specs=(block, block, block, block, plane, plane, P("loop", None), P("grp"), P()),
        out_specs=(block, plane),
        check_vma=False,
    )
```

```python
import jax
import jax.numpy as jnp
from jax import lax
from jax.experimental import pallas as pl
from jax.experimental.pallas import tpu as pltpu
from jax.sharding import PartitionSpec as P

time_step = 0.06
courant = 0.5
heat_gain = 0.5
TILE = 128
CHUNK = 2
F32 = jnp.float32
BF16 = jnp.bfloat16


def split3(value):
    high = value.astype(BF16)
    rest = value - high.astype(F32)
    middle = rest.astype(BF16)
    low = (rest - middle.astype(F32)).astype(BF16)
    return high, middle, low


def pick(chooser, value, dims):
    total = None
    for part in split3(value):
        term = lax.dot_general(chooser, part, (dims, ((), ())), preferred_element_type=F32)
        total = term if total is None else total + term
    return total


def pick_rows(value, chooser):
    total = None
    for part in split3(value):
        term = lax.dot_general(part, chooser, (((1,), (0,)), ((), ())), preferred_element_type=F32)
        total = term if total is None else total + term
    return total


def one_hot(index_row, first, count):
    shape = (count, index_row.shape[1])
    here = lax.broadcasted_iota(jnp.int32, shape, 0) + first
    return jnp.where(index_row == here, 1.0, 0.0).astype(BF16)


def face(cond_a, cond_b, temp_a, temp_b):
    return 0.5 * (cond_a + cond_b) * (temp_b - temp_a)


def closed_heat(temp_ref, kappa_ref, slope_ref, emit, ready=lambda z: None):
    layers, rows, cols = temp_ref.shape
    lane = lax.broadcasted_iota(jnp.int32, (rows, cols), 1)
    row = lax.broadcasted_iota(jnp.int32, (rows, cols), 0)
    ready(0)
    temp = temp_ref[0]
    cond = kappa_ref[0] * (1.0 + slope_ref[0] * temp)
    flux_below = None
    for z in range(layers):
        if z + 1 < layers:
            ready(z + 1)
        flux_x = face(cond, pltpu.roll(cond, cols - 1, 1), temp, pltpu.roll(temp, cols - 1, 1))
        flux_x = jnp.where(lane == cols - 1, 0.0, flux_x)
        heat = flux_x - pltpu.roll(flux_x, 1, 1)
        flux_y = face(cond, pltpu.roll(cond, rows - 1, 0), temp, pltpu.roll(temp, rows - 1, 0))
        flux_y = jnp.where(row == rows - 1, 0.0, flux_y)
        heat = heat + flux_y - pltpu.roll(flux_y, 1, 0)
        if flux_below is not None:
            heat = heat - flux_below
        if z + 1 < layers:
            temp_up = temp_ref[z + 1]
            cond_up = kappa_ref[z + 1] * (1.0 + slope_ref[z + 1] * temp_up)
            flux_below = face(cond, cond_up, temp, temp_up)
            heat = heat + flux_below
        emit(z, temp, cond, heat)
        if z + 1 < layers:
            temp, cond = temp_up, cond_up


def open_kernel(
    temp_hbm, kappa_hbm, slope_hbm, power_hbm, flow_hbm, wall_hbm, dir_hbm, map_hbm, link_hbm,
    next_ref, temp_ref, kappa_ref, slope_ref, power_ref, ya_ref, yb_ref, share_ref, map_ref, link_ref,
    tmp_ref, row_ref, dir_ref, block_sem, small_sem,
):
    layers, rows, cols = temp_ref.shape
    group = lax.axis_index("grp")
    even = lax.rem(group, 2) == 0
    blocks = []
    for z in range(0, layers, CHUNK):
        part = pl.ds(z, CHUNK)
        blocks.append([
            pltpu.make_async_copy(source.at[part], target.at[part], block_sem.at[n, z // CHUNK])
            for n, (source, target) in enumerate((
                (temp_hbm, temp_ref), (kappa_hbm, kappa_ref), (slope_hbm, slope_ref), (power_hbm, power_ref),
            ))
        ])
    smalls = [
        pltpu.make_async_copy(source, target, small_sem.at[n])
        for n, (source, target) in enumerate((
            (flow_hbm, share_ref.at[0:rows]), (wall_hbm, share_ref.at[rows : 2 * rows]),
            (dir_hbm, dir_ref), (map_hbm, map_ref), (link_hbm, link_ref),
        ))
    ]
    for block in blocks:
        for copy in block:
            copy.start()
    for copy in smalls:
        copy.start()

    def ready(z):
        if z % CHUNK == 0:
            for copy in blocks[z // CHUNK]:
                copy.wait()

    def emit(z, temp, cond, heat):
        next_ref[z] = temp + time_step * (heat + power_ref[z])
        if z == 0:
            lane = lax.broadcasted_iota(jnp.int32, (rows, TILE), 1)
            packed = jnp.where(lane == 0, temp[:, 0:TILE], pltpu.roll(temp[:, cols - TILE :], 2, 1))
            packed = jnp.where(lane == 3, pltpu.roll(cond[:, 0:TILE], 3, 1), packed)
            packed = jnp.where(lane == 4, pltpu.roll(cond[:, cols - TILE :], 5, 1), packed)
            tmp_ref[...] = jnp.zeros_like(tmp_ref)
            tmp_ref[0:rows, :] = packed

    closed_heat(temp_ref, kappa_ref, slope_ref, emit, ready)
    for q, ref in enumerate((next_ref, temp_ref, kappa_ref, slope_ref)):
        for z in range(layers):
            first = ref[z, 0:1, :]
            last = ref[z, rows - 1 : rows, :]
            at = q * layers + z
            ya_ref[at : at + 1, :] = jnp.where(even, last, first)
            yb_ref[at : at + 1, :] = jnp.where(even, first, last)
    for copy in smalls:
        copy.wait()
    row_ref[...] = jnp.zeros_like(row_ref)
    row_ref[0:8, 0:TILE] = tmp_ref[...].T[0:8, :]
    row_ref[2:3, 0:rows] = dir_ref[...].astype(F32)
    share_ref[2 * rows :, :] = pltpu.roll(row_ref[...], group * rows, 1)


def edge_kernel(
    first_ref, temp_ref, kappa_ref, slope_ref, ya_ref, yb_ref, share_ref, map_ref,
    next_ref, yo_ref, sa_ref, sb_ref, fw_ref, crow_ref, flow_ref, strip_ref, small_ref,
):
    layers, rows, cols = temp_ref.shape
    span = 2 * rows + 8
    groups = share_ref.shape[0] // span
    group = lax.axis_index("grp")
    even = lax.rem(group, 2) == 0
    place_even = lax.rem(lax.axis_index("loop"), 2) == 0
    ya, yb = ya_ref[...], yb_ref[...]
    low, high = jnp.where(even, yb, ya), jnp.where(even, ya, yb)
    yo_ref[0 : 4 * layers, :] = low
    yo_ref[4 * layers :, :] = high
    low_open = jnp.where(group == 0, 0.0, 1.0)
    high_open = jnp.where(group == groups - 1, 0.0, 1.0)

    flow_all = jnp.concatenate([share_ref[i * span : i * span + rows, :] for i in range(groups)], 0)
    wall_all = jnp.concatenate(
        [share_ref[i * span + rows : i * span + 2 * rows, :] for i in range(groups)], 0
    )
    extra = share_ref[2 * rows : span, :]
    for i in range(1, groups):
        extra = extra + share_ref[i * span + 2 * rows : (i + 1) * span, :]
    chooser = one_hot(map_ref[...], group * rows - 8, rows + 16)
    both = pick(chooser, jnp.concatenate([flow_all, wall_all], 1), ((1,), (0,)))
    flow_y, wall_y = both[:, :cols], both[:, cols:]
    flow, wall = flow_y[8 : 8 + rows], wall_y[8 : 8 + rows]
    sink = wall * (temp_ref[0] - flow)
    temp_low, temp_high = yo_ref[layers : layers + 1, :], yo_ref[5 * layers : 5 * layers + 1, :]
    sink_low = wall_y[7:8] * (temp_low - flow_y[7:8])
    sink_high = wall_y[8 + rows : 9 + rows] * (temp_high - flow_y[8 + rows : 9 + rows])

    row = lax.broadcasted_iota(jnp.int32, (rows, cols), 0)
    lane = lax.broadcasted_iota(jnp.int32, (rows, TILE), 1)
    small_ref[...] = jnp.zeros_like(small_ref)
    lane1 = lax.broadcasted_iota(jnp.int32, (1, TILE), 1)
    for z in range(layers):
        temp, kappa, slope = temp_ref[z], kappa_ref[z], slope_ref[z]
        after = first_ref[z]
        edges = []
        for side, base, at, opened, sunk in (
            (0, 0, 0, low_open, sink_low),
            (1, 4 * layers, rows - 1, high_open, sink_high),
        ):
            temp_h = yo_ref[base + layers + z : base + layers + z + 1, :]
            cond_h = yo_ref[base + 2 * layers + z : base + 2 * layers + z + 1, :] * (
                1.0 + yo_ref[base + 3 * layers + z : base + 3 * layers + z + 1, :] * temp_h
            )
            temp_e = temp[at : at + 1]
            cond_e = kappa[at : at + 1] * (1.0 + slope[at : at + 1] * temp_e)
            flux = opened * face(cond_e, cond_h, temp_e, temp_h)
            halo = yo_ref[base + z : base + z + 1, :] - time_step * flux
            if z == 0:
                halo = halo - time_step * sunk
            yo_ref[base + z : base + z + 1, :] = halo
            edges.append(time_step * flux)
            corner = jnp.where(
                lane1 == 0,
                temp_h[:, 0:TILE],
                jnp.where(
                    lane1 == 1,
                    pltpu.roll(cond_h[:, 0:TILE], 1, 1),
                    jnp.where(
                        lane1 == 4,
                        pltpu.roll(temp_h[:, cols - TILE :], 5, 1),
                        pltpu.roll(cond_h[:, cols - TILE :], 6, 1),
                    ),
                ),
            )
            small_ref[16 * side + z : 16 * side + z + 1, :] = corner
        after = after + jnp.where(row == 0, edges[0], jnp.where(row == rows - 1, edges[1], 0.0))
        if z == 0:
            after = after - time_step * sink
        next_ref[z] = after
        packed = None
        for n, value in enumerate((after, temp, kappa, slope)):
            left = value[:, 0:TILE]
            right = pltpu.roll(value[:, cols - TILE :], n + 5, 1)
            left = pltpu.roll(left, n, 1) if n else left
            packed = left if packed is None else jnp.where(lane == n, left, packed)
            packed = jnp.where(lane == n + 4, right, packed)
        strip_ref[z * rows : (z + 1) * rows, :] = packed
    toward_y = pick(chooser[8 : 8 + rows], jnp.broadcast_to(extra[2:3], (TILE, groups * rows)), ((1,), (1,)))
    toward_y = jnp.concatenate([toward_y] * (cols // TILE), 1) > 0.5
    lane_w = lax.broadcasted_iota(jnp.int32, (rows, cols), 1)

    def upstream(values):
        before = jnp.where(lane_w == 0, 0.0, pltpu.roll(values, 1, 1))
        after = jnp.where(lane_w == cols - 1, 0.0, pltpu.roll(values, cols - 1, 1))
        return jnp.where(toward_y, before, after)

    flow = flow - courant * (flow - upstream(flow)) + heat_gain * sink
    fw_ref[0:rows, :] = flow
    fw_ref[rows:, :] = wall
    flux = wall * (next_ref[0] - flow)
    flow_ref[...] = flow - courant * (flow - upstream(flow)) + heat_gain * flux

    strips = strip_ref[...].T[0:8, :]
    corners = small_ref[...].T[0:8, :]

    lane_c = lax.broadcasted_iota(jnp.int32, (groups * rows, TILE), 1)
    right_flow = flow_all[:, cols - TILE :]
    pack = jnp.where(lane_c < 2, flow_all[:, 0:TILE], pltpu.roll(right_flow, 4, 1))
    pack = jnp.where(lane_c == 4, pltpu.roll(wall_all[:, 0:TILE], 4, 1), pack)
    pack = jnp.where(lane_c == 5, pltpu.roll(wall_all[:, cols - TILE :], 6, 1), pack)
    turned = pack.T
    flow_0, flow_1 = turned[0:1], turned[1:2]
    flow_m, flow_e = turned[2:3], turned[3:4]
    wall_0, wall_e = turned[4:5], turned[5:6]
    top = pick_rows(extra, one_hot(map_ref[...], 0, groups * rows))
    toward = extra[2:3]
    flux_0 = wall_0 * (top[0:1] - flow_0)
    flux_e = wall_e * (top[1:2] - flow_e)
    part_0 = (1.0 - courant) * flow_0 + courant * (1.0 - toward) * flow_1 + heat_gain * flux_0
    part_e = (1.0 - courant) * flow_e + courant * toward * flow_m + heat_gain * flux_e
    crow_ref[...] = jnp.zeros_like(crow_ref)
    crow_ref[0:1, :] = toward
    crow_ref[1:2, :] = flow_0
    crow_ref[2:3, :] = flow_e
    crow_ref[3:4, :] = wall_0
    crow_ref[4:5, :] = wall_e
    channels = groups * rows
    for ref, pick_right in ((sa_ref, place_even), (sb_ref, jnp.logical_not(place_even))):
        ref[...] = jnp.zeros_like(ref)
        ref[0:4, :] = jnp.where(pick_right, strips[4:8], strips[0:4])
        ref[4:6, 0:TILE] = jnp.where(pick_right, corners[4:6], corners[0:2])
        ref[4:5, channels : 2 * channels] = jnp.where(pick_right, extra[1:2], extra[0:1])
        ref[5:6, channels : 2 * channels] = jnp.where(pick_right, extra[4:5], extra[3:4])
        ref[6:7, 0:channels] = jnp.where(pick_right, flow_e, flow_0)
        ref[7:8, 0:channels] = jnp.where(pick_right, part_e, part_0)


def close_kernel(
    temp_ref, kappa_ref, slope_ref, power_ref, yo_ref, ra_ref, rb_ref, sa_ref, sb_ref,
    fw_ref, crow_ref, map_ref, link_ref, all_ref,
    out_hbm, flow_hbm, wide_ref, xt_ref, xc_ref, xf_ref, full_ref, out_ref, flow_ref, sel_ref, turn_ref, out_sem,
):
    layers, rows, cols = temp_ref.shape
    group, groups = lax.axis_index("grp"), lax.axis_size("grp")
    place, places = lax.axis_index("loop"), lax.axis_size("loop")
    even = lax.rem(place, 2) == 0
    channels = crow_ref.shape[1]
    low_open = jnp.where(group == 0, 0.0, 1.0)
    high_open = jnp.where(group == groups - 1, 0.0, 1.0)
    got_a, got_b, own_a, own_b = ra_ref[...], rb_ref[...], sa_ref[...], sb_ref[...]
    got = (jnp.where(even, got_b, got_a), jnp.where(even, got_a, got_b))
    own = (jnp.where(even, own_b, own_a), jnp.where(even, own_a, own_b))

    def turn(first, last, ref):
        wide_ref[0:1, 0 : first.shape[1]] = first
        wide_ref[TILE - 1 : TILE, 0 : last.shape[1]] = last
        ref[...] = wide_ref[:, 0 : ref.shape[0]].T

    wide_ref[...] = jnp.zeros_like(wide_ref)
    temps, conds, fluxes = [], [], []
    for side in range(2):
        temp_n, temp_o = got[side][1:2], own[side][1:2]
        cond_n = got[side][2:3] * (1.0 + got[side][3:4] * temp_n)
        cond_o = own[side][2:3] * (1.0 + own[side][3:4] * temp_o)
        flux = time_step * face(cond_o, cond_n, temp_o, temp_n)
        after = got[side][0:1] - flux
        temps.append(after)
        conds.append(got[side][2:3] * (1.0 + got[side][3:4] * after))
        fluxes.append(flux)
    turn(temps[0], temps[1], xt_ref)
    turn(conds[0], conds[1], xc_ref)
    turn(fluxes[0], fluxes[1], xf_ref)

    wide_ref[0:1, 0:TILE] = got[0][4:5, 0:TILE]
    wide_ref[TILE - 1 : TILE, 0:TILE] = got[1][4:5, 0:TILE]
    corner_t = wide_ref[:, 0:TILE].T
    wide_ref[0:1, 0:TILE] = got[0][5:6, 0:TILE]
    wide_ref[TILE - 1 : TILE, 0:TILE] = got[1][5:6, 0:TILE]
    corner_c = wide_ref[:, 0:TILE].T
    lane_l = lax.broadcasted_iota(jnp.int32, (layers, TILE), 1)
    halo = []
    for side in range(2):
        base = 4 * layers * side
        after = yo_ref[base : base + layers, :]
        before = yo_ref[base + layers : base + 2 * layers, :]
        kappa = yo_ref[base + 2 * layers : base + 3 * layers, :]
        slope = yo_ref[base + 3 * layers : base + 4 * layers, :]
        cond = kappa * (1.0 + slope * before)
        c_t, c_c = corner_t[16 * side : 16 * side + layers], corner_c[16 * side : 16 * side + layers]
        tiles = []
        for start, at in ((0, 0), (cols - TILE, TILE - 1)):
            flux = time_step * face(
                cond[:, start : start + TILE], c_c, before[:, start : start + TILE], c_t
            )
            tiles.append(after[:, start : start + TILE] + jnp.where(lane_l == at, flux, 0.0))
        after = jnp.concatenate([tiles[0], after[:, TILE : cols - TILE], tiles[1]], 1) if (
            cols > 2 * TILE
        ) else jnp.concatenate(tiles, 1)
        halo.append((after, kappa * (1.0 + slope * after)))

    lane = lax.broadcasted_iota(jnp.int32, (rows, TILE), 1)
    for z in range(layers):
        add = xf_ref[z * rows : (z + 1) * rows, :]
        full_ref[z] = temp_ref[z]
        full_ref[z, :, 0:TILE] = temp_ref[z, :, 0:TILE] + jnp.where(lane == 0, add, 0.0)
        full_ref[z, :, cols - TILE :] = temp_ref[z, :, cols - TILE :] + jnp.where(
            lane == TILE - 1, add, 0.0
        )

    toward_c = crow_ref[0:1, :]
    first_place = place == 0
    last_place = place == places - 1
    link = one_hot(link_ref[...], 0, channels)
    stack = jnp.concatenate(
        [got[0][6:7, 0:channels], got[1][6:7, 0:channels], crow_ref[1:3, :], crow_ref[4:8, :]], 0
    )
    moved = pick_rows(stack, link)
    own_0 = jnp.where(first_place, moved[2:3], stack[2:3])
    own_e = jnp.where(last_place, moved[3:4], stack[3:4])
    late_l = got[0][7:8, 0:channels] + courant * (1.0 - toward_c) * own_0
    late_r = got[1][7:8, 0:channels] + courant * toward_c * own_e
    late = jnp.concatenate([late_l, late_r, crow_ref[2:8, :]], 0)
    late_moved = pick_rows(late, link)
    edge_rows = (
        (jnp.where(first_place, moved[0:1], stack[0:1]), jnp.where(last_place, moved[1:2], stack[1:2])),
        (jnp.where(first_place, late_moved[0:1], late_l), jnp.where(last_place, late_moved[1:2], late_r)),
    )
    shift_0 = courant * toward_c * edge_rows[0][0]
    shift_e = courant * (1.0 - toward_c) * edge_rows[0][1]
    tops = [
        time_step * face(
            own[side][5:6, channels : 2 * channels], got[side][5:6, channels : 2 * channels],
            own[side][4:5, channels : 2 * channels], got[side][4:5, channels : 2 * channels],
        )
        for side in range(2)
    ]
    every = one_hot(map_ref[...], 0, channels)
    tops = pick_rows(jnp.concatenate(tops + [crow_ref[2:8, :]], 0), every)
    wall_0, wall_e = crow_ref[3:4, :], crow_ref[4:5, :]
    add_0 = (
        courant * toward_c * edge_rows[1][0]
        + ((1.0 - courant) - heat_gain * wall_0) * shift_0
        + heat_gain * wall_0 * tops[0:1]
    )
    add_e = (
        courant * (1.0 - toward_c) * edge_rows[1][1]
        + ((1.0 - courant) - heat_gain * wall_e) * shift_e
        + heat_gain * wall_e * tops[1:2]
    )
    wide_row = lax.broadcasted_iota(jnp.int32, (TILE, channels), 0)
    chooser = one_hot(map_ref[...], group * rows, rows)
    edge_y = pick(chooser, jnp.where(wide_row == 0, shift_0, shift_e), ((1,), (1,)))
    adds = jnp.where(wide_row == 0, add_0, jnp.where(wide_row == 1, courant * toward_c * shift_0, add_e))
    adds = jnp.where(wide_row == TILE - 2, courant * (1.0 - toward_c) * shift_e, adds)
    turn_ref[...] = adds.T
    sel_ref[...] = pick(every, all_ref[...], ((0,), (0,)))
    mine = pl.ds(pl.multiple_of(group * rows, 8), rows)
    adds, flow = turn_ref[mine, :], sel_ref[mine, :]
    pad = [jnp.zeros((rows, cols - 2 * TILE), F32)] if cols > 2 * TILE else []
    flow_ref[...] = flow + jnp.concatenate(
        [jnp.where(lane < 2, adds, 0.0)] + pad + [jnp.where(lane >= TILE - 2, adds, 0.0)], 1
    )
    flow_copy = pltpu.make_async_copy(flow_ref, flow_hbm, out_sem.at[layers])
    flow_copy.start()
    flow = fw_ref[0:rows, :] + jnp.concatenate(
        [jnp.where(lane == 0, edge_y, 0.0)] + pad + [jnp.where(lane == TILE - 1, edge_y, 0.0)], 1
    )
    flux = fw_ref[rows:, :] * (full_ref[0] - flow)

    row8 = lax.broadcasted_iota(jnp.int32, (8, cols), 0)

    def emit(z, temp, cond, heat):
        result = temp + time_step * (heat + power_ref[z])
        if z == 0:
            result = result - time_step * flux
        halo_t = xt_ref[z * rows : (z + 1) * rows, :]
        halo_c = xc_ref[z * rows : (z + 1) * rows, :]
        sides = []
        for start, at in ((0, 0), (cols - TILE, TILE - 1)):
            part = slice(start, start + TILE)
            extra = time_step * face(cond[:, part], halo_c, temp[:, part], halo_t)
            sides.append(jnp.where(lane == at, extra, 0.0))
        middle = [jnp.zeros((rows, cols - 2 * TILE), F32)] if cols > 2 * TILE else []
        result = result + jnp.concatenate([sides[0]] + middle + [sides[1]], 1)
        out_ref[z] = result
        for side, opened, start, at in ((0, low_open, 0, 0), (1, high_open, rows - 8, 7)):
            part = slice(start, start + 8)
            extra = (time_step * opened) * face(
                cond[part], halo[side][1][z : z + 1], temp[part], halo[side][0][z : z + 1]
            )
            out_ref[z, part, :] = result[part] + jnp.where(row8 == at, extra, 0.0)

        copies.append(pltpu.make_async_copy(out_ref.at[z], out_hbm.at[z], out_sem.at[z]))
        copies[-1].start()

    copies = [flow_copy]
    closed_heat(full_ref, kappa_ref, slope_ref, emit)
    for copy in copies:
        copy.wait()


def pairs(count, first, closed):
    swaps = []
    for low in range(first, count, 2):
        high = low + 1
        if high == count:
            if not closed:
                continue
            high = 0
        swaps += [(low, high), (high, low)]
    return swaps


def shards(
    solid_temp, kappa, slope, power, coolant_temp, wall_coeff, channel_map, flow_dir, loop_link
):
    groups, places = lax.axis_size("grp"), lax.axis_size("loop")
    layers, rows, cols = solid_temp.shape
    channels = groups * rows
    strip = layers * rows
    params = pltpu.CompilerParams(vmem_limit_bytes=48 * 1024 * 1024)

    def shape(*dims):
        return jax.ShapeDtypeStruct(dims, F32)

    def call(body, outs, scratch, *args, ins=None, places=None):
        return pl.pallas_call(
            body,
            out_shape=outs,
            in_specs=[pl.BlockSpec(memory_space=ins or pltpu.VMEM)] * len(args),
            out_specs=[pl.BlockSpec(memory_space=places or pltpu.VMEM)] * len(outs),
            scratch_shapes=scratch,
            compiler_params=params,
        )(*[pltpu.with_memory_space_constraint(a, ins) if ins else a for a in args])

    def vmem(*dims):
        return pltpu.VMEM(dims, F32)

    block = shape(layers, rows, cols)
    halo = shape(4 * layers, cols)
    index = jax.ShapeDtypeStruct((1, channels), jnp.int32)
    first, temp, kappa, slope, power, ya, yb, share, map_row, link_row = call(
        open_kernel,
        (block, block, block, block, block, halo, halo, shape(2 * rows + 8, cols), index, index),
        [
            vmem(TILE, TILE), vmem(8, cols), pltpu.VMEM((1, rows), jnp.int32),
            pltpu.SemaphoreType.DMA((4, layers // CHUNK)), pltpu.SemaphoreType.DMA((5,)),
        ],
        solid_temp, kappa, slope, power, coolant_temp, wall_coeff, flow_dir.reshape(1, rows),
        channel_map, loop_link.reshape(1, channels),
        ins=pltpu.HBM,
    )
    ya = lax.ppermute(ya, "grp", pairs(groups, 0, False))
    yb = lax.ppermute(yb, "grp", pairs(groups, 1, False))
    share = lax.all_gather(share, "grp", axis=0, tiled=True)
    after, yo, sa, sb, fw, crow, flow = call(
        edge_kernel,
        (
            block, shape(8 * layers, cols), shape(8, strip), shape(8, strip),
            shape(2 * rows, cols), shape(8, channels), shape(rows, cols),
        ),
        [vmem(strip, TILE), vmem(TILE, TILE)],
        first, temp, kappa, slope, ya, yb, share, map_row,
    )
    ra = lax.ppermute(sa, "loop", pairs(places, 0, True))
    rb = lax.ppermute(sb, "loop", pairs(places, 1, True))
    flow = lax.all_gather(flow, "grp", axis=0, tiled=True)
    return call(
        close_kernel,
        (block, shape(rows, cols)),
        [
            vmem(TILE, strip), vmem(strip, TILE), vmem(strip, TILE), vmem(strip, TILE),
            vmem(layers, rows, cols), vmem(layers, rows, cols), vmem(rows, cols),
            vmem(channels, cols), vmem(channels, TILE), pltpu.SemaphoreType.DMA((layers + 1,)),
        ],
        after, kappa, slope, power, yo, ra, rb, sa, sb, fw, crow, map_row, link_row, flow,
        places=pltpu.HBM,
    )


def solution(mesh):
    block = P(None, "grp", "loop")
    plane = P("grp", "loop")
    return jax.shard_map(
        shards,
        mesh=mesh,
        in_specs=(block, block, block, block, plane, plane, P("loop", None), P("grp"), P()),
        out_specs=(block, plane),
        check_vma=False,
    )
```

```python
import jax
import jax.numpy as jnp
from jax import lax
from jax.experimental import pallas as pl
from jax.experimental.pallas import tpu as pltpu
from jax.sharding import PartitionSpec as P

time_step = 0.06
courant = 0.5
heat_gain = 0.5
TILE = 128
CHUNK = 4
F32 = jnp.float32
BF16 = jnp.bfloat16


def split3(value):
    high = value.astype(BF16)
    rest = value - high.astype(F32)
    middle = rest.astype(BF16)
    low = (rest - middle.astype(F32)).astype(BF16)
    return high, middle, low


def pick(chooser, value, dims):
    total = None
    for part in split3(value):
        term = lax.dot_general(chooser, part, (dims, ((), ())), preferred_element_type=F32)
        total = term if total is None else total + term
    return total


def pick_rows(value, chooser):
    total = None
    for part in split3(value):
        term = lax.dot_general(part, chooser, (((1,), (0,)), ((), ())), preferred_element_type=F32)
        total = term if total is None else total + term
    return total


def one_hot(index_row, first, count):
    shape = (count, index_row.shape[1])
    here = lax.broadcasted_iota(jnp.int32, shape, 0) + first
    return jnp.where(index_row == here, 1.0, 0.0).astype(BF16)


def face(cond_a, cond_b, temp_a, temp_b):
    return 0.5 * (cond_a + cond_b) * (temp_b - temp_a)


def closed_heat(temp_ref, kappa_ref, slope_ref, emit, ready=lambda z: None):
    layers, rows, cols = temp_ref.shape
    lane = lax.broadcasted_iota(jnp.int32, (rows, cols), 1)
    row = lax.broadcasted_iota(jnp.int32, (rows, cols), 0)
    ready(0)
    temp = temp_ref[0]
    cond = kappa_ref[0] * (1.0 + slope_ref[0] * temp)
    flux_below = None
    for z in range(layers):
        if z + 1 < layers:
            ready(z + 1)
        flux_x = face(cond, pltpu.roll(cond, cols - 1, 1), temp, pltpu.roll(temp, cols - 1, 1))
        flux_x = jnp.where(lane == cols - 1, 0.0, flux_x)
        heat = flux_x - pltpu.roll(flux_x, 1, 1)
        flux_y = face(cond, pltpu.roll(cond, rows - 1, 0), temp, pltpu.roll(temp, rows - 1, 0))
        flux_y = jnp.where(row == rows - 1, 0.0, flux_y)
        heat = heat + flux_y - pltpu.roll(flux_y, 1, 0)
        if flux_below is not None:
            heat = heat - flux_below
        if z + 1 < layers:
            temp_up = temp_ref[z + 1]
            cond_up = kappa_ref[z + 1] * (1.0 + slope_ref[z + 1] * temp_up)
            flux_below = face(cond, cond_up, temp, temp_up)
            heat = heat + flux_below
        emit(z, temp, cond, heat)
        if z + 1 < layers:
            temp, cond = temp_up, cond_up


def pack_kernel(
    temp_hbm, kappa_hbm, slope_hbm, power_hbm, flow_hbm, wall_hbm, dir_hbm, map_hbm, link_hbm,
    core_ref, cross_ref, map_ref, link_ref,
    temp_ref, kappa_ref, slope_ref, power_ref, top_ref, tmp_ref, row_ref, dir_ref,
    block_sem, top_sem, share_sem, small_sem,
):
    layers, rows, cols = temp_hbm.shape
    share = 2 * rows + 8
    group = lax.axis_index("grp")
    even = lax.rem(group, 2) == 0
    copies = []
    for n, (source, target) in enumerate((
        (temp_hbm, temp_ref), (kappa_hbm, kappa_ref), (slope_hbm, slope_ref), (power_hbm, power_ref),
    )):
        copies.append(pltpu.make_async_copy(source.at[:, 0:8], target.at[:, 0:8], block_sem.at[n, 0]))
        copies.append(
            pltpu.make_async_copy(source.at[:, rows - 8 : rows], target.at[:, 8:16], block_sem.at[n, 1])
        )
    tops = [
        pltpu.make_async_copy(source.at[0], top_ref.at[n], top_sem.at[n])
        for n, source in enumerate((temp_hbm, kappa_hbm, slope_hbm))
    ]
    smalls = [
        pltpu.make_async_copy(source, target, small_sem.at[n])
        for n, (source, target) in enumerate(((dir_hbm, dir_ref), (map_hbm, map_ref), (link_hbm, link_ref)))
    ]
    for m, target in enumerate((core_ref, cross_ref)):
        smalls.append(pltpu.make_async_copy(flow_hbm, target.at[0:rows], share_sem.at[m, 0]))
        smalls.append(pltpu.make_async_copy(wall_hbm, target.at[rows : 2 * rows], share_sem.at[m, 1]))
    for copy in copies + tops + smalls:
        copy.start()
    tmp_ref[...] = jnp.zeros_like(tmp_ref)
    row_ref[...] = jnp.zeros_like(row_ref)
    for copy in copies:
        copy.wait()

    def emit(z, temp, cond, heat):
        after = temp + time_step * (heat + power_ref[z])
        for q, value in enumerate((after, temp, kappa_ref[z], slope_ref[z])):
            at = share + q * layers + z
            core_ref[at : at + 1, :] = jnp.where(even, value[15:16], value[0:1])
            cross_ref[at : at + 1, :] = jnp.where(even, value[0:1], value[15:16])

    closed_heat(temp_ref, kappa_ref, slope_ref, emit)
    for copy in tops:
        copy.wait()
    temp = top_ref[0]
    cond = top_ref[1] * (1.0 + top_ref[2] * temp)
    lane = lax.broadcasted_iota(jnp.int32, (rows, TILE), 1)
    packed = jnp.where(lane == 0, temp[:, 0:TILE], pltpu.roll(temp[:, cols - TILE :], 2, 1))
    packed = jnp.where(lane == 3, pltpu.roll(cond[:, 0:TILE], 3, 1), packed)
    packed = jnp.where(lane == 4, pltpu.roll(cond[:, cols - TILE :], 5, 1), packed)
    tmp_ref[0:rows, :] = packed
    row_ref[0:8, 0:TILE] = tmp_ref[...].T[0:8, :]
    for copy in smalls:
        copy.wait()
    row_ref[2:3, 0:rows] = dir_ref[...].astype(F32)
    extra = pltpu.roll(row_ref[...], group * rows, 1)
    core_ref[2 * rows : share, :] = extra
    cross_ref[2 * rows : share, :] = extra


def open_kernel(
    temp_hbm, kappa_hbm, slope_hbm, power_hbm, after_ref,
    next_ref, temp_ref, kappa_ref, slope_ref, power_ref, block_sem,
):
    layers = temp_ref.shape[0]
    blocks = []
    for z in range(0, layers, CHUNK):
        part = pl.ds(z, CHUNK)
        blocks.append([
            pltpu.make_async_copy(source.at[part], target.at[part], block_sem.at[n, z // CHUNK])
            for n, (source, target) in enumerate((
                (temp_hbm, temp_ref), (kappa_hbm, kappa_ref), (slope_hbm, slope_ref), (power_hbm, power_ref),
            ))
        ])
    for block in blocks:
        for copy in block:
            copy.start()

    def ready(z):
        if z % CHUNK == 0:
            for copy in blocks[z // CHUNK]:
                copy.wait()

    def emit(z, temp, cond, heat):
        next_ref[z] = temp + time_step * (heat + power_ref[z])

    closed_heat(temp_ref, kappa_ref, slope_ref, emit, ready)


def edge_kernel(
    first_ref, temp_ref, kappa_ref, slope_ref, own_ref, core_ref, cross_ref, relay_ref, map_ref,
    next_ref, yo_ref, sa_ref, sb_ref, fw_ref, crow_ref, flow_ref, strip_ref, small_ref, all_ref,
):
    layers, rows, cols = temp_ref.shape
    span = 2 * rows + 8
    groups = lax.axis_size("grp")
    group = lax.axis_index("grp")
    even = lax.rem(group, 2) == 0
    place_even = lax.rem(lax.axis_index("loop"), 2) == 0
    ya, yb = core_ref[span : span + 4 * layers, :], cross_ref[span : span + 4 * layers, :]
    low, high = jnp.where(even, yb, ya), jnp.where(even, ya, yb)
    yo_ref[0 : 4 * layers, :] = low
    yo_ref[4 * layers :, :] = high
    low_open = jnp.where(group == 0, 0.0, 1.0)
    high_open = jnp.where(group == groups - 1, 0.0, 1.0)

    beside = group + 1 - 2 * lax.rem(group, 2)
    extra = jnp.zeros((8, cols), F32)
    for ref, owner in (
        (own_ref, group), (core_ref, beside), (cross_ref, groups - 1 - group), (relay_ref, groups - 1 - beside),
    ):
        part = pl.ds(pl.multiple_of(owner * rows, 8), rows)
        all_ref[part, 0:cols] = ref[0:rows, :]
        all_ref[part, cols : 2 * cols] = ref[rows : 2 * rows, :]
        extra = extra + ref[2 * rows : span, :]
    flow_all, wall_all = all_ref[:, 0:cols], all_ref[:, cols : 2 * cols]
    chooser = one_hot(map_ref[...], group * rows - 8, rows + 16)
    both = pick(chooser, all_ref[...], ((1,), (0,)))
    flow_y, wall_y = both[:, :cols], both[:, cols:]
    flow, wall = flow_y[8 : 8 + rows], wall_y[8 : 8 + rows]
    sink = wall * (temp_ref[0] - flow)
    temp_low, temp_high = yo_ref[layers : layers + 1, :], yo_ref[5 * layers : 5 * layers + 1, :]
    sink_low = wall_y[7:8] * (temp_low - flow_y[7:8])
    sink_high = wall_y[8 + rows : 9 + rows] * (temp_high - flow_y[8 + rows : 9 + rows])

    row = lax.broadcasted_iota(jnp.int32, (rows, cols), 0)
    lane = lax.broadcasted_iota(jnp.int32, (rows, TILE), 1)
    small_ref[...] = jnp.zeros_like(small_ref)
    lane1 = lax.broadcasted_iota(jnp.int32, (1, TILE), 1)
    for z in range(layers):
        temp, kappa, slope = temp_ref[z], kappa_ref[z], slope_ref[z]
        after = first_ref[z]
        edges = []
        for side, base, at, opened, sunk in (
            (0, 0, 0, low_open, sink_low),
            (1, 4 * layers, rows - 1, high_open, sink_high),
        ):
            temp_h = yo_ref[base + layers + z : base + layers + z + 1, :]
            cond_h = yo_ref[base + 2 * layers + z : base + 2 * layers + z + 1, :] * (
                1.0 + yo_ref[base + 3 * layers + z : base + 3 * layers + z + 1, :] * temp_h
            )
            temp_e = temp[at : at + 1]
            cond_e = kappa[at : at + 1] * (1.0 + slope[at : at + 1] * temp_e)
            flux = opened * face(cond_e, cond_h, temp_e, temp_h)
            halo = yo_ref[base + z : base + z + 1, :] - time_step * flux
            if z == 0:
                halo = halo - time_step * sunk
            yo_ref[base + z : base + z + 1, :] = halo
            edges.append(time_step * flux)
            corner = jnp.where(
                lane1 == 0,
                temp_h[:, 0:TILE],
                jnp.where(
                    lane1 == 1,
                    pltpu.roll(cond_h[:, 0:TILE], 1, 1),
                    jnp.where(
                        lane1 == 4,
                        pltpu.roll(temp_h[:, cols - TILE :], 5, 1),
                        pltpu.roll(cond_h[:, cols - TILE :], 6, 1),
                    ),
                ),
            )
            small_ref[16 * side + z : 16 * side + z + 1, :] = corner
        after = after + jnp.where(row == 0, edges[0], jnp.where(row == rows - 1, edges[1], 0.0))
        if z == 0:
            after = after - time_step * sink
        next_ref[z] = after
        packed = None
        for n, value in enumerate((after, temp, kappa, slope)):
            left = value[:, 0:TILE]
            right = pltpu.roll(value[:, cols - TILE :], n + 5, 1)
            left = pltpu.roll(left, n, 1) if n else left
            packed = left if packed is None else jnp.where(lane == n, left, packed)
            packed = jnp.where(lane == n + 4, right, packed)
        strip_ref[z * rows : (z + 1) * rows, :] = packed
    toward_y = pick(chooser[8 : 8 + rows], jnp.broadcast_to(extra[2:3], (TILE, groups * rows)), ((1,), (1,)))
    toward_y = jnp.concatenate([toward_y] * (cols // TILE), 1) > 0.5
    lane_w = lax.broadcasted_iota(jnp.int32, (rows, cols), 1)

    def upstream(values):
        before = jnp.where(lane_w == 0, 0.0, pltpu.roll(values, 1, 1))
        after = jnp.where(lane_w == cols - 1, 0.0, pltpu.roll(values, cols - 1, 1))
        return jnp.where(toward_y, before, after)

    flow = flow - courant * (flow - upstream(flow)) + heat_gain * sink
    fw_ref[0:rows, :] = flow
    fw_ref[rows:, :] = wall
    flux = wall * (next_ref[0] - flow)
    flow_ref[...] = flow - courant * (flow - upstream(flow)) + heat_gain * flux

    strips = strip_ref[...].T[0:8, :]
    corners = small_ref[...].T[0:8, :]

    lane_c = lax.broadcasted_iota(jnp.int32, (groups * rows, TILE), 1)
    right_flow = flow_all[:, cols - TILE :]
    pack = jnp.where(lane_c < 2, flow_all[:, 0:TILE], pltpu.roll(right_flow, 4, 1))
    pack = jnp.where(lane_c == 4, pltpu.roll(wall_all[:, 0:TILE], 4, 1), pack)
    pack = jnp.where(lane_c == 5, pltpu.roll(wall_all[:, cols - TILE :], 6, 1), pack)
    turned = pack.T
    flow_0, flow_1 = turned[0:1], turned[1:2]
    flow_m, flow_e = turned[2:3], turned[3:4]
    wall_0, wall_e = turned[4:5], turned[5:6]
    top = pick_rows(extra, one_hot(map_ref[...], 0, groups * rows))
    toward = extra[2:3]
    flux_0 = wall_0 * (top[0:1] - flow_0)
    flux_e = wall_e * (top[1:2] - flow_e)
    part_0 = (1.0 - courant) * flow_0 + courant * (1.0 - toward) * flow_1 + heat_gain * flux_0
    part_e = (1.0 - courant) * flow_e + courant * toward * flow_m + heat_gain * flux_e
    crow_ref[...] = jnp.zeros_like(crow_ref)
    crow_ref[0:1, :] = toward
    crow_ref[1:2, :] = flow_0
    crow_ref[2:3, :] = flow_e
    crow_ref[3:4, :] = wall_0
    crow_ref[4:5, :] = wall_e
    channels = groups * rows
    for ref, pick_right in ((sa_ref, place_even), (sb_ref, jnp.logical_not(place_even))):
        ref[...] = jnp.zeros_like(ref)
        ref[0:4, :] = jnp.where(pick_right, strips[4:8], strips[0:4])
        ref[4:6, 0:TILE] = jnp.where(pick_right, corners[4:6], corners[0:2])
        ref[4:5, channels : 2 * channels] = jnp.where(pick_right, extra[1:2], extra[0:1])
        ref[5:6, channels : 2 * channels] = jnp.where(pick_right, extra[4:5], extra[3:4])
        ref[6:7, 0:channels] = jnp.where(pick_right, flow_e, flow_0)
        ref[7:8, 0:channels] = jnp.where(pick_right, part_e, part_0)


def close_kernel(
    temp_ref, kappa_ref, slope_ref, power_ref, yo_ref, ra_ref, rb_ref, sa_ref, sb_ref,
    fw_ref, crow_ref, map_ref, link_ref, all_ref,
    out_hbm, flow_hbm, wide_ref, xt_ref, xc_ref, xf_ref, full_ref, out_ref, flow_ref, sel_ref, turn_ref, out_sem,
):
    layers, rows, cols = temp_ref.shape
    group, groups = lax.axis_index("grp"), lax.axis_size("grp")
    place, places = lax.axis_index("loop"), lax.axis_size("loop")
    even = lax.rem(place, 2) == 0
    channels = crow_ref.shape[1]
    low_open = jnp.where(group == 0, 0.0, 1.0)
    high_open = jnp.where(group == groups - 1, 0.0, 1.0)
    got_a, got_b, own_a, own_b = ra_ref[...], rb_ref[...], sa_ref[...], sb_ref[...]
    got = (jnp.where(even, got_b, got_a), jnp.where(even, got_a, got_b))
    own = (jnp.where(even, own_b, own_a), jnp.where(even, own_a, own_b))

    def turn(first, last, ref):
        wide_ref[0:1, 0 : first.shape[1]] = first
        wide_ref[TILE - 1 : TILE, 0 : last.shape[1]] = last
        ref[...] = wide_ref[:, 0 : ref.shape[0]].T

    wide_ref[...] = jnp.zeros_like(wide_ref)
    temps, conds, fluxes = [], [], []
    for side in range(2):
        temp_n, temp_o = got[side][1:2], own[side][1:2]
        cond_n = got[side][2:3] * (1.0 + got[side][3:4] * temp_n)
        cond_o = own[side][2:3] * (1.0 + own[side][3:4] * temp_o)
        flux = time_step * face(cond_o, cond_n, temp_o, temp_n)
        after = got[side][0:1] - flux
        temps.append(after)
        conds.append(got[side][2:3] * (1.0 + got[side][3:4] * after))
        fluxes.append(flux)
    turn(temps[0], temps[1], xt_ref)
    turn(conds[0], conds[1], xc_ref)
    turn(fluxes[0], fluxes[1], xf_ref)

    wide_ref[0:1, 0:TILE] = got[0][4:5, 0:TILE]
    wide_ref[TILE - 1 : TILE, 0:TILE] = got[1][4:5, 0:TILE]
    corner_t = wide_ref[:, 0:TILE].T
    wide_ref[0:1, 0:TILE] = got[0][5:6, 0:TILE]
    wide_ref[TILE - 1 : TILE, 0:TILE] = got[1][5:6, 0:TILE]
    corner_c = wide_ref[:, 0:TILE].T
    lane_l = lax.broadcasted_iota(jnp.int32, (layers, TILE), 1)
    halo = []
    for side in range(2):
        base = 4 * layers * side
        after = yo_ref[base : base + layers, :]
        before = yo_ref[base + layers : base + 2 * layers, :]
        kappa = yo_ref[base + 2 * layers : base + 3 * layers, :]
        slope = yo_ref[base + 3 * layers : base + 4 * layers, :]
        cond = kappa * (1.0 + slope * before)
        c_t, c_c = corner_t[16 * side : 16 * side + layers], corner_c[16 * side : 16 * side + layers]
        tiles = []
        for start, at in ((0, 0), (cols - TILE, TILE - 1)):
            flux = time_step * face(
                cond[:, start : start + TILE], c_c, before[:, start : start + TILE], c_t
            )
            tiles.append(after[:, start : start + TILE] + jnp.where(lane_l == at, flux, 0.0))
        after = jnp.concatenate([tiles[0], after[:, TILE : cols - TILE], tiles[1]], 1) if (
            cols > 2 * TILE
        ) else jnp.concatenate(tiles, 1)
        halo.append((after, kappa * (1.0 + slope * after)))

    lane = lax.broadcasted_iota(jnp.int32, (rows, TILE), 1)
    for z in range(layers):
        add = xf_ref[z * rows : (z + 1) * rows, :]
        full_ref[z] = temp_ref[z]
        full_ref[z, :, 0:TILE] = temp_ref[z, :, 0:TILE] + jnp.where(lane == 0, add, 0.0)
        full_ref[z, :, cols - TILE :] = temp_ref[z, :, cols - TILE :] + jnp.where(
            lane == TILE - 1, add, 0.0
        )

    toward_c = crow_ref[0:1, :]
    first_place = place == 0
    last_place = place == places - 1
    link = one_hot(link_ref[...], 0, channels)
    stack = jnp.concatenate(
        [got[0][6:7, 0:channels], got[1][6:7, 0:channels], crow_ref[1:3, :], crow_ref[4:8, :]], 0
    )
    moved = pick_rows(stack, link)
    own_0 = jnp.where(first_place, moved[2:3], stack[2:3])
    own_e = jnp.where(last_place, moved[3:4], stack[3:4])
    late_l = got[0][7:8, 0:channels] + courant * (1.0 - toward_c) * own_0
    late_r = got[1][7:8, 0:channels] + courant * toward_c * own_e
    late = jnp.concatenate([late_l, late_r, crow_ref[2:8, :]], 0)
    late_moved = pick_rows(late, link)
    edge_rows = (
        (jnp.where(first_place, moved[0:1], stack[0:1]), jnp.where(last_place, moved[1:2], stack[1:2])),
        (jnp.where(first_place, late_moved[0:1], late_l), jnp.where(last_place, late_moved[1:2], late_r)),
    )
    shift_0 = courant * toward_c * edge_rows[0][0]
    shift_e = courant * (1.0 - toward_c) * edge_rows[0][1]
    tops = [
        time_step * face(
            own[side][5:6, channels : 2 * channels], got[side][5:6, channels : 2 * channels],
            own[side][4:5, channels : 2 * channels], got[side][4:5, channels : 2 * channels],
        )
        for side in range(2)
    ]
    every = one_hot(map_ref[...], 0, channels)
    tops = pick_rows(jnp.concatenate(tops + [crow_ref[2:8, :]], 0), every)
    wall_0, wall_e = crow_ref[3:4, :], crow_ref[4:5, :]
    add_0 = (
        courant * toward_c * edge_rows[1][0]
        + ((1.0 - courant) - heat_gain * wall_0) * shift_0
        + heat_gain * wall_0 * tops[0:1]
    )
    add_e = (
        courant * (1.0 - toward_c) * edge_rows[1][1]
        + ((1.0 - courant) - heat_gain * wall_e) * shift_e
        + heat_gain * wall_e * tops[1:2]
    )
    wide_row = lax.broadcasted_iota(jnp.int32, (TILE, channels), 0)
    chooser = one_hot(map_ref[...], group * rows, rows)
    edge_y = pick(chooser, jnp.where(wide_row == 0, shift_0, shift_e), ((1,), (1,)))
    adds = jnp.where(wide_row == 0, add_0, jnp.where(wide_row == 1, courant * toward_c * shift_0, add_e))
    adds = jnp.where(wide_row == TILE - 2, courant * (1.0 - toward_c) * shift_e, adds)
    turn_ref[...] = adds.T
    sel_ref[...] = pick(every, all_ref[...], ((0,), (0,)))
    mine = pl.ds(pl.multiple_of(group * rows, 8), rows)
    adds, flow = turn_ref[mine, :], sel_ref[mine, :]
    pad = [jnp.zeros((rows, cols - 2 * TILE), F32)] if cols > 2 * TILE else []
    flow_ref[...] = flow + jnp.concatenate(
        [jnp.where(lane < 2, adds, 0.0)] + pad + [jnp.where(lane >= TILE - 2, adds, 0.0)], 1
    )
    flow_copy = pltpu.make_async_copy(flow_ref, flow_hbm, out_sem.at[layers])
    flow_copy.start()
    flow = fw_ref[0:rows, :] + jnp.concatenate(
        [jnp.where(lane == 0, edge_y, 0.0)] + pad + [jnp.where(lane == TILE - 1, edge_y, 0.0)], 1
    )
    flux = fw_ref[rows:, :] * (full_ref[0] - flow)

    row8 = lax.broadcasted_iota(jnp.int32, (8, cols), 0)

    def emit(z, temp, cond, heat):
        result = temp + time_step * (heat + power_ref[z])
        if z == 0:
            result = result - time_step * flux
        halo_t = xt_ref[z * rows : (z + 1) * rows, :]
        halo_c = xc_ref[z * rows : (z + 1) * rows, :]
        sides = []
        for start, at in ((0, 0), (cols - TILE, TILE - 1)):
            part = slice(start, start + TILE)
            extra = time_step * face(cond[:, part], halo_c, temp[:, part], halo_t)
            sides.append(jnp.where(lane == at, extra, 0.0))
        middle = [jnp.zeros((rows, cols - 2 * TILE), F32)] if cols > 2 * TILE else []
        result = result + jnp.concatenate([sides[0]] + middle + [sides[1]], 1)
        out_ref[z] = result
        for side, opened, start, at in ((0, low_open, 0, 0), (1, high_open, rows - 8, 7)):
            part = slice(start, start + 8)
            extra = (time_step * opened) * face(
                cond[part], halo[side][1][z : z + 1], temp[part], halo[side][0][z : z + 1]
            )
            out_ref[z, part, :] = result[part] + jnp.where(row8 == at, extra, 0.0)

        copies.append(pltpu.make_async_copy(out_ref.at[z], out_hbm.at[z], out_sem.at[z]))
        copies[-1].start()

    copies = [flow_copy]
    closed_heat(full_ref, kappa_ref, slope_ref, emit)
    for copy in copies:
        copy.wait()


def pairs(count, first, closed):
    swaps = []
    for low in range(first, count, 2):
        high = low + 1
        if high == count:
            if not closed:
                continue
            high = 0
        swaps += [(low, high), (high, low)]
    return swaps


def shards(
    solid_temp, kappa, slope, power, coolant_temp, wall_coeff, channel_map, flow_dir, loop_link
):
    groups, places = lax.axis_size("grp"), lax.axis_size("loop")
    layers, rows, cols = solid_temp.shape
    channels = groups * rows
    strip = layers * rows
    params = pltpu.CompilerParams(vmem_limit_bytes=48 * 1024 * 1024)

    def shape(*dims):
        return jax.ShapeDtypeStruct(dims, F32)

    def call(body, outs, scratch, *args, far=0, places=None, cost=None):
        return pl.pallas_call(
            body,
            out_shape=outs,
            in_specs=[pl.BlockSpec(memory_space=pltpu.HBM)] * far + [pl.BlockSpec(memory_space=pltpu.VMEM)] * (len(args) - far),
            out_specs=[pl.BlockSpec(memory_space=places or pltpu.VMEM)] * len(outs),
            scratch_shapes=scratch,
            compiler_params=params,
            cost_estimate=cost,
        )(*[pltpu.with_memory_space_constraint(arg, pltpu.HBM) for arg in args[:far]], *args[far:])

    def vmem(*dims):
        return pltpu.VMEM(dims, F32)

    block = shape(layers, rows, cols)
    share = shape(2 * rows + 8 + 4 * layers, cols)
    index = jax.ShapeDtypeStruct((1, channels), jnp.int32)
    core, cross, map_row, link_row = call(
        pack_kernel,
        (share, share, index, index),
        [
            vmem(layers, 16, cols), vmem(layers, 16, cols), vmem(layers, 16, cols), vmem(layers, 16, cols),
            vmem(3, rows, cols), vmem(TILE, TILE), vmem(8, cols), pltpu.VMEM((1, rows), jnp.int32),
            pltpu.SemaphoreType.DMA((4, 2)), pltpu.SemaphoreType.DMA((3,)), pltpu.SemaphoreType.DMA((2, 2)),
            pltpu.SemaphoreType.DMA((3,)),
        ],
        solid_temp, kappa, slope, power, coolant_temp, wall_coeff, flow_dir.reshape(1, rows),
        channel_map, loop_link.reshape(1, channels),
        far=9,
    )
    beside = [(i, i + 1 - 2 * (i % 2)) for i in range(groups)]
    across = [(i, groups - 1 - i) for i in range(groups)]
    got_cross = lax.ppermute(cross, "grp", across)
    got_core = lax.ppermute(core, "grp", beside)
    first, temp, kappa, slope, power = call(
        open_kernel,
        (block, block, block, block, block),
        [pltpu.SemaphoreType.DMA((4, layers // CHUNK))],
        solid_temp, kappa, slope, power, map_row,
        far=4,
        cost=pl.CostEstimate(flops=30 * layers * rows * cols, bytes_accessed=36 * layers * rows * cols, transcendentals=0),
    )
    got_cross, first = lax.optimization_barrier((got_cross, first))
    relay = lax.ppermute(got_cross, "grp", beside)
    after, yo, sa, sb, fw, crow, flow = call(
        edge_kernel,
        (
            block, shape(8 * layers, cols), shape(8, strip), shape(8, strip),
            shape(2 * rows, cols), shape(8, channels), shape(rows, cols),
        ),
        [vmem(strip, TILE), vmem(TILE, TILE), vmem(channels, 2 * cols)],
        first, temp, kappa, slope, core, got_core, got_cross, relay, map_row,
    )
    ra = lax.ppermute(sa, "loop", pairs(places, 0, True))
    rb = lax.ppermute(sb, "loop", pairs(places, 1, True))
    flow = lax.all_gather(flow, "grp", axis=0, tiled=True)
    return call(
        close_kernel,
        (block, shape(rows, cols)),
        [
            vmem(TILE, strip), vmem(strip, TILE), vmem(strip, TILE), vmem(strip, TILE),
            vmem(layers, rows, cols), vmem(layers, rows, cols), vmem(rows, cols),
            vmem(channels, cols), vmem(channels, TILE), pltpu.SemaphoreType.DMA((layers + 1,)),
        ],
        after, kappa, slope, power, yo, ra, rb, sa, sb, fw, crow, map_row, link_row, flow,
        places=pltpu.HBM,
    )


def solution(mesh):
    block = P(None, "grp", "loop")
    plane = P("grp", "loop")
    return jax.shard_map(
        shards,
        mesh=mesh,
        in_specs=(block, block, block, block, plane, plane, P("loop", None), P("grp"), P()),
        out_specs=(block, plane),
        check_vma=False,
    )
```

```python
import jax
import jax.numpy as jnp
from jax import lax
from jax.experimental import pallas as pl
from jax.experimental.pallas import tpu as pltpu
from jax.sharding import PartitionSpec as P

time_step = 0.06
courant = 0.5
heat_gain = 0.5
TILE = 128
CHUNK = 4
F32 = jnp.float32
BF16 = jnp.bfloat16


def split3(value):
    high = value.astype(BF16)
    rest = value - high.astype(F32)
    middle = rest.astype(BF16)
    low = (rest - middle.astype(F32)).astype(BF16)
    return high, middle, low


def pick(chooser, value, dims):
    total = None
    for part in split3(value):
        term = lax.dot_general(chooser, part, (dims, ((), ())), preferred_element_type=F32)
        total = term if total is None else total + term
    return total


def pick_rows(value, chooser):
    total = None
    for part in split3(value):
        term = lax.dot_general(part, chooser, (((1,), (0,)), ((), ())), preferred_element_type=F32)
        total = term if total is None else total + term
    return total


def one_hot(index_row, first, count):
    shape = (count, index_row.shape[1])
    here = lax.broadcasted_iota(jnp.int32, shape, 0) + first
    return jnp.where(index_row == here, 1.0, 0.0).astype(BF16)


def conduct(kappa, slope, temp):
    return (0.5 * time_step) * kappa * (1.0 + slope * temp)


def face(cond_a, cond_b, temp_a, temp_b):
    return (cond_a + cond_b) * (temp_b - temp_a)


def closed_heat(temp_ref, kappa_ref, slope_ref, emit, ready=lambda z: None):
    layers, rows, cols = temp_ref.shape
    lane = lax.broadcasted_iota(jnp.int32, (rows, cols), 1)
    row = lax.broadcasted_iota(jnp.int32, (rows, cols), 0)
    ready(0)
    temp = temp_ref[0]
    cond = conduct(kappa_ref[0], slope_ref[0], temp)
    flux_below = None
    for z in range(layers):
        if z + 1 < layers:
            ready(z + 1)
        flux_x = face(cond, pltpu.roll(cond, cols - 1, 1), temp, pltpu.roll(temp, cols - 1, 1))
        flux_x = jnp.where(lane == cols - 1, 0.0, flux_x)
        heat = flux_x - pltpu.roll(flux_x, 1, 1)
        flux_y = face(cond, pltpu.roll(cond, rows - 1, 0), temp, pltpu.roll(temp, rows - 1, 0))
        flux_y = jnp.where(row == rows - 1, 0.0, flux_y)
        heat = heat + flux_y - pltpu.roll(flux_y, 1, 0)
        if flux_below is not None:
            heat = heat - flux_below
        if z + 1 < layers:
            temp_up = temp_ref[z + 1]
            cond_up = conduct(kappa_ref[z + 1], slope_ref[z + 1], temp_up)
            flux_below = face(cond, cond_up, temp, temp_up)
            heat = heat + flux_below
        emit(z, temp, cond, heat)
        if z + 1 < layers:
            temp, cond = temp_up, cond_up


def pack_kernel(
    temp_hbm, kappa_hbm, slope_hbm, power_hbm, flow_hbm, wall_hbm, dir_hbm, map_hbm, link_hbm,
    core_ref, cross_ref, step_ref, map_ref, link_ref,
    temp_ref, kappa_ref, slope_ref, power_ref, top_ref, tmp_ref, row_ref, dir_ref,
    block_sem, top_sem, share_sem, small_sem,
):
    layers, rows, cols = temp_hbm.shape
    share = 2 * rows + 8
    group = lax.axis_index("grp")
    even = lax.rem(group, 2) == 0
    copies = []
    for n, (source, target) in enumerate((
        (temp_hbm, temp_ref), (kappa_hbm, kappa_ref), (slope_hbm, slope_ref), (power_hbm, power_ref),
    )):
        copies.append(pltpu.make_async_copy(source.at[:, 0:8], target.at[:, 0:8], block_sem.at[n, 0]))
        copies.append(
            pltpu.make_async_copy(source.at[:, rows - 8 : rows], target.at[:, 8:16], block_sem.at[n, 1])
        )
    tops = [
        pltpu.make_async_copy(source.at[0], top_ref.at[n], top_sem.at[n])
        for n, source in enumerate((temp_hbm, kappa_hbm, slope_hbm))
    ]
    smalls = [
        pltpu.make_async_copy(source, target, small_sem.at[n])
        for n, (source, target) in enumerate(((dir_hbm, dir_ref), (map_hbm, map_ref), (link_hbm, link_ref)))
    ]
    for m, target in enumerate((core_ref, cross_ref)):
        smalls.append(pltpu.make_async_copy(flow_hbm, target.at[0:rows], share_sem.at[m, 0]))
        smalls.append(pltpu.make_async_copy(wall_hbm, target.at[rows : 2 * rows], share_sem.at[m, 1]))
    for copy in copies + tops + smalls:
        copy.start()
    tmp_ref[...] = jnp.zeros_like(tmp_ref)
    row_ref[...] = jnp.zeros_like(row_ref)
    for copy in copies:
        copy.wait()

    def emit(z, temp, cond, heat):
        after = temp + heat + time_step * power_ref[z]
        for q, value in enumerate((after, temp, kappa_ref[z], slope_ref[z])):
            at = q * layers + z
            core_ref[share + at : share + at + 1, :] = jnp.where(even, value[15:16], value[0:1])
            step_ref[at : at + 1, :] = jnp.where(even, value[0:1], value[15:16])

    closed_heat(temp_ref, kappa_ref, slope_ref, emit)
    for copy in tops:
        copy.wait()
    temp = top_ref[0]
    cond = conduct(top_ref[1], top_ref[2], temp)
    lane = lax.broadcasted_iota(jnp.int32, (rows, TILE), 1)
    packed = jnp.where(lane == 0, temp[:, 0:TILE], pltpu.roll(temp[:, cols - TILE :], 2, 1))
    packed = jnp.where(lane == 3, pltpu.roll(cond[:, 0:TILE], 3, 1), packed)
    packed = jnp.where(lane == 4, pltpu.roll(cond[:, cols - TILE :], 5, 1), packed)
    tmp_ref[0:rows, :] = packed
    row_ref[0:8, 0:TILE] = tmp_ref[...].T[0:8, :]
    for copy in smalls:
        copy.wait()
    row_ref[2:3, 0:rows] = dir_ref[...].astype(F32)
    extra = pltpu.roll(row_ref[...], group * rows, 1)
    core_ref[2 * rows : share, :] = extra
    cross_ref[2 * rows : share, :] = extra


def open_kernel(
    temp_hbm, kappa_hbm, slope_hbm, power_hbm, after_ref,
    next_ref, temp_ref, kappa_ref, slope_ref, power_ref, block_sem,
):
    layers = temp_ref.shape[0]
    blocks = []
    for z in range(0, layers, CHUNK):
        part = pl.ds(z, CHUNK)
        blocks.append([
            pltpu.make_async_copy(source.at[part], target.at[part], block_sem.at[n, z // CHUNK])
            for n, (source, target) in enumerate((
                (temp_hbm, temp_ref), (kappa_hbm, kappa_ref), (slope_hbm, slope_ref), (power_hbm, power_ref),
            ))
        ])
    for block in blocks:
        for copy in block:
            copy.start()

    def ready(z):
        if z % CHUNK == 0:
            for copy in blocks[z // CHUNK]:
                copy.wait()

    def emit(z, temp, cond, heat):
        next_ref[z] = temp + heat + time_step * power_ref[z]

    closed_heat(temp_ref, kappa_ref, slope_ref, emit, ready)


def edge_kernel(
    first_ref, temp_ref, kappa_ref, slope_ref, own_ref, core_ref, cross_ref, relay_ref, step_ref, map_ref,
    next_ref, yo_ref, sa_ref, sb_ref, fw_ref, crow_ref, strip_ref, small_ref, all_ref,
):
    layers, rows, cols = temp_ref.shape
    span = 2 * rows + 8
    groups = lax.axis_size("grp")
    group = lax.axis_index("grp")
    even = lax.rem(group, 2) == 0
    place_even = lax.rem(lax.axis_index("loop"), 2) == 0
    ya, yb = core_ref[span : span + 4 * layers, :], step_ref[...]
    low, high = jnp.where(even, yb, ya), jnp.where(even, ya, yb)
    yo_ref[0 : 4 * layers, :] = low
    yo_ref[4 * layers :, :] = high
    low_open = jnp.where(group == 0, 0.0, 1.0)
    high_open = jnp.where(group == groups - 1, 0.0, 1.0)

    beside = group + 1 - 2 * lax.rem(group, 2)
    extra = jnp.zeros((8, cols), F32)
    for ref, owner in (
        (own_ref, group), (core_ref, beside), (cross_ref, groups - 1 - group), (relay_ref, groups - 1 - beside),
    ):
        part = pl.ds(pl.multiple_of(owner * rows, 8), rows)
        all_ref[part, 0:cols] = ref[0:rows, :]
        all_ref[part, cols : 2 * cols] = ref[rows : 2 * rows, :]
        extra = extra + ref[2 * rows : span, :]
    flow_all, wall_all = all_ref[:, 0:cols], all_ref[:, cols : 2 * cols]
    chooser = one_hot(map_ref[...], group * rows - 8, rows + 16)
    both = pick(chooser, all_ref[...], ((1,), (0,)))
    flow_y, wall_y = both[:, :cols], both[:, cols:]
    flow, wall = flow_y[8 : 8 + rows], wall_y[8 : 8 + rows]
    fw_ref[0:rows, :] = flow
    fw_ref[rows:, :] = wall
    sink = wall * (temp_ref[0] - flow)
    temp_low, temp_high = yo_ref[layers : layers + 1, :], yo_ref[5 * layers : 5 * layers + 1, :]
    sink_low = wall_y[7:8] * (temp_low - flow_y[7:8])
    sink_high = wall_y[8 + rows : 9 + rows] * (temp_high - flow_y[8 + rows : 9 + rows])

    row = lax.broadcasted_iota(jnp.int32, (rows, cols), 0)
    lane = lax.broadcasted_iota(jnp.int32, (rows, TILE), 1)
    small_ref[...] = jnp.zeros_like(small_ref)
    lane1 = lax.broadcasted_iota(jnp.int32, (1, TILE), 1)
    for z in range(layers):
        temp, kappa, slope = temp_ref[z], kappa_ref[z], slope_ref[z]
        after = first_ref[z]
        edges = []
        for side, base, at, opened, sunk in (
            (0, 0, 0, low_open, sink_low),
            (1, 4 * layers, rows - 1, high_open, sink_high),
        ):
            temp_h = yo_ref[base + layers + z : base + layers + z + 1, :]
            cond_h = conduct(
                yo_ref[base + 2 * layers + z : base + 2 * layers + z + 1, :],
                yo_ref[base + 3 * layers + z : base + 3 * layers + z + 1, :],
                temp_h,
            )
            temp_e = temp[at : at + 1]
            cond_e = conduct(kappa[at : at + 1], slope[at : at + 1], temp_e)
            flux = opened * face(cond_e, cond_h, temp_e, temp_h)
            halo = yo_ref[base + z : base + z + 1, :] - flux
            if z == 0:
                halo = halo - time_step * sunk
            yo_ref[base + z : base + z + 1, :] = halo
            edges.append(flux)
            corner = jnp.where(
                lane1 == 0,
                temp_h[:, 0:TILE],
                jnp.where(
                    lane1 == 1,
                    pltpu.roll(cond_h[:, 0:TILE], 1, 1),
                    jnp.where(
                        lane1 == 4,
                        pltpu.roll(temp_h[:, cols - TILE :], 5, 1),
                        pltpu.roll(cond_h[:, cols - TILE :], 6, 1),
                    ),
                ),
            )
            small_ref[16 * side + z : 16 * side + z + 1, :] = corner
        after = after + jnp.where(row == 0, edges[0], jnp.where(row == rows - 1, edges[1], 0.0))
        if z == 0:
            after = after - time_step * sink
        next_ref[z] = after
        packed = None
        for n, value in enumerate((after, temp, kappa, slope)):
            left = value[:, 0:TILE]
            right = pltpu.roll(value[:, cols - TILE :], n + 5, 1)
            left = pltpu.roll(left, n, 1) if n else left
            packed = left if packed is None else jnp.where(lane == n, left, packed)
            packed = jnp.where(lane == n + 4, right, packed)
        strip_ref[z * rows : (z + 1) * rows, :] = packed
    strips = strip_ref[...].T[0:8, :]
    corners = small_ref[...].T[0:8, :]

    lane_c = lax.broadcasted_iota(jnp.int32, (groups * rows, TILE), 1)
    right_flow = flow_all[:, cols - TILE :]
    pack = jnp.where(lane_c < 2, flow_all[:, 0:TILE], pltpu.roll(right_flow, 4, 1))
    pack = jnp.where(lane_c == 4, pltpu.roll(wall_all[:, 0:TILE], 4, 1), pack)
    pack = jnp.where(lane_c == 5, pltpu.roll(wall_all[:, cols - TILE :], 6, 1), pack)
    turned = pack.T
    flow_0, flow_1 = turned[0:1], turned[1:2]
    flow_m, flow_e = turned[2:3], turned[3:4]
    wall_0, wall_e = turned[4:5], turned[5:6]
    top = pick_rows(extra, one_hot(map_ref[...], 0, groups * rows))
    toward = extra[2:3]
    flux_0 = wall_0 * (top[0:1] - flow_0)
    flux_e = wall_e * (top[1:2] - flow_e)
    part_0 = (1.0 - courant) * flow_0 + courant * (1.0 - toward) * flow_1 + heat_gain * flux_0
    part_e = (1.0 - courant) * flow_e + courant * toward * flow_m + heat_gain * flux_e
    crow_ref[...] = jnp.zeros_like(crow_ref)
    crow_ref[0:1, :] = toward
    crow_ref[1:2, :] = flow_0
    crow_ref[2:3, :] = flow_e
    crow_ref[3:4, :] = wall_0
    crow_ref[4:5, :] = wall_e
    channels = groups * rows
    for ref, pick_right in ((sa_ref, place_even), (sb_ref, jnp.logical_not(place_even))):
        ref[...] = jnp.zeros_like(ref)
        ref[0:4, :] = jnp.where(pick_right, strips[4:8], strips[0:4])
        ref[4:6, 0:TILE] = jnp.where(pick_right, corners[4:6], corners[0:2])
        ref[4:5, channels : 2 * channels] = jnp.where(pick_right, extra[1:2], extra[0:1])
        ref[5:6, channels : 2 * channels] = jnp.where(pick_right, extra[4:5], extra[3:4])
        ref[6:7, 0:channels] = jnp.where(pick_right, flow_e, flow_0)
        ref[7:8, 0:channels] = jnp.where(pick_right, part_e, part_0)


def coolant_kernel(fw_ref, temp_ref, after_ref, crow_ref, map_ref, first_ref, second_ref):
    rows, cols = first_ref.shape
    channels = crow_ref.shape[1]
    chooser = one_hot(map_ref[...], lax.axis_index("grp") * rows, rows)
    toward = pick(chooser, jnp.broadcast_to(crow_ref[0:1, :], (TILE, channels)), ((1,), (1,)))
    toward = jnp.concatenate([toward] * (cols // TILE), 1) > 0.5
    lane = lax.broadcasted_iota(jnp.int32, (rows, cols), 1)

    def advance(flow, temp):
        before = jnp.where(lane == 0, 0.0, pltpu.roll(flow, 1, 1))
        after = jnp.where(lane == cols - 1, 0.0, pltpu.roll(flow, cols - 1, 1))
        flux = fw_ref[rows:, :] * (temp - flow)
        return flow - courant * (flow - jnp.where(toward, before, after)) + heat_gain * flux

    first = advance(fw_ref[0:rows, :], temp_ref[0])
    first_ref[...] = first
    second_ref[...] = advance(first, after_ref[0])


def close_kernel(
    temp_ref, kappa_ref, slope_ref, power_ref, yo_ref, ra_ref, rb_ref, sa_ref, sb_ref,
    flow_ref, fw_ref, crow_ref, map_ref, link_ref,
    out_hbm, tail_ref, add_ref, wide_ref, xt_ref, xc_ref, xf_ref, full_ref, out_ref, turn_ref, out_sem,
):
    layers, rows, cols = temp_ref.shape
    group, groups = lax.axis_index("grp"), lax.axis_size("grp")
    place, places = lax.axis_index("loop"), lax.axis_size("loop")
    even = lax.rem(place, 2) == 0
    channels = crow_ref.shape[1]
    low_open = jnp.where(group == 0, 0.0, 1.0)
    high_open = jnp.where(group == groups - 1, 0.0, 1.0)
    got_a, got_b, own_a, own_b = ra_ref[...], rb_ref[...], sa_ref[...], sb_ref[...]
    got = (jnp.where(even, got_b, got_a), jnp.where(even, got_a, got_b))
    own = (jnp.where(even, own_b, own_a), jnp.where(even, own_a, own_b))

    def turn(first, last, ref):
        wide_ref[0:1, 0 : first.shape[1]] = first
        wide_ref[TILE - 1 : TILE, 0 : last.shape[1]] = last
        ref[...] = wide_ref[:, 0 : ref.shape[0]].T

    wide_ref[...] = jnp.zeros_like(wide_ref)
    temps, conds, fluxes = [], [], []
    for side in range(2):
        temp_n, temp_o = got[side][1:2], own[side][1:2]
        cond_n = conduct(got[side][2:3], got[side][3:4], temp_n)
        cond_o = conduct(own[side][2:3], own[side][3:4], temp_o)
        flux = face(cond_o, cond_n, temp_o, temp_n)
        after = got[side][0:1] - flux
        temps.append(after)
        conds.append(conduct(got[side][2:3], got[side][3:4], after))
        fluxes.append(flux)
    turn(temps[0], temps[1], xt_ref)
    turn(conds[0], conds[1], xc_ref)
    turn(fluxes[0], fluxes[1], xf_ref)

    wide_ref[0:1, 0:TILE] = got[0][4:5, 0:TILE]
    wide_ref[TILE - 1 : TILE, 0:TILE] = got[1][4:5, 0:TILE]
    corner_t = wide_ref[:, 0:TILE].T
    wide_ref[0:1, 0:TILE] = got[0][5:6, 0:TILE]
    wide_ref[TILE - 1 : TILE, 0:TILE] = got[1][5:6, 0:TILE]
    corner_c = wide_ref[:, 0:TILE].T
    lane_l = lax.broadcasted_iota(jnp.int32, (layers, TILE), 1)
    halo = []
    for side in range(2):
        base = 4 * layers * side
        after = yo_ref[base : base + layers, :]
        before = yo_ref[base + layers : base + 2 * layers, :]
        kappa = yo_ref[base + 2 * layers : base + 3 * layers, :]
        slope = yo_ref[base + 3 * layers : base + 4 * layers, :]
        cond = conduct(kappa, slope, before)
        c_t, c_c = corner_t[16 * side : 16 * side + layers], corner_c[16 * side : 16 * side + layers]
        tiles = []
        for start, at in ((0, 0), (cols - TILE, TILE - 1)):
            flux = face(
                cond[:, start : start + TILE], c_c, before[:, start : start + TILE], c_t
            )
            tiles.append(after[:, start : start + TILE] + jnp.where(lane_l == at, flux, 0.0))
        after = jnp.concatenate([tiles[0], after[:, TILE : cols - TILE], tiles[1]], 1) if (
            cols > 2 * TILE
        ) else jnp.concatenate(tiles, 1)
        halo.append((after, conduct(kappa, slope, after)))

    lane = lax.broadcasted_iota(jnp.int32, (rows, TILE), 1)
    for z in range(layers):
        add = xf_ref[z * rows : (z + 1) * rows, :]
        full_ref[z] = temp_ref[z]
        full_ref[z, :, 0:TILE] = temp_ref[z, :, 0:TILE] + jnp.where(lane == 0, add, 0.0)
        full_ref[z, :, cols - TILE :] = temp_ref[z, :, cols - TILE :] + jnp.where(
            lane == TILE - 1, add, 0.0
        )

    toward_c = crow_ref[0:1, :]
    first_place = place == 0
    last_place = place == places - 1
    link = one_hot(link_ref[...], 0, channels)
    stack = jnp.concatenate(
        [got[0][6:7, 0:channels], got[1][6:7, 0:channels], crow_ref[1:3, :], crow_ref[4:8, :]], 0
    )
    moved = pick_rows(stack, link)
    own_0 = jnp.where(first_place, moved[2:3], stack[2:3])
    own_e = jnp.where(last_place, moved[3:4], stack[3:4])
    late_l = got[0][7:8, 0:channels] + courant * (1.0 - toward_c) * own_0
    late_r = got[1][7:8, 0:channels] + courant * toward_c * own_e
    late = jnp.concatenate([late_l, late_r, crow_ref[2:8, :]], 0)
    late_moved = pick_rows(late, link)
    edge_rows = (
        (jnp.where(first_place, moved[0:1], stack[0:1]), jnp.where(last_place, moved[1:2], stack[1:2])),
        (jnp.where(first_place, late_moved[0:1], late_l), jnp.where(last_place, late_moved[1:2], late_r)),
    )
    shift_0 = courant * toward_c * edge_rows[0][0]
    shift_e = courant * (1.0 - toward_c) * edge_rows[0][1]
    tops = [
        face(
            own[side][5:6, channels : 2 * channels], got[side][5:6, channels : 2 * channels],
            own[side][4:5, channels : 2 * channels], got[side][4:5, channels : 2 * channels],
        )
        for side in range(2)
    ]
    every = one_hot(map_ref[...], 0, channels)
    tops = pick_rows(jnp.concatenate(tops + [crow_ref[2:8, :]], 0), every)
    wall_0, wall_e = crow_ref[3:4, :], crow_ref[4:5, :]
    add_0 = (
        courant * toward_c * edge_rows[1][0]
        + ((1.0 - courant) - heat_gain * wall_0) * shift_0
        + heat_gain * wall_0 * tops[0:1]
    )
    add_e = (
        courant * (1.0 - toward_c) * edge_rows[1][1]
        + ((1.0 - courant) - heat_gain * wall_e) * shift_e
        + heat_gain * wall_e * tops[1:2]
    )
    wide_row = lax.broadcasted_iota(jnp.int32, (TILE, channels), 0)
    chooser = one_hot(map_ref[...], group * rows, rows)
    edge_y = pick(chooser, jnp.where(wide_row == 0, shift_0, shift_e), ((1,), (1,)))
    adds = jnp.where(wide_row == 0, add_0, jnp.where(wide_row == 1, courant * toward_c * shift_0, add_e))
    adds = jnp.where(wide_row == TILE - 2, courant * (1.0 - toward_c) * shift_e, adds)
    turn_ref[0:channels, :] = adds.T
    turn_ref[channels:, :] = jnp.broadcast_to(map_ref[...].astype(F32), (TILE, channels)).T
    add_ref[0:rows, :] = turn_ref[pl.ds(pl.multiple_of(group * rows, 8), rows), :]
    add_ref[rows:, :] = turn_ref[pl.ds(pl.multiple_of(channels + group * rows, 8), rows), :]
    pad = [jnp.zeros((rows, cols - 2 * TILE), F32)] if cols > 2 * TILE else []
    flow = flow_ref[...] + jnp.concatenate(
        [jnp.where(lane == 0, edge_y, 0.0)] + pad + [jnp.where(lane == TILE - 1, edge_y, 0.0)], 1
    )
    flux = fw_ref[rows:, :] * (full_ref[0] - flow)

    row8 = lax.broadcasted_iota(jnp.int32, (8, cols), 0)

    def emit(z, temp, cond, heat):
        result = temp + heat + time_step * power_ref[z]
        if z == 0:
            result = result - time_step * flux
        halo_t = xt_ref[z * rows : (z + 1) * rows, :]
        halo_c = xc_ref[z * rows : (z + 1) * rows, :]
        sides = []
        for start, at in ((0, 0), (cols - TILE, TILE - 1)):
            part = slice(start, start + TILE)
            extra = face(cond[:, part], halo_c, temp[:, part], halo_t)
            sides.append(jnp.where(lane == at, extra, 0.0))
        middle = [jnp.zeros((rows, cols - 2 * TILE), F32)] if cols > 2 * TILE else []
        result = result + jnp.concatenate([sides[0]] + middle + [sides[1]], 1)
        early = layers - tail_ref.shape[0]
        target, at_z = (out_ref, z) if z < early else (tail_ref, z - early)
        target[at_z] = result
        for side, opened, start, at in ((0, low_open, 0, 0), (1, high_open, rows - 8, 7)):
            part = slice(start, start + 8)
            extra = opened * face(
                cond[part], halo[side][1][z : z + 1], temp[part], halo[side][0][z : z + 1]
            )
            target[at_z, part, :] = result[part] + jnp.where(row8 == at, extra, 0.0)
        if z < early:
            copies.append(pltpu.make_async_copy(out_ref.at[z], out_hbm.at[z], out_sem.at[z]))
            copies[-1].start()

    copies = []
    closed_heat(full_ref, kappa_ref, slope_ref, emit)
    for copy in copies:
        copy.wait()


def return_kernel(
    part_hbm, tail_ref, own_ref, core_ref, cross_ref, relay_ref, add_ref,
    out_hbm, flow_hbm, all_ref, out_ref, sem,
):
    rows, cols = out_ref.shape
    layers, late = out_hbm.shape[0], tail_ref.shape[0]
    tail = pltpu.make_async_copy(tail_ref, out_hbm.at[layers - late : layers], sem.at[0])
    tail.start()
    group, groups = lax.axis_index("grp"), lax.axis_size("grp")
    beside = group + 1 - 2 * lax.rem(group, 2)
    for ref, owner in (
        (own_ref, group), (core_ref, beside), (cross_ref, groups - 1 - group), (relay_ref, groups - 1 - beside),
    ):
        all_ref[pl.ds(pl.multiple_of(owner * rows, 8), rows), :] = ref[...]
    lane = lax.broadcasted_iota(jnp.int32, (rows, TILE), 1)
    adds, row = add_ref[0:rows, :], add_ref[rows:, :]
    channels = groups * rows
    chooser = jnp.concatenate(
        [jnp.where(row == (lane + start).astype(F32), 1.0, 0.0) for start in range(0, channels, TILE)], 1
    ).astype(BF16)
    flow = pick(chooser, all_ref[...], ((1,), (0,)))
    pad = [jnp.zeros((rows, cols - 2 * TILE), F32)] if cols > 2 * TILE else []
    out_ref[...] = flow + jnp.concatenate(
        [jnp.where(lane < 2, adds, 0.0)] + pad + [jnp.where(lane >= TILE - 2, adds, 0.0)], 1
    )
    back = pltpu.make_async_copy(out_ref, flow_hbm, sem.at[1])
    back.start()
    tail.wait()
    back.wait()


def pairs(count, first, closed):
    swaps = []
    for low in range(first, count, 2):
        high = low + 1
        if high == count:
            if not closed:
                continue
            high = 0
        swaps += [(low, high), (high, low)]
    return swaps


def shards(
    solid_temp, kappa, slope, power, coolant_temp, wall_coeff, channel_map, flow_dir, loop_link
):
    groups, places = lax.axis_size("grp"), lax.axis_size("loop")
    layers, rows, cols = solid_temp.shape
    channels = groups * rows
    strip = layers * rows
    params = pltpu.CompilerParams(vmem_limit_bytes=48 * 1024 * 1024)

    def shape(*dims):
        return jax.ShapeDtypeStruct(dims, F32)

    def call(body, outs, scratch, *args, far=0, outs_far=0, cost=None, alias={}):
        return pl.pallas_call(
            body,
            out_shape=outs,
            in_specs=[pl.BlockSpec(memory_space=pltpu.HBM)] * far + [pl.BlockSpec(memory_space=pltpu.VMEM)] * (len(args) - far),
            out_specs=[pl.BlockSpec(memory_space=pltpu.HBM)] * outs_far
            + [pl.BlockSpec(memory_space=pltpu.VMEM)] * (len(outs) - outs_far),
            scratch_shapes=scratch,
            compiler_params=params,
            cost_estimate=cost,
            input_output_aliases=alias,
        )(*[pltpu.with_memory_space_constraint(arg, pltpu.HBM) for arg in args[:far]], *args[far:])

    def vmem(*dims):
        return pltpu.VMEM(dims, F32)

    heavy = pl.CostEstimate(
        flops=30 * layers * rows * cols, bytes_accessed=36 * layers * rows * cols, transcendentals=0
    )
    block = shape(layers, rows, cols)
    share = shape(2 * rows + 8, cols)
    wide = shape(2 * rows + 8 + 4 * layers, cols)
    index = jax.ShapeDtypeStruct((1, channels), jnp.int32)
    core, cross, step, map_row, link_row = call(
        pack_kernel,
        (wide, share, shape(4 * layers, cols), index, index),
        [
            vmem(layers, 16, cols), vmem(layers, 16, cols), vmem(layers, 16, cols), vmem(layers, 16, cols),
            vmem(3, rows, cols), vmem(TILE, TILE), vmem(8, cols), pltpu.VMEM((1, rows), jnp.int32),
            pltpu.SemaphoreType.DMA((4, 2)), pltpu.SemaphoreType.DMA((3,)), pltpu.SemaphoreType.DMA((2, 2)),
            pltpu.SemaphoreType.DMA((3,)),
        ],
        solid_temp, kappa, slope, power, coolant_temp, wall_coeff, flow_dir.reshape(1, rows),
        channel_map, loop_link.reshape(1, channels),
        far=9,
    )
    beside = [(i, i + 1 - 2 * (i % 2)) for i in range(groups)]
    across = [(i, groups - 1 - i) for i in range(groups)]
    got_cross = lax.ppermute(cross, "grp", across)
    got_step = lax.ppermute(step, "grp", pairs(groups, 1, False))
    got_core = lax.ppermute(core, "grp", beside)
    first, temp, kappa, slope, power = call(
        open_kernel,
        (block, block, block, block, block),
        [pltpu.SemaphoreType.DMA((4, layers // CHUNK))],
        solid_temp, kappa, slope, power, map_row,
        far=4,
        cost=heavy,
    )
    got_cross, got_step, first = lax.optimization_barrier((got_cross, got_step, first))
    relay = lax.ppermute(got_cross, "grp", beside)
    after, yo, sa, sb, fw, crow = call(
        edge_kernel,
        (
            block, shape(8 * layers, cols), shape(24, strip), shape(24, strip),
            shape(2 * rows, cols), shape(8, channels),
        ),
        [vmem(strip, TILE), vmem(TILE, TILE), vmem(channels, 2 * cols)],
        first, temp, kappa, slope, core, got_core, got_cross, relay, got_step, map_row,
    )
    ra = lax.ppermute(sa, "loop", pairs(places, 0, True))
    rb = lax.ppermute(sb, "loop", pairs(places, 1, True))
    flow1, flow = call(
        coolant_kernel, (shape(rows, cols), shape(rows, cols)), [], fw, temp, after, crow, map_row,
    )
    got_across = lax.ppermute(flow, "grp", across)
    got_over = lax.ppermute(flow, "grp", [(i, (i + groups // 2) % groups) for i in range(groups)])
    got_beside = lax.ppermute(flow, "grp", beside)
    late = layers // 3
    out, tail, adds = call(
        close_kernel,
        (block, shape(late, rows, cols), shape(2 * rows, TILE)),
        [
            vmem(TILE, strip), vmem(strip, TILE), vmem(strip, TILE), vmem(strip, TILE),
            vmem(layers, rows, cols), vmem(layers - late, rows, cols), vmem(2 * channels, TILE),
            pltpu.SemaphoreType.DMA((layers - late,)),
        ],
        after, kappa, slope, power, yo, ra, rb, sa, sb, flow1, fw, crow, map_row, link_row,
        outs_far=1,
        cost=heavy,
    )
    return call(
        return_kernel,
        (block, shape(rows, cols)),
        [vmem(channels, cols), vmem(rows, cols), pltpu.SemaphoreType.DMA((2,))],
        out, tail, flow, got_beside, got_across, got_over, adds,
        far=1,
        outs_far=2,
        alias={0: 0},
    )


def solution(mesh):
    block = P(None, "grp", "loop")
    plane = P("grp", "loop")
    return jax.shard_map(
        shards,
        mesh=mesh,
        in_specs=(block, block, block, block, plane, plane, P("loop", None), P("grp"), P()),
        out_specs=(block, plane),
        check_vma=False,
    )
```

```python
import jax
import jax.numpy as jnp
from jax import lax
from jax.experimental import pallas as pl
from jax.experimental.pallas import tpu as pltpu
from jax.sharding import PartitionSpec as P

time_step = 0.06
courant = 0.5
heat_gain = 0.5
TILE = 128
CHUNK = 4
F32 = jnp.float32
BF16 = jnp.bfloat16


def split3(value):
    high = value.astype(BF16)
    rest = value - high.astype(F32)
    middle = rest.astype(BF16)
    low = (rest - middle.astype(F32)).astype(BF16)
    return high, middle, low


def pick(chooser, value, dims):
    total = None
    for part in split3(value):
        term = lax.dot_general(chooser, part, (dims, ((), ())), preferred_element_type=F32)
        total = term if total is None else total + term
    return total


def pick_rows(value, chooser):
    total = None
    for part in split3(value):
        term = lax.dot_general(part, chooser, (((1,), (0,)), ((), ())), preferred_element_type=F32)
        total = term if total is None else total + term
    return total


def one_hot(index_row, first, count):
    shape = (count, index_row.shape[1])
    here = lax.broadcasted_iota(jnp.int32, shape, 0) + first
    return jnp.where(index_row == here, 1.0, 0.0).astype(BF16)


def conduct(kappa, slope, temp):
    return (0.5 * time_step) * kappa * (1.0 + slope * temp)


def face(cond_a, cond_b, temp_a, temp_b):
    return (cond_a + cond_b) * (temp_b - temp_a)


def closed_heat(temp_ref, kappa_ref, slope_ref, emit, ready=lambda z: None):
    layers, rows, cols = temp_ref.shape
    lane = lax.broadcasted_iota(jnp.int32, (rows, cols), 1)
    row = lax.broadcasted_iota(jnp.int32, (rows, cols), 0)
    ready(0)
    temp = temp_ref[0]
    cond = conduct(kappa_ref[0], slope_ref[0], temp)
    flux_below = None
    for z in range(layers):
        if z + 1 < layers:
            ready(z + 1)
        flux_x = face(cond, pltpu.roll(cond, cols - 1, 1), temp, pltpu.roll(temp, cols - 1, 1))
        flux_x = jnp.where(lane == cols - 1, 0.0, flux_x)
        heat = flux_x - pltpu.roll(flux_x, 1, 1)
        flux_y = face(cond, pltpu.roll(cond, rows - 1, 0), temp, pltpu.roll(temp, rows - 1, 0))
        flux_y = jnp.where(row == rows - 1, 0.0, flux_y)
        heat = heat + flux_y - pltpu.roll(flux_y, 1, 0)
        if flux_below is not None:
            heat = heat - flux_below
        if z + 1 < layers:
            temp_up = temp_ref[z + 1]
            cond_up = conduct(kappa_ref[z + 1], slope_ref[z + 1], temp_up)
            flux_below = face(cond, cond_up, temp, temp_up)
            heat = heat + flux_below
        emit(z, temp, cond, heat)
        if z + 1 < layers:
            temp, cond = temp_up, cond_up


def pack_kernel(
    temp_hbm, kappa_hbm, slope_hbm, power_hbm, flow_hbm, wall_hbm, dir_hbm, map_hbm, link_hbm,
    core_ref, cross_ref, step_ref, map_ref, link_ref,
    temp_ref, kappa_ref, slope_ref, power_ref, top_ref, tmp_ref, row_ref, dir_ref,
    block_sem, top_sem, share_sem, small_sem,
):
    layers, rows, cols = temp_hbm.shape
    share = 2 * rows + 8
    group = lax.axis_index("grp")
    even = lax.rem(group, 2) == 0
    copies = []
    for n, (source, target) in enumerate((
        (temp_hbm, temp_ref), (kappa_hbm, kappa_ref), (slope_hbm, slope_ref), (power_hbm, power_ref),
    )):
        copies.append(pltpu.make_async_copy(source.at[:, 0:8], target.at[:, 0:8], block_sem.at[n, 0]))
        copies.append(
            pltpu.make_async_copy(source.at[:, rows - 8 : rows], target.at[:, 8:16], block_sem.at[n, 1])
        )
    tops = [
        pltpu.make_async_copy(source.at[0], top_ref.at[n], top_sem.at[n])
        for n, source in enumerate((temp_hbm, kappa_hbm, slope_hbm))
    ]
    smalls = [
        pltpu.make_async_copy(source, target, small_sem.at[n])
        for n, (source, target) in enumerate(((dir_hbm, dir_ref), (map_hbm, map_ref), (link_hbm, link_ref)))
    ]
    for m, target in enumerate((core_ref, cross_ref)):
        smalls.append(pltpu.make_async_copy(flow_hbm, target.at[0:rows], share_sem.at[m, 0]))
        smalls.append(pltpu.make_async_copy(wall_hbm, target.at[rows : 2 * rows], share_sem.at[m, 1]))
    for copy in copies + tops + smalls:
        copy.start()
    tmp_ref[...] = jnp.zeros_like(tmp_ref)
    row_ref[...] = jnp.zeros_like(row_ref)
    for copy in copies:
        copy.wait()

    def emit(z, temp, cond, heat):
        after = temp + heat + time_step * power_ref[z]
        for q, value in enumerate((after, temp, kappa_ref[z], slope_ref[z])):
            at = q * layers + z
            core_ref[share + at : share + at + 1, :] = jnp.where(even, value[15:16], value[0:1])
            step_ref[at : at + 1, :] = jnp.where(even, value[0:1], value[15:16])

    closed_heat(temp_ref, kappa_ref, slope_ref, emit)
    for copy in tops:
        copy.wait()
    temp = top_ref[0]
    cond = conduct(top_ref[1], top_ref[2], temp)
    lane = lax.broadcasted_iota(jnp.int32, (rows, TILE), 1)
    packed = jnp.where(lane == 0, temp[:, 0:TILE], pltpu.roll(temp[:, cols - TILE :], 2, 1))
    packed = jnp.where(lane == 3, pltpu.roll(cond[:, 0:TILE], 3, 1), packed)
    packed = jnp.where(lane == 4, pltpu.roll(cond[:, cols - TILE :], 5, 1), packed)
    tmp_ref[0:rows, :] = packed
    row_ref[0:8, 0:TILE] = tmp_ref[...].T[0:8, :]
    for copy in smalls:
        copy.wait()
    row_ref[2:3, 0:rows] = dir_ref[...].astype(F32)
    extra = pltpu.roll(row_ref[...], group * rows, 1)
    core_ref[2 * rows : share, :] = extra
    cross_ref[2 * rows : share, :] = extra


def open_kernel(
    temp_hbm, kappa_hbm, slope_hbm, power_hbm, after_ref,
    next_ref, temp_ref, kappa_ref, slope_ref, power_ref, block_sem,
):
    layers = temp_ref.shape[0]
    blocks = []
    for z in range(0, layers, CHUNK):
        part = pl.ds(z, CHUNK)
        blocks.append([
            pltpu.make_async_copy(source.at[part], target.at[part], block_sem.at[n, z // CHUNK])
            for n, (source, target) in enumerate((
                (temp_hbm, temp_ref), (kappa_hbm, kappa_ref), (slope_hbm, slope_ref), (power_hbm, power_ref),
            ))
        ])
    for block in blocks:
        for copy in block:
            copy.start()

    def ready(z):
        if z % CHUNK == 0:
            for copy in blocks[z // CHUNK]:
                copy.wait()

    def emit(z, temp, cond, heat):
        next_ref[z] = temp + heat + time_step * power_ref[z]

    closed_heat(temp_ref, kappa_ref, slope_ref, emit, ready)


def edge_kernel(
    first_ref, temp_ref, kappa_ref, slope_ref, core_ref, step_ref,
    next_ref, yo_ref, line_ref, strip_ref, small_ref,
):
    layers, rows, cols = temp_ref.shape
    span = 2 * rows + 8
    group, groups = lax.axis_index("grp"), lax.axis_size("grp")
    even = lax.rem(group, 2) == 0
    ya, yb = core_ref[span : span + 4 * layers, :], step_ref[...]
    low, high = jnp.where(even, yb, ya), jnp.where(even, ya, yb)
    yo_ref[0 : 4 * layers, :] = low
    yo_ref[4 * layers :, :] = high
    low_open = jnp.where(group == 0, 0.0, 1.0)
    high_open = jnp.where(group == groups - 1, 0.0, 1.0)

    row = lax.broadcasted_iota(jnp.int32, (rows, cols), 0)
    lane = lax.broadcasted_iota(jnp.int32, (rows, TILE), 1)
    small_ref[...] = jnp.zeros_like(small_ref)
    lane1 = lax.broadcasted_iota(jnp.int32, (1, TILE), 1)
    for z in range(layers):
        temp, kappa, slope = temp_ref[z], kappa_ref[z], slope_ref[z]
        after = first_ref[z]
        edges = []
        for side, base, at, opened in ((0, 0, 0, low_open), (1, 4 * layers, rows - 1, high_open)):
            temp_h = yo_ref[base + layers + z : base + layers + z + 1, :]
            cond_h = conduct(
                yo_ref[base + 2 * layers + z : base + 2 * layers + z + 1, :],
                yo_ref[base + 3 * layers + z : base + 3 * layers + z + 1, :],
                temp_h,
            )
            temp_e = temp[at : at + 1]
            cond_e = conduct(kappa[at : at + 1], slope[at : at + 1], temp_e)
            flux = opened * face(cond_e, cond_h, temp_e, temp_h)
            halo = yo_ref[base + z : base + z + 1, :] - flux
            yo_ref[base + z : base + z + 1, :] = halo
            edges.append(flux)
            corner = jnp.where(
                lane1 == 0,
                temp_h[:, 0:TILE],
                jnp.where(
                    lane1 == 1,
                    pltpu.roll(cond_h[:, 0:TILE], 1, 1),
                    jnp.where(
                        lane1 == 4,
                        pltpu.roll(temp_h[:, cols - TILE :], 5, 1),
                        pltpu.roll(cond_h[:, cols - TILE :], 6, 1),
                    ),
                ),
            )
            small_ref[16 * side + z : 16 * side + z + 1, :] = corner
        after = after + jnp.where(row == 0, edges[0], jnp.where(row == rows - 1, edges[1], 0.0))
        next_ref[z] = after
        packed = None
        for n, value in enumerate((after, temp, kappa, slope)):
            left = value[:, 0:TILE]
            right = pltpu.roll(value[:, cols - TILE :], n + 5, 1)
            left = pltpu.roll(left, n, 1) if n else left
            packed = left if packed is None else jnp.where(lane == n, left, packed)
            packed = jnp.where(lane == n + 4, right, packed)
        strip_ref[z * rows : (z + 1) * rows, :] = packed
    line_ref[0:8, :] = strip_ref[...].T[0:8, :]
    line_ref[8:16, 0:TILE] = small_ref[...].T[0:8, :]


def select_kernel(
    old_ref, halo_ref, line_ref, temp_ref, own_ref, core_ref, cross_ref, relay_ref, map_ref,
    top_ref, yo_ref, sa_ref, sb_ref, fw_ref, crow_ref, all_ref, tmp_ref,
):
    rows, cols = old_ref.shape[1:]
    layers = temp_ref.shape[0]
    span = 2 * rows + 8
    group, groups = lax.axis_index("grp"), lax.axis_size("grp")
    place_even = lax.rem(lax.axis_index("loop"), 2) == 0
    beside = group + 1 - 2 * lax.rem(group, 2)
    extra = jnp.zeros((8, cols), F32)
    for ref, owner in (
        (own_ref, group), (core_ref, beside), (cross_ref, groups - 1 - group), (relay_ref, groups - 1 - beside),
    ):
        part = pl.ds(pl.multiple_of(owner * rows, 8), rows)
        all_ref[part, 0:cols] = ref[0:rows, :]
        all_ref[part, cols : 2 * cols] = ref[rows : 2 * rows, :]
        extra = extra + ref[2 * rows : span, :]
    flow_all, wall_all = all_ref[:, 0:cols], all_ref[:, cols : 2 * cols]
    chooser = one_hot(map_ref[...], group * rows - 8, rows + 16)
    both = pick(chooser, all_ref[...], ((1,), (0,)))
    flow_y, wall_y = both[:, :cols], both[:, cols:]
    flow, wall = flow_y[8 : 8 + rows], wall_y[8 : 8 + rows]
    fw_ref[0:rows, :] = flow
    fw_ref[rows:, :] = wall
    sink = wall * (temp_ref[0] - flow)
    for base, at in ((0, 7), (4 * layers, 8 + rows)):
        temp = halo_ref[base + layers : base + layers + 1, :]
        heat = wall_y[at : at + 1] * (temp - flow_y[at : at + 1])
        yo_ref[base : base + 8, :] = halo_ref[base : base + 8, :]
        yo_ref[base : base + 1, :] = halo_ref[base : base + 1, :] - time_step * heat
    top_ref[0] = old_ref[0] - time_step * sink
    lane = lax.broadcasted_iota(jnp.int32, (rows, TILE), 1)
    tmp_ref[...] = jnp.zeros_like(tmp_ref)
    tmp_ref[0:rows, :] = jnp.where(lane == 0, sink[:, 0:TILE], pltpu.roll(sink[:, cols - TILE :], 2, 1))
    sunk = tmp_ref[...].T[0:8, :]
    lane_c = lax.broadcasted_iota(jnp.int32, (groups * rows, TILE), 1)
    right_flow = flow_all[:, cols - TILE :]
    pack = jnp.where(lane_c < 2, flow_all[:, 0:TILE], pltpu.roll(right_flow, 4, 1))
    pack = jnp.where(lane_c == 4, pltpu.roll(wall_all[:, 0:TILE], 4, 1), pack)
    pack = jnp.where(lane_c == 5, pltpu.roll(wall_all[:, cols - TILE :], 6, 1), pack)
    turned = pack.T
    flow_0, flow_1 = turned[0:1], turned[1:2]
    flow_m, flow_e = turned[2:3], turned[3:4]
    wall_0, wall_e = turned[4:5], turned[5:6]
    top = pick_rows(extra, one_hot(map_ref[...], 0, groups * rows))
    toward = extra[2:3]
    flux_0 = wall_0 * (top[0:1] - flow_0)
    flux_e = wall_e * (top[1:2] - flow_e)
    part_0 = (1.0 - courant) * flow_0 + courant * (1.0 - toward) * flow_1 + heat_gain * flux_0
    part_e = (1.0 - courant) * flow_e + courant * toward * flow_m + heat_gain * flux_e
    crow_ref[...] = jnp.zeros_like(crow_ref)
    crow_ref[0:1, :] = toward
    crow_ref[1:2, :] = flow_0
    crow_ref[2:3, :] = flow_e
    crow_ref[3:4, :] = wall_0
    crow_ref[4:5, :] = wall_e
    channels = groups * rows
    for ref, pick_right in ((sa_ref, place_even), (sb_ref, jnp.logical_not(place_even))):
        ref[...] = jnp.zeros_like(ref)
        ref[0:4, :] = jnp.where(pick_right, line_ref[4:8, :], line_ref[0:4, :])
        ref[0:1, 0:rows] = ref[0:1, 0:rows] - time_step * jnp.where(
            pick_right, sunk[1:2, 0:rows], sunk[0:1, 0:rows]
        )
        ref[4:6, 0:TILE] = jnp.where(pick_right, line_ref[12:14, 0:TILE], line_ref[8:10, 0:TILE])
        ref[4:5, channels : 2 * channels] = jnp.where(pick_right, extra[1:2], extra[0:1])
        ref[5:6, channels : 2 * channels] = jnp.where(pick_right, extra[4:5], extra[3:4])
        ref[6:7, 0:channels] = jnp.where(pick_right, flow_e, flow_0)
        ref[7:8, 0:channels] = jnp.where(pick_right, part_e, part_0)


def coolant_kernel(fw_ref, temp_ref, after_ref, crow_ref, map_ref, first_ref, second_ref):
    rows, cols = first_ref.shape
    channels = crow_ref.shape[1]
    chooser = one_hot(map_ref[...], lax.axis_index("grp") * rows, rows)
    toward = pick(chooser, jnp.broadcast_to(crow_ref[0:1, :], (TILE, channels)), ((1,), (1,)))
    toward = jnp.concatenate([toward] * (cols // TILE), 1) > 0.5
    lane = lax.broadcasted_iota(jnp.int32, (rows, cols), 1)

    def advance(flow, temp):
        before = jnp.where(lane == 0, 0.0, pltpu.roll(flow, 1, 1))
        after = jnp.where(lane == cols - 1, 0.0, pltpu.roll(flow, cols - 1, 1))
        flux = fw_ref[rows:, :] * (temp - flow)
        return flow - courant * (flow - jnp.where(toward, before, after)) + heat_gain * flux

    first = advance(fw_ref[0:rows, :], temp_ref[0])
    first_ref[...] = first
    second_ref[...] = advance(first, after_ref[0])


def close_kernel(
    temp_ref, kappa_ref, slope_ref, power_ref, yo_ref, ra_ref, rb_ref, sa_ref, sb_ref,
    flow_ref, fw_ref, crow_ref, map_ref, link_ref,
    out_hbm, tail_ref, add_ref, wide_ref, xt_ref, xc_ref, xf_ref, full_ref, out_ref, turn_ref, out_sem,
):
    layers, rows, cols = temp_ref.shape
    group, groups = lax.axis_index("grp"), lax.axis_size("grp")
    place, places = lax.axis_index("loop"), lax.axis_size("loop")
    even = lax.rem(place, 2) == 0
    channels = crow_ref.shape[1]
    low_open = jnp.where(group == 0, 0.0, 1.0)
    high_open = jnp.where(group == groups - 1, 0.0, 1.0)
    got_a, got_b, own_a, own_b = ra_ref[...], rb_ref[...], sa_ref[...], sb_ref[...]
    got = (jnp.where(even, got_b, got_a), jnp.where(even, got_a, got_b))
    own = (jnp.where(even, own_b, own_a), jnp.where(even, own_a, own_b))

    def turn(first, last, ref):
        wide_ref[0:1, 0 : first.shape[1]] = first
        wide_ref[TILE - 1 : TILE, 0 : last.shape[1]] = last
        ref[...] = wide_ref[:, 0 : ref.shape[0]].T

    wide_ref[...] = jnp.zeros_like(wide_ref)
    temps, conds, fluxes = [], [], []
    for side in range(2):
        temp_n, temp_o = got[side][1:2], own[side][1:2]
        cond_n = conduct(got[side][2:3], got[side][3:4], temp_n)
        cond_o = conduct(own[side][2:3], own[side][3:4], temp_o)
        flux = face(cond_o, cond_n, temp_o, temp_n)
        after = got[side][0:1] - flux
        temps.append(after)
        conds.append(conduct(got[side][2:3], got[side][3:4], after))
        fluxes.append(flux)
    turn(temps[0], temps[1], xt_ref)
    turn(conds[0], conds[1], xc_ref)
    turn(fluxes[0], fluxes[1], xf_ref)

    wide_ref[0:1, 0:TILE] = got[0][4:5, 0:TILE]
    wide_ref[TILE - 1 : TILE, 0:TILE] = got[1][4:5, 0:TILE]
    corner_t = wide_ref[:, 0:TILE].T
    wide_ref[0:1, 0:TILE] = got[0][5:6, 0:TILE]
    wide_ref[TILE - 1 : TILE, 0:TILE] = got[1][5:6, 0:TILE]
    corner_c = wide_ref[:, 0:TILE].T
    lane_l = lax.broadcasted_iota(jnp.int32, (layers, TILE), 1)
    halo = []
    for side in range(2):
        base = 4 * layers * side
        after = yo_ref[base : base + layers, :]
        before = yo_ref[base + layers : base + 2 * layers, :]
        kappa = yo_ref[base + 2 * layers : base + 3 * layers, :]
        slope = yo_ref[base + 3 * layers : base + 4 * layers, :]
        cond = conduct(kappa, slope, before)
        c_t, c_c = corner_t[16 * side : 16 * side + layers], corner_c[16 * side : 16 * side + layers]
        tiles = []
        for start, at in ((0, 0), (cols - TILE, TILE - 1)):
            flux = face(
                cond[:, start : start + TILE], c_c, before[:, start : start + TILE], c_t
            )
            tiles.append(after[:, start : start + TILE] + jnp.where(lane_l == at, flux, 0.0))
        after = jnp.concatenate([tiles[0], after[:, TILE : cols - TILE], tiles[1]], 1) if (
            cols > 2 * TILE
        ) else jnp.concatenate(tiles, 1)
        halo.append((after, conduct(kappa, slope, after)))

    lane = lax.broadcasted_iota(jnp.int32, (rows, TILE), 1)
    for z in range(layers):
        add = xf_ref[z * rows : (z + 1) * rows, :]
        full_ref[z] = temp_ref[z]
        full_ref[z, :, 0:TILE] = temp_ref[z, :, 0:TILE] + jnp.where(lane == 0, add, 0.0)
        full_ref[z, :, cols - TILE :] = temp_ref[z, :, cols - TILE :] + jnp.where(
            lane == TILE - 1, add, 0.0
        )

    toward_c = crow_ref[0:1, :]
    first_place = place == 0
    last_place = place == places - 1
    link = one_hot(link_ref[...], 0, channels)
    stack = jnp.concatenate(
        [got[0][6:7, 0:channels], got[1][6:7, 0:channels], crow_ref[1:3, :], crow_ref[4:8, :]], 0
    )
    moved = pick_rows(stack, link)
    own_0 = jnp.where(first_place, moved[2:3], stack[2:3])
    own_e = jnp.where(last_place, moved[3:4], stack[3:4])
    late_l = got[0][7:8, 0:channels] + courant * (1.0 - toward_c) * own_0
    late_r = got[1][7:8, 0:channels] + courant * toward_c * own_e
    late = jnp.concatenate([late_l, late_r, crow_ref[2:8, :]], 0)
    late_moved = pick_rows(late, link)
    edge_rows = (
        (jnp.where(first_place, moved[0:1], stack[0:1]), jnp.where(last_place, moved[1:2], stack[1:2])),
        (jnp.where(first_place, late_moved[0:1], late_l), jnp.where(last_place, late_moved[1:2], late_r)),
    )
    shift_0 = courant * toward_c * edge_rows[0][0]
    shift_e = courant * (1.0 - toward_c) * edge_rows[0][1]
    tops = [
        face(
            own[side][5:6, channels : 2 * channels], got[side][5:6, channels : 2 * channels],
            own[side][4:5, channels : 2 * channels], got[side][4:5, channels : 2 * channels],
        )
        for side in range(2)
    ]
    every = one_hot(map_ref[...], 0, channels)
    tops = pick_rows(jnp.concatenate(tops + [crow_ref[2:8, :]], 0), every)
    wall_0, wall_e = crow_ref[3:4, :], crow_ref[4:5, :]
    add_0 = (
        courant * toward_c * edge_rows[1][0]
        + ((1.0 - courant) - heat_gain * wall_0) * shift_0
        + heat_gain * wall_0 * tops[0:1]
    )
    add_e = (
        courant * (1.0 - toward_c) * edge_rows[1][1]
        + ((1.0 - courant) - heat_gain * wall_e) * shift_e
        + heat_gain * wall_e * tops[1:2]
    )
    wide_row = lax.broadcasted_iota(jnp.int32, (TILE, channels), 0)
    chooser = one_hot(map_ref[...], group * rows, rows)
    edge_y = pick(chooser, jnp.where(wide_row == 0, shift_0, shift_e), ((1,), (1,)))
    adds = jnp.where(wide_row == 0, add_0, jnp.where(wide_row == 1, courant * toward_c * shift_0, add_e))
    adds = jnp.where(wide_row == TILE - 2, courant * (1.0 - toward_c) * shift_e, adds)
    turn_ref[0:channels, :] = adds.T
    turn_ref[channels:, :] = jnp.broadcast_to(map_ref[...].astype(F32), (TILE, channels)).T
    add_ref[0:rows, :] = turn_ref[pl.ds(pl.multiple_of(group * rows, 8), rows), :]
    add_ref[rows:, :] = turn_ref[pl.ds(pl.multiple_of(channels + group * rows, 8), rows), :]
    pad = [jnp.zeros((rows, cols - 2 * TILE), F32)] if cols > 2 * TILE else []
    flow = flow_ref[...] + jnp.concatenate(
        [jnp.where(lane == 0, edge_y, 0.0)] + pad + [jnp.where(lane == TILE - 1, edge_y, 0.0)], 1
    )
    flux = fw_ref[rows:, :] * (full_ref[0] - flow)

    row8 = lax.broadcasted_iota(jnp.int32, (8, cols), 0)

    def emit(z, temp, cond, heat):
        result = temp + heat + time_step * power_ref[z]
        if z == 0:
            result = result - time_step * flux
        halo_t = xt_ref[z * rows : (z + 1) * rows, :]
        halo_c = xc_ref[z * rows : (z + 1) * rows, :]
        sides = []
        for start, at in ((0, 0), (cols - TILE, TILE - 1)):
            part = slice(start, start + TILE)
            extra = face(cond[:, part], halo_c, temp[:, part], halo_t)
            sides.append(jnp.where(lane == at, extra, 0.0))
        middle = [jnp.zeros((rows, cols - 2 * TILE), F32)] if cols > 2 * TILE else []
        result = result + jnp.concatenate([sides[0]] + middle + [sides[1]], 1)
        early = layers - tail_ref.shape[0]
        target, at_z = (out_ref, z) if z < early else (tail_ref, z - early)
        target[at_z] = result
        for side, opened, start, at in ((0, low_open, 0, 0), (1, high_open, rows - 8, 7)):
            part = slice(start, start + 8)
            extra = opened * face(
                cond[part], halo[side][1][z : z + 1], temp[part], halo[side][0][z : z + 1]
            )
            target[at_z, part, :] = result[part] + jnp.where(row8 == at, extra, 0.0)
        if z < early:
            copies.append(pltpu.make_async_copy(out_ref.at[z], out_hbm.at[z], out_sem.at[z]))
            copies[-1].start()

    copies = []
    closed_heat(full_ref, kappa_ref, slope_ref, emit)
    for copy in copies:
        copy.wait()


def return_kernel(
    part_hbm, tail_ref, own_ref, core_ref, cross_ref, relay_ref, add_ref,
    out_hbm, flow_hbm, all_ref, out_ref, sem,
):
    rows, cols = out_ref.shape
    layers, late = out_hbm.shape[0], tail_ref.shape[0]
    tail = pltpu.make_async_copy(tail_ref, out_hbm.at[layers - late : layers], sem.at[0])
    tail.start()
    group, groups = lax.axis_index("grp"), lax.axis_size("grp")
    beside = group + 1 - 2 * lax.rem(group, 2)
    for ref, owner in (
        (own_ref, group), (core_ref, beside), (cross_ref, groups - 1 - group), (relay_ref, groups - 1 - beside),
    ):
        all_ref[pl.ds(pl.multiple_of(owner * rows, 8), rows), :] = ref[...]
    lane = lax.broadcasted_iota(jnp.int32, (rows, TILE), 1)
    adds, row = add_ref[0:rows, :], add_ref[rows:, :]
    channels = groups * rows
    chooser = jnp.concatenate(
        [jnp.where(row == (lane + start).astype(F32), 1.0, 0.0) for start in range(0, channels, TILE)], 1
    ).astype(BF16)
    flow = pick(chooser, all_ref[...], ((1,), (0,)))
    pad = [jnp.zeros((rows, cols - 2 * TILE), F32)] if cols > 2 * TILE else []
    out_ref[...] = flow + jnp.concatenate(
        [jnp.where(lane < 2, adds, 0.0)] + pad + [jnp.where(lane >= TILE - 2, adds, 0.0)], 1
    )
    back = pltpu.make_async_copy(out_ref, flow_hbm, sem.at[1])
    back.start()
    tail.wait()
    back.wait()


def pairs(count, first, closed):
    swaps = []
    for low in range(first, count, 2):
        high = low + 1
        if high == count:
            if not closed:
                continue
            high = 0
        swaps += [(low, high), (high, low)]
    return swaps


def shards(
    solid_temp, kappa, slope, power, coolant_temp, wall_coeff, channel_map, flow_dir, loop_link
):
    groups, places = lax.axis_size("grp"), lax.axis_size("loop")
    layers, rows, cols = solid_temp.shape
    channels = groups * rows
    strip = layers * rows
    params = pltpu.CompilerParams(vmem_limit_bytes=48 * 1024 * 1024)

    def shape(*dims):
        return jax.ShapeDtypeStruct(dims, F32)

    def call(body, outs, scratch, *args, far=0, outs_far=0, cost=None, alias={}):
        return pl.pallas_call(
            body,
            out_shape=outs,
            in_specs=[pl.BlockSpec(memory_space=pltpu.HBM)] * far + [pl.BlockSpec(memory_space=pltpu.VMEM)] * (len(args) - far),
            out_specs=[pl.BlockSpec(memory_space=pltpu.HBM)] * outs_far
            + [pl.BlockSpec(memory_space=pltpu.VMEM)] * (len(outs) - outs_far),
            scratch_shapes=scratch,
            compiler_params=params,
            cost_estimate=cost,
            input_output_aliases=alias,
        )(*[pltpu.with_memory_space_constraint(arg, pltpu.HBM) for arg in args[:far]], *args[far:])

    def vmem(*dims):
        return pltpu.VMEM(dims, F32)

    heavy = pl.CostEstimate(
        flops=30 * layers * rows * cols, bytes_accessed=36 * layers * rows * cols, transcendentals=0
    )
    block = shape(layers, rows, cols)
    share = shape(2 * rows + 8, cols)
    wide = shape(2 * rows + 8 + 4 * layers, cols)
    index = jax.ShapeDtypeStruct((1, channels), jnp.int32)
    core, cross, step, map_row, link_row = call(
        pack_kernel,
        (wide, share, shape(4 * layers, cols), index, index),
        [
            vmem(layers, 16, cols), vmem(layers, 16, cols), vmem(layers, 16, cols), vmem(layers, 16, cols),
            vmem(3, rows, cols), vmem(TILE, TILE), vmem(8, cols), pltpu.VMEM((1, rows), jnp.int32),
            pltpu.SemaphoreType.DMA((4, 2)), pltpu.SemaphoreType.DMA((3,)), pltpu.SemaphoreType.DMA((2, 2)),
            pltpu.SemaphoreType.DMA((3,)),
        ],
        solid_temp, kappa, slope, power, coolant_temp, wall_coeff, flow_dir.reshape(1, rows),
        channel_map, loop_link.reshape(1, channels),
        far=9,
    )
    beside = [(i, i + 1 - 2 * (i % 2)) for i in range(groups)]
    across = [(i, groups - 1 - i) for i in range(groups)]
    got_cross = lax.ppermute(cross, "grp", across)
    got_step = lax.ppermute(step, "grp", pairs(groups, 1, False))
    got_core = lax.ppermute(core, "grp", beside)
    first, temp, kappa, slope, power = call(
        open_kernel,
        (block, block, block, block, block),
        [pltpu.SemaphoreType.DMA((4, layers // CHUNK))],
        solid_temp, kappa, slope, power, map_row,
        far=4,
        cost=heavy,
    )
    got_cross, got_step, first = lax.optimization_barrier((got_cross, got_step, first))
    relay = lax.ppermute(got_cross, "grp", beside)
    after, yo, line = call(
        edge_kernel,
        (block, shape(8 * layers, cols), shape(16, strip)),
        [vmem(strip, TILE), vmem(TILE, TILE)],
        first, temp, kappa, slope, got_core, got_step,
        cost=heavy,
    )
    after, yo, sa, sb, fw, crow = call(
        select_kernel,
        (
            block, shape(8 * layers, cols), shape(24, strip), shape(24, strip),
            shape(2 * rows, cols), shape(8, channels),
        ),
        [vmem(channels, 2 * cols), vmem(TILE, TILE)],
        after, yo, line, temp, core, got_core, got_cross, relay, map_row,
        alias={0: 0, 1: 1},
    )
    ra = lax.ppermute(sa, "loop", pairs(places, 0, True))
    rb = lax.ppermute(sb, "loop", pairs(places, 1, True))
    flow1, flow = call(
        coolant_kernel, (shape(rows, cols), shape(rows, cols)), [], fw, temp, after, crow, map_row,
    )
    got_across = lax.ppermute(flow, "grp", across)
    got_over = lax.ppermute(flow, "grp", [(i, (i + groups // 2) % groups) for i in range(groups)])
    got_beside = lax.ppermute(flow, "grp", beside)
    late = layers // 3
    out, tail, adds = call(
        close_kernel,
        (block, shape(late, rows, cols), shape(2 * rows, TILE)),
        [
            vmem(TILE, strip), vmem(strip, TILE), vmem(strip, TILE), vmem(strip, TILE),
            vmem(layers, rows, cols), vmem(layers - late, rows, cols), vmem(2 * channels, TILE),
            pltpu.SemaphoreType.DMA((layers - late,)),
        ],
        after, kappa, slope, power, yo, ra, rb, sa, sb, flow1, fw, crow, map_row, link_row,
        outs_far=1,
        cost=heavy,
    )
    return call(
        return_kernel,
        (block, shape(rows, cols)),
        [vmem(channels, cols), vmem(rows, cols), pltpu.SemaphoreType.DMA((2,))],
        out, tail, flow, got_beside, got_across, got_over, adds,
        far=1,
        outs_far=2,
        alias={0: 0},
    )


def solution(mesh):
    block = P(None, "grp", "loop")
    plane = P("grp", "loop")
    return jax.shard_map(
        shards,
        mesh=mesh,
        in_specs=(block, block, block, block, plane, plane, P("loop", None), P("grp"), P()),
        out_specs=(block, plane),
        check_vma=False,
    )
```

```python
import jax
import jax.numpy as jnp
from jax import lax
from jax.experimental import pallas as pl
from jax.experimental.pallas import tpu as pltpu
from jax.sharding import PartitionSpec as P

time_step = 0.06
courant = 0.5
heat_gain = 0.5
TILE = 128
CHUNK = 4
F32 = jnp.float32
BF16 = jnp.bfloat16


def split3(value):
    high = value.astype(BF16)
    rest = value - high.astype(F32)
    middle = rest.astype(BF16)
    low = (rest - middle.astype(F32)).astype(BF16)
    return high, middle, low


def pick(chooser, value, dims):
    total = None
    for part in split3(value):
        term = lax.dot_general(chooser, part, (dims, ((), ())), preferred_element_type=F32)
        total = term if total is None else total + term
    return total


def pick_rows(value, chooser):
    total = None
    for part in split3(value):
        term = lax.dot_general(part, chooser, (((1,), (0,)), ((), ())), preferred_element_type=F32)
        total = term if total is None else total + term
    return total


def one_hot(index_row, first, count):
    shape = (count, index_row.shape[1])
    here = lax.broadcasted_iota(jnp.int32, shape, 0) + first
    return jnp.where(index_row == here, 1.0, 0.0).astype(BF16)


def conduct(kappa, slope, temp):
    return (0.5 * time_step) * kappa * (1.0 + slope * temp)


def face(cond_a, cond_b, temp_a, temp_b):
    return (cond_a + cond_b) * (temp_b - temp_a)


def closed_heat(temp_ref, kappa_ref, slope_ref, emit, ready=lambda z: None):
    layers, rows, cols = temp_ref.shape
    lane = lax.broadcasted_iota(jnp.int32, (rows, cols), 1)
    row = lax.broadcasted_iota(jnp.int32, (rows, cols), 0)
    ready(0)
    temp = temp_ref[0]
    cond = conduct(kappa_ref[0], slope_ref[0], temp)
    flux_below = None
    for z in range(layers):
        if z + 1 < layers:
            ready(z + 1)
        flux_x = face(cond, pltpu.roll(cond, cols - 1, 1), temp, pltpu.roll(temp, cols - 1, 1))
        flux_x = jnp.where(lane == cols - 1, 0.0, flux_x)
        heat = flux_x - pltpu.roll(flux_x, 1, 1)
        flux_y = face(cond, pltpu.roll(cond, rows - 1, 0), temp, pltpu.roll(temp, rows - 1, 0))
        flux_y = jnp.where(row == rows - 1, 0.0, flux_y)
        heat = heat + flux_y - pltpu.roll(flux_y, 1, 0)
        if flux_below is not None:
            heat = heat - flux_below
        if z + 1 < layers:
            temp_up = temp_ref[z + 1]
            cond_up = conduct(kappa_ref[z + 1], slope_ref[z + 1], temp_up)
            flux_below = face(cond, cond_up, temp, temp_up)
            heat = heat + flux_below
        emit(z, temp, cond, heat)
        if z + 1 < layers:
            temp, cond = temp_up, cond_up


def pack_kernel(
    temp_hbm, kappa_hbm, slope_hbm, power_hbm, flow_hbm, wall_hbm, dir_hbm, map_hbm, link_hbm,
    core_ref, cross_ref, step_ref, map_ref, link_ref,
    temp_ref, kappa_ref, slope_ref, power_ref, top_ref, tmp_ref, row_ref, dir_ref,
    block_sem, top_sem, share_sem, small_sem,
):
    layers, rows, cols = temp_hbm.shape
    share = 2 * rows + 8
    group = lax.axis_index("grp")
    even = lax.rem(group, 2) == 0
    copies = []
    for n, (source, target) in enumerate((
        (temp_hbm, temp_ref), (kappa_hbm, kappa_ref), (slope_hbm, slope_ref), (power_hbm, power_ref),
    )):
        copies.append(pltpu.make_async_copy(source.at[:, 0:2], target.at[:, 0:2], block_sem.at[n, 0]))
        copies.append(
            pltpu.make_async_copy(source.at[:, rows - 2 : rows], target.at[:, 6:8], block_sem.at[n, 1])
        )
    tops = [
        pltpu.make_async_copy(source.at[0], top_ref.at[n], top_sem.at[n])
        for n, source in enumerate((temp_hbm, kappa_hbm, slope_hbm))
    ]
    smalls = [
        pltpu.make_async_copy(source, target, small_sem.at[n])
        for n, (source, target) in enumerate(((dir_hbm, dir_ref), (map_hbm, map_ref), (link_hbm, link_ref)))
    ]
    smalls.append(pltpu.make_async_copy(flow_hbm, cross_ref.at[0:rows], share_sem.at[0]))
    smalls.append(pltpu.make_async_copy(wall_hbm, cross_ref.at[rows : 2 * rows], share_sem.at[1]))
    for copy in copies + tops + smalls:
        copy.start()
    tmp_ref[...] = jnp.zeros_like(tmp_ref)
    row_ref[...] = jnp.zeros_like(row_ref)
    for copy in copies:
        copy.wait()

    def emit(z, temp, cond, heat):
        after = temp + heat + time_step * power_ref[z]
        for q, value in enumerate((after, temp, kappa_ref[z], slope_ref[z])):
            at = q * layers + z
            core_ref[share + at : share + at + 1, :] = jnp.where(even, value[7:8], value[0:1])
            step_ref[at : at + 1, :] = jnp.where(even, value[0:1], value[7:8])

    closed_heat(temp_ref, kappa_ref, slope_ref, emit)
    for copy in tops:
        copy.wait()
    temp = top_ref[0]
    cond = conduct(top_ref[1], top_ref[2], temp)
    lane = lax.broadcasted_iota(jnp.int32, (rows, TILE), 1)
    packed = jnp.where(lane == 0, temp[:, 0:TILE], pltpu.roll(temp[:, cols - TILE :], 2, 1))
    packed = jnp.where(lane == 3, pltpu.roll(cond[:, 0:TILE], 3, 1), packed)
    packed = jnp.where(lane == 4, pltpu.roll(cond[:, cols - TILE :], 5, 1), packed)
    tmp_ref[0:rows, :] = packed
    row_ref[0:8, 0:TILE] = tmp_ref[...].T[0:8, :]
    for copy in smalls:
        copy.wait()
    row_ref[2:3, 0:rows] = dir_ref[...].astype(F32)
    extra = pltpu.roll(row_ref[...], group * rows, 1)
    cross_ref[2 * rows : share, :] = extra
    core_ref[2 * rows : share, :] = extra
    core_ref[0 : 2 * rows, :] = cross_ref[0 : 2 * rows, :]


def open_kernel(
    temp_hbm, kappa_hbm, slope_hbm, power_hbm, after_ref,
    next_ref, temp_ref, kappa_ref, slope_ref, power_ref, block_sem,
):
    layers = temp_ref.shape[0]
    blocks = []
    for z in range(0, layers, CHUNK):
        part = pl.ds(z, CHUNK)
        blocks.append([
            pltpu.make_async_copy(source.at[part], target.at[part], block_sem.at[n, z // CHUNK])
            for n, (source, target) in enumerate((
                (temp_hbm, temp_ref), (kappa_hbm, kappa_ref), (slope_hbm, slope_ref), (power_hbm, power_ref),
            ))
        ])
    for block in blocks:
        for copy in block:
            copy.start()

    def ready(z):
        if z % CHUNK == 0:
            for copy in blocks[z // CHUNK]:
                copy.wait()

    def emit(z, temp, cond, heat):
        next_ref[z] = temp + heat + time_step * power_ref[z]

    closed_heat(temp_ref, kappa_ref, slope_ref, emit, ready)


def edge_kernel(
    first_ref, temp_ref, kappa_ref, slope_ref, core_ref, step_ref,
    next_ref, yo_ref, line_ref, strip_ref, small_ref,
):
    layers, rows, cols = temp_ref.shape
    span = 2 * rows + 8
    group, groups = lax.axis_index("grp"), lax.axis_size("grp")
    even = lax.rem(group, 2) == 0
    ya, yb = core_ref[span : span + 4 * layers, :], step_ref[...]
    low, high = jnp.where(even, yb, ya), jnp.where(even, ya, yb)
    yo_ref[0 : 4 * layers, :] = low
    yo_ref[4 * layers :, :] = high
    low_open = jnp.where(group == 0, 0.0, 1.0)
    high_open = jnp.where(group == groups - 1, 0.0, 1.0)

    row = lax.broadcasted_iota(jnp.int32, (rows, cols), 0)
    lane = lax.broadcasted_iota(jnp.int32, (rows, TILE), 1)
    small_ref[...] = jnp.zeros_like(small_ref)
    lane1 = lax.broadcasted_iota(jnp.int32, (1, TILE), 1)
    for z in range(layers):
        temp, kappa, slope = temp_ref[z], kappa_ref[z], slope_ref[z]
        after = first_ref[z]
        edges = []
        for side, base, at, opened in ((0, 0, 0, low_open), (1, 4 * layers, rows - 1, high_open)):
            temp_h = yo_ref[base + layers + z : base + layers + z + 1, :]
            cond_h = conduct(
                yo_ref[base + 2 * layers + z : base + 2 * layers + z + 1, :],
                yo_ref[base + 3 * layers + z : base + 3 * layers + z + 1, :],
                temp_h,
            )
            temp_e = temp[at : at + 1]
            cond_e = conduct(kappa[at : at + 1], slope[at : at + 1], temp_e)
            flux = opened * face(cond_e, cond_h, temp_e, temp_h)
            halo = yo_ref[base + z : base + z + 1, :] - flux
            yo_ref[base + z : base + z + 1, :] = halo
            edges.append(flux)
            corner = jnp.where(
                lane1 == 0,
                temp_h[:, 0:TILE],
                jnp.where(
                    lane1 == 1,
                    pltpu.roll(cond_h[:, 0:TILE], 1, 1),
                    jnp.where(
                        lane1 == 4,
                        pltpu.roll(temp_h[:, cols - TILE :], 5, 1),
                        pltpu.roll(cond_h[:, cols - TILE :], 6, 1),
                    ),
                ),
            )
            small_ref[16 * side + z : 16 * side + z + 1, :] = corner
        after = after + jnp.where(row == 0, edges[0], jnp.where(row == rows - 1, edges[1], 0.0))
        next_ref[z] = after
        packed = None
        for n, value in enumerate((after, temp, kappa, slope)):
            left = value[:, 0:TILE]
            right = pltpu.roll(value[:, cols - TILE :], n + 5, 1)
            left = pltpu.roll(left, n, 1) if n else left
            packed = left if packed is None else jnp.where(lane == n, left, packed)
            packed = jnp.where(lane == n + 4, right, packed)
        strip_ref[z * rows : (z + 1) * rows, :] = packed
    line_ref[0:8, :] = strip_ref[...].T[0:8, :]
    line_ref[8:16, 0:TILE] = small_ref[...].T[0:8, :]


def select_kernel(
    old_ref, halo_ref, line_ref, temp_ref, own_ref, core_ref, cross_ref, relay_ref, map_ref,
    top_ref, yo_ref, sa_ref, sb_ref, fw_ref, crow_ref, all_ref, tmp_ref,
):
    rows, cols = old_ref.shape[1:]
    layers = temp_ref.shape[0]
    span = 2 * rows + 8
    group, groups = lax.axis_index("grp"), lax.axis_size("grp")
    place_even = lax.rem(lax.axis_index("loop"), 2) == 0
    beside = group + 1 - 2 * lax.rem(group, 2)
    extra = jnp.zeros((8, cols), F32)
    for ref, owner in (
        (own_ref, group), (core_ref, beside), (cross_ref, groups - 1 - group), (relay_ref, groups - 1 - beside),
    ):
        part = pl.ds(pl.multiple_of(owner * rows, 8), rows)
        all_ref[part, 0:cols] = ref[0:rows, :]
        all_ref[part, cols : 2 * cols] = ref[rows : 2 * rows, :]
        extra = extra + ref[2 * rows : span, :]
    flow_all, wall_all = all_ref[:, 0:cols], all_ref[:, cols : 2 * cols]
    chooser = one_hot(map_ref[...], group * rows - 8, rows + 16)
    both = pick(chooser, all_ref[...], ((1,), (0,)))
    flow_y, wall_y = both[:, :cols], both[:, cols:]
    flow, wall = flow_y[8 : 8 + rows], wall_y[8 : 8 + rows]
    fw_ref[0:rows, :] = flow
    fw_ref[rows:, :] = wall
    sink = wall * (temp_ref[0] - flow)
    for base, at in ((0, 7), (4 * layers, 8 + rows)):
        temp = halo_ref[base + layers : base + layers + 1, :]
        heat = wall_y[at : at + 1] * (temp - flow_y[at : at + 1])
        yo_ref[base : base + 8, :] = halo_ref[base : base + 8, :]
        yo_ref[base : base + 1, :] = halo_ref[base : base + 1, :] - time_step * heat
    top_ref[0] = old_ref[0] - time_step * sink
    lane = lax.broadcasted_iota(jnp.int32, (rows, TILE), 1)
    tmp_ref[...] = jnp.zeros_like(tmp_ref)
    tmp_ref[0:rows, :] = jnp.where(lane == 0, sink[:, 0:TILE], pltpu.roll(sink[:, cols - TILE :], 2, 1))
    sunk = tmp_ref[...].T[0:8, :]
    lane_c = lax.broadcasted_iota(jnp.int32, (groups * rows, TILE), 1)
    right_flow = flow_all[:, cols - TILE :]
    pack = jnp.where(lane_c < 2, flow_all[:, 0:TILE], pltpu.roll(right_flow, 4, 1))
    pack = jnp.where(lane_c == 4, pltpu.roll(wall_all[:, 0:TILE], 4, 1), pack)
    pack = jnp.where(lane_c == 5, pltpu.roll(wall_all[:, cols - TILE :], 6, 1), pack)
    turned = pack.T
    flow_0, flow_1 = turned[0:1], turned[1:2]
    flow_m, flow_e = turned[2:3], turned[3:4]
    wall_0, wall_e = turned[4:5], turned[5:6]
    top = pick_rows(extra, one_hot(map_ref[...], 0, groups * rows))
    toward = extra[2:3]
    flux_0 = wall_0 * (top[0:1] - flow_0)
    flux_e = wall_e * (top[1:2] - flow_e)
    part_0 = (1.0 - courant) * flow_0 + courant * (1.0 - toward) * flow_1 + heat_gain * flux_0
    part_e = (1.0 - courant) * flow_e + courant * toward * flow_m + heat_gain * flux_e
    crow_ref[...] = jnp.zeros_like(crow_ref)
    crow_ref[0:1, :] = toward
    crow_ref[1:2, :] = flow_0
    crow_ref[2:3, :] = flow_e
    crow_ref[3:4, :] = wall_0
    crow_ref[4:5, :] = wall_e
    channels = groups * rows
    for ref, pick_right in ((sa_ref, place_even), (sb_ref, jnp.logical_not(place_even))):
        ref[...] = jnp.zeros_like(ref)
        ref[0:4, 0 : layers * rows] = jnp.where(pick_right, line_ref[4:8, :], line_ref[0:4, :])
        ref[0:1, 0:rows] = ref[0:1, 0:rows] - time_step * jnp.where(
            pick_right, sunk[1:2, 0:rows], sunk[0:1, 0:rows]
        )
        ref[4:6, 0:TILE] = jnp.where(pick_right, line_ref[12:14, 0:TILE], line_ref[8:10, 0:TILE])
        ref[4:5, channels : 2 * channels] = jnp.where(pick_right, extra[1:2], extra[0:1])
        ref[5:6, channels : 2 * channels] = jnp.where(pick_right, extra[4:5], extra[3:4])
        ref[6:7, 0:channels] = jnp.where(pick_right, flow_e, flow_0)
        ref[7:8, 0:channels] = jnp.where(pick_right, part_e, part_0)


def coolant_kernel(fw_ref, temp_ref, after_ref, crow_ref, map_ref, first_ref, second_ref):
    rows, cols = first_ref.shape
    channels = crow_ref.shape[1]
    chooser = one_hot(map_ref[...], lax.axis_index("grp") * rows, rows)
    toward = pick(chooser, jnp.broadcast_to(crow_ref[0:1, :], (TILE, channels)), ((1,), (1,)))
    toward = jnp.concatenate([toward] * (cols // TILE), 1) > 0.5
    lane = lax.broadcasted_iota(jnp.int32, (rows, cols), 1)

    def advance(flow, temp):
        before = jnp.where(lane == 0, 0.0, pltpu.roll(flow, 1, 1))
        after = jnp.where(lane == cols - 1, 0.0, pltpu.roll(flow, cols - 1, 1))
        flux = fw_ref[rows:, :] * (temp - flow)
        return flow - courant * (flow - jnp.where(toward, before, after)) + heat_gain * flux

    first = advance(fw_ref[0:rows, :], temp_ref[0])
    first_ref[...] = first
    second_ref[...] = advance(first, after_ref[0])


def close_kernel(
    temp_ref, kappa_ref, slope_ref, power_ref, yo_ref, ra_ref, rb_ref, sa_ref, sb_ref,
    flow_ref, fw_ref, crow_ref, map_ref, link_ref,
    out_hbm, tail_ref, add_ref, wide_ref, xt_ref, xc_ref, xf_ref, full_ref, out_ref, turn_ref, out_sem,
):
    layers, rows, cols = temp_ref.shape
    group, groups = lax.axis_index("grp"), lax.axis_size("grp")
    place, places = lax.axis_index("loop"), lax.axis_size("loop")
    even = lax.rem(place, 2) == 0
    channels = crow_ref.shape[1]
    low_open = jnp.where(group == 0, 0.0, 1.0)
    high_open = jnp.where(group == groups - 1, 0.0, 1.0)
    got_a, got_b, own_a, own_b = (ref[0:8, 0 : layers * rows] for ref in (ra_ref, rb_ref, sa_ref, sb_ref))
    got = (jnp.where(even, got_b, got_a), jnp.where(even, got_a, got_b))
    own = (jnp.where(even, own_b, own_a), jnp.where(even, own_a, own_b))

    def turn(first, last, ref):
        wide_ref[0:1, 0 : first.shape[1]] = first
        wide_ref[TILE - 1 : TILE, 0 : last.shape[1]] = last
        ref[...] = wide_ref[:, 0 : ref.shape[0]].T

    wide_ref[...] = jnp.zeros_like(wide_ref)
    temps, conds, fluxes = [], [], []
    for side in range(2):
        temp_n, temp_o = got[side][1:2], own[side][1:2]
        cond_n = conduct(got[side][2:3], got[side][3:4], temp_n)
        cond_o = conduct(own[side][2:3], own[side][3:4], temp_o)
        flux = face(cond_o, cond_n, temp_o, temp_n)
        after = got[side][0:1] - flux
        temps.append(after)
        conds.append(conduct(got[side][2:3], got[side][3:4], after))
        fluxes.append(flux)
    turn(temps[0], temps[1], xt_ref)
    turn(conds[0], conds[1], xc_ref)
    turn(fluxes[0], fluxes[1], xf_ref)

    wide_ref[0:1, 0:TILE] = got[0][4:5, 0:TILE]
    wide_ref[TILE - 1 : TILE, 0:TILE] = got[1][4:5, 0:TILE]
    corner_t = wide_ref[:, 0:TILE].T
    wide_ref[0:1, 0:TILE] = got[0][5:6, 0:TILE]
    wide_ref[TILE - 1 : TILE, 0:TILE] = got[1][5:6, 0:TILE]
    corner_c = wide_ref[:, 0:TILE].T
    lane_l = lax.broadcasted_iota(jnp.int32, (layers, TILE), 1)
    halo = []
    for side in range(2):
        base = 4 * layers * side
        after = yo_ref[base : base + layers, :]
        before = yo_ref[base + layers : base + 2 * layers, :]
        kappa = yo_ref[base + 2 * layers : base + 3 * layers, :]
        slope = yo_ref[base + 3 * layers : base + 4 * layers, :]
        cond = conduct(kappa, slope, before)
        c_t, c_c = corner_t[16 * side : 16 * side + layers], corner_c[16 * side : 16 * side + layers]
        tiles = []
        for start, at in ((0, 0), (cols - TILE, TILE - 1)):
            flux = face(
                cond[:, start : start + TILE], c_c, before[:, start : start + TILE], c_t
            )
            tiles.append(after[:, start : start + TILE] + jnp.where(lane_l == at, flux, 0.0))
        after = jnp.concatenate([tiles[0], after[:, TILE : cols - TILE], tiles[1]], 1) if (
            cols > 2 * TILE
        ) else jnp.concatenate(tiles, 1)
        halo.append((after, conduct(kappa, slope, after)))

    lane = lax.broadcasted_iota(jnp.int32, (rows, TILE), 1)
    for z in range(layers):
        add = xf_ref[z * rows : (z + 1) * rows, :]
        full_ref[z] = temp_ref[z]
        full_ref[z, :, 0:TILE] = temp_ref[z, :, 0:TILE] + jnp.where(lane == 0, add, 0.0)
        full_ref[z, :, cols - TILE :] = temp_ref[z, :, cols - TILE :] + jnp.where(
            lane == TILE - 1, add, 0.0
        )

    toward_c = crow_ref[0:1, :]
    first_place = place == 0
    last_place = place == places - 1
    link = one_hot(link_ref[...], 0, channels)
    stack = jnp.concatenate(
        [got[0][6:7, 0:channels], got[1][6:7, 0:channels], crow_ref[1:3, :], crow_ref[4:8, :]], 0
    )
    moved = pick_rows(stack, link)
    own_0 = jnp.where(first_place, moved[2:3], stack[2:3])
    own_e = jnp.where(last_place, moved[3:4], stack[3:4])
    late_l = got[0][7:8, 0:channels] + courant * (1.0 - toward_c) * own_0
    late_r = got[1][7:8, 0:channels] + courant * toward_c * own_e
    late = jnp.concatenate([late_l, late_r, crow_ref[2:8, :]], 0)
    late_moved = pick_rows(late, link)
    edge_rows = (
        (jnp.where(first_place, moved[0:1], stack[0:1]), jnp.where(last_place, moved[1:2], stack[1:2])),
        (jnp.where(first_place, late_moved[0:1], late_l), jnp.where(last_place, late_moved[1:2], late_r)),
    )
    shift_0 = courant * toward_c * edge_rows[0][0]
    shift_e = courant * (1.0 - toward_c) * edge_rows[0][1]
    tops = [
        face(
            own[side][5:6, channels : 2 * channels], got[side][5:6, channels : 2 * channels],
            own[side][4:5, channels : 2 * channels], got[side][4:5, channels : 2 * channels],
        )
        for side in range(2)
    ]
    every = one_hot(map_ref[...], 0, channels)
    tops = pick_rows(jnp.concatenate(tops + [crow_ref[2:8, :]], 0), every)
    wall_0, wall_e = crow_ref[3:4, :], crow_ref[4:5, :]
    add_0 = (
        courant * toward_c * edge_rows[1][0]
        + ((1.0 - courant) - heat_gain * wall_0) * shift_0
        + heat_gain * wall_0 * tops[0:1]
    )
    add_e = (
        courant * (1.0 - toward_c) * edge_rows[1][1]
        + ((1.0 - courant) - heat_gain * wall_e) * shift_e
        + heat_gain * wall_e * tops[1:2]
    )
    wide_row = lax.broadcasted_iota(jnp.int32, (TILE, channels), 0)
    chooser = one_hot(map_ref[...], group * rows, rows)
    edge_y = pick(chooser, jnp.where(wide_row == 0, shift_0, shift_e), ((1,), (1,)))
    adds = jnp.where(wide_row == 0, add_0, jnp.where(wide_row == 1, courant * toward_c * shift_0, add_e))
    adds = jnp.where(wide_row == TILE - 2, courant * (1.0 - toward_c) * shift_e, adds)
    turn_ref[0:channels, :] = adds.T
    turn_ref[channels:, :] = jnp.broadcast_to(map_ref[...].astype(F32), (TILE, channels)).T
    add_ref[0:rows, :] = turn_ref[pl.ds(pl.multiple_of(group * rows, 8), rows), :]
    add_ref[rows:, :] = turn_ref[pl.ds(pl.multiple_of(channels + group * rows, 8), rows), :]
    pad = [jnp.zeros((rows, cols - 2 * TILE), F32)] if cols > 2 * TILE else []
    flow = flow_ref[...] + jnp.concatenate(
        [jnp.where(lane == 0, edge_y, 0.0)] + pad + [jnp.where(lane == TILE - 1, edge_y, 0.0)], 1
    )
    flux = fw_ref[rows:, :] * (full_ref[0] - flow)

    row8 = lax.broadcasted_iota(jnp.int32, (8, cols), 0)

    def emit(z, temp, cond, heat):
        result = temp + heat + time_step * power_ref[z]
        if z == 0:
            result = result - time_step * flux
        halo_t = xt_ref[z * rows : (z + 1) * rows, :]
        halo_c = xc_ref[z * rows : (z + 1) * rows, :]
        sides = []
        for start, at in ((0, 0), (cols - TILE, TILE - 1)):
            part = slice(start, start + TILE)
            extra = face(cond[:, part], halo_c, temp[:, part], halo_t)
            sides.append(jnp.where(lane == at, extra, 0.0))
        middle = [jnp.zeros((rows, cols - 2 * TILE), F32)] if cols > 2 * TILE else []
        result = result + jnp.concatenate([sides[0]] + middle + [sides[1]], 1)
        early = layers - tail_ref.shape[0]
        target, at_z = (out_ref, z) if z < early else (tail_ref, z - early)
        target[at_z] = result
        for side, opened, start, at in ((0, low_open, 0, 0), (1, high_open, rows - 8, 7)):
            part = slice(start, start + 8)
            extra = opened * face(
                cond[part], halo[side][1][z : z + 1], temp[part], halo[side][0][z : z + 1]
            )
            target[at_z, part, :] = result[part] + jnp.where(row8 == at, extra, 0.0)
        if z < early:
            copies.append(pltpu.make_async_copy(out_ref.at[z], out_hbm.at[z], out_sem.at[z]))
            copies[-1].start()

    copies = []
    closed_heat(full_ref, kappa_ref, slope_ref, emit)
    for copy in copies:
        copy.wait()


def return_kernel(
    part_hbm, tail_ref, own_ref, core_ref, cross_ref, relay_ref, add_ref,
    out_hbm, flow_hbm, all_ref, out_ref, sem,
):
    rows, cols = out_ref.shape
    layers, late = out_hbm.shape[0], tail_ref.shape[0]
    tail = pltpu.make_async_copy(tail_ref, out_hbm.at[layers - late : layers], sem.at[0])
    tail.start()
    group, groups = lax.axis_index("grp"), lax.axis_size("grp")
    beside = group + 1 - 2 * lax.rem(group, 2)
    for ref, owner in (
        (own_ref, group), (core_ref, beside), (cross_ref, groups - 1 - group), (relay_ref, groups - 1 - beside),
    ):
        all_ref[pl.ds(pl.multiple_of(owner * rows, 8), rows), :] = ref[...]
    lane = lax.broadcasted_iota(jnp.int32, (rows, TILE), 1)
    adds, row = add_ref[0:rows, :], add_ref[rows:, :]
    channels = groups * rows
    chooser = jnp.concatenate(
        [jnp.where(row == (lane + start).astype(F32), 1.0, 0.0) for start in range(0, channels, TILE)], 1
    ).astype(BF16)
    flow = pick(chooser, all_ref[...], ((1,), (0,)))
    pad = [jnp.zeros((rows, cols - 2 * TILE), F32)] if cols > 2 * TILE else []
    out_ref[...] = flow + jnp.concatenate(
        [jnp.where(lane < 2, adds, 0.0)] + pad + [jnp.where(lane >= TILE - 2, adds, 0.0)], 1
    )
    back = pltpu.make_async_copy(out_ref, flow_hbm, sem.at[1])
    back.start()
    tail.wait()
    back.wait()


def pairs(count, first, closed):
    swaps = []
    for low in range(first, count, 2):
        high = low + 1
        if high == count:
            if not closed:
                continue
            high = 0
        swaps += [(low, high), (high, low)]
    return swaps


def shards(
    solid_temp, kappa, slope, power, coolant_temp, wall_coeff, channel_map, flow_dir, loop_link
):
    groups, places = lax.axis_size("grp"), lax.axis_size("loop")
    layers, rows, cols = solid_temp.shape
    channels = groups * rows
    strip = layers * rows
    params = pltpu.CompilerParams(vmem_limit_bytes=48 * 1024 * 1024)

    def shape(*dims):
        return jax.ShapeDtypeStruct(dims, F32)

    def call(body, outs, scratch, *args, far=0, outs_far=0, cost=None, alias={}):
        return pl.pallas_call(
            body,
            out_shape=outs,
            in_specs=[pl.BlockSpec(memory_space=pltpu.HBM)] * far + [pl.BlockSpec(memory_space=pltpu.VMEM)] * (len(args) - far),
            out_specs=[pl.BlockSpec(memory_space=pltpu.HBM)] * outs_far
            + [pl.BlockSpec(memory_space=pltpu.VMEM)] * (len(outs) - outs_far),
            scratch_shapes=scratch,
            compiler_params=params,
            cost_estimate=cost,
            input_output_aliases=alias,
        )(*[pltpu.with_memory_space_constraint(arg, pltpu.HBM) for arg in args[:far]], *args[far:])

    def vmem(*dims):
        return pltpu.VMEM(dims, F32)

    heavy = pl.CostEstimate(
        flops=30 * layers * rows * cols, bytes_accessed=36 * layers * rows * cols, transcendentals=0
    )
    block = shape(layers, rows, cols)
    share = shape(2 * rows + 8, cols)
    wide = shape(2 * rows + 8 + 4 * layers, cols)
    index = jax.ShapeDtypeStruct((1, channels), jnp.int32)
    core, cross, step, map_row, link_row = call(
        pack_kernel,
        (wide, share, shape(4 * layers, cols), index, index),
        [
            vmem(layers, 8, cols), vmem(layers, 8, cols), vmem(layers, 8, cols), vmem(layers, 8, cols),
            vmem(3, rows, cols), vmem(TILE, TILE), vmem(8, cols), pltpu.VMEM((1, rows), jnp.int32),
            pltpu.SemaphoreType.DMA((4, 2)), pltpu.SemaphoreType.DMA((3,)), pltpu.SemaphoreType.DMA((2,)),
            pltpu.SemaphoreType.DMA((3,)),
        ],
        solid_temp, kappa, slope, power, coolant_temp, wall_coeff, flow_dir.reshape(1, rows),
        channel_map, loop_link.reshape(1, channels),
        far=9,
    )
    beside = [(i, i + 1 - 2 * (i % 2)) for i in range(groups)]
    across = [(i, groups - 1 - i) for i in range(groups)]
    got_cross = lax.ppermute(cross, "grp", across)
    got_step = lax.ppermute(step, "grp", pairs(groups, 1, False))
    got_core = lax.ppermute(core, "grp", beside)
    first, temp, kappa, slope, power = call(
        open_kernel,
        (block, block, block, block, block),
        [pltpu.SemaphoreType.DMA((4, layers // CHUNK))],
        solid_temp, kappa, slope, power, map_row,
        far=4,
        cost=heavy,
    )
    got_cross, got_step, first = lax.optimization_barrier((got_cross, got_step, first))
    relay = lax.ppermute(got_cross, "grp", beside)
    after, yo, line = call(
        edge_kernel,
        (block, shape(8 * layers, cols), shape(16, strip)),
        [vmem(strip, TILE), vmem(TILE, TILE)],
        first, temp, kappa, slope, got_core, got_step,
        cost=heavy,
    )
    after, yo, sa, sb, fw, crow = call(
        select_kernel,
        (
            block, shape(8 * layers, cols), shape(16, strip + strip // 3), shape(16, strip + strip // 3),
            shape(2 * rows, cols), shape(8, channels),
        ),
        [vmem(channels, 2 * cols), vmem(TILE, TILE)],
        after, yo, line, temp, core, got_core, got_cross, relay, map_row,
        alias={0: 0, 1: 1},
    )
    ra = lax.ppermute(sa, "loop", pairs(places, 0, True))
    rb = lax.ppermute(sb, "loop", pairs(places, 1, True))
    flow1, flow = call(
        coolant_kernel, (shape(rows, cols), shape(rows, cols)), [], fw, temp, after, crow, map_row,
    )
    got_across = lax.ppermute(flow, "grp", across)
    got_over = lax.ppermute(flow, "grp", [(i, (i + groups // 2) % groups) for i in range(groups)])
    got_beside = lax.ppermute(flow, "grp", beside)
    late = layers // 3
    out, tail, adds = call(
        close_kernel,
        (block, shape(late, rows, cols), shape(2 * rows, TILE)),
        [
            vmem(TILE, strip), vmem(strip, TILE), vmem(strip, TILE), vmem(strip, TILE),
            vmem(layers, rows, cols), vmem(layers - late, rows, cols), vmem(2 * channels, TILE),
            pltpu.SemaphoreType.DMA((layers - late,)),
        ],
        after, kappa, slope, power, yo, ra, rb, sa, sb, flow1, fw, crow, map_row, link_row,
        outs_far=1,
        cost=heavy,
    )
    return call(
        return_kernel,
        (block, shape(rows, cols)),
        [vmem(channels, cols), vmem(rows, cols), pltpu.SemaphoreType.DMA((2,))],
        out, tail, flow, got_beside, got_across, got_over, adds,
        far=1,
        outs_far=2,
        alias={0: 0},
    )


def solution(mesh):
    block = P(None, "grp", "loop")
    plane = P("grp", "loop")
    return jax.shard_map(
        shards,
        mesh=mesh,
        in_specs=(block, block, block, block, plane, plane, P("loop", None), P("grp"), P()),
        out_specs=(block, plane),
        check_vma=False,
    )
```

```python
import jax
import jax.numpy as jnp
from jax import lax
from jax.experimental import pallas as pl
from jax.experimental.pallas import tpu as pltpu
from jax.sharding import PartitionSpec as P

time_step = 0.06
courant = 0.5
heat_gain = 0.5
TILE = 128
CHUNK = 4
F32 = jnp.float32
BF16 = jnp.bfloat16


def split3(value):
    high = value.astype(BF16)
    rest = value - high.astype(F32)
    middle = rest.astype(BF16)
    low = (rest - middle.astype(F32)).astype(BF16)
    return high, middle, low


def pick(chooser, value, dims):
    total = None
    for part in split3(value):
        term = lax.dot_general(chooser, part, (dims, ((), ())), preferred_element_type=F32)
        total = term if total is None else total + term
    return total


def pick_rows(value, chooser):
    total = None
    for part in split3(value):
        term = lax.dot_general(part, chooser, (((1,), (0,)), ((), ())), preferred_element_type=F32)
        total = term if total is None else total + term
    return total


def one_hot(index_row, first, count):
    shape = (count, index_row.shape[1])
    here = lax.broadcasted_iota(jnp.int32, shape, 0) + first
    return jnp.where(index_row == here, 1.0, 0.0).astype(BF16)


def conduct(kappa, slope, temp):
    return (0.5 * time_step) * kappa * (1.0 + slope * temp)


def face(cond_a, cond_b, temp_a, temp_b):
    return (cond_a + cond_b) * (temp_b - temp_a)


def closed_heat(temp_ref, kappa_ref, slope_ref, emit, ready=lambda z: None):
    layers, rows, cols = temp_ref.shape
    lane = lax.broadcasted_iota(jnp.int32, (rows, cols), 1)
    row = lax.broadcasted_iota(jnp.int32, (rows, cols), 0)
    ready(0)
    temp = temp_ref[0]
    cond = conduct(kappa_ref[0], slope_ref[0], temp)
    flux_below = None
    for z in range(layers):
        if z + 1 < layers:
            ready(z + 1)
        flux_x = face(cond, pltpu.roll(cond, cols - 1, 1), temp, pltpu.roll(temp, cols - 1, 1))
        flux_x = jnp.where(lane == cols - 1, 0.0, flux_x)
        heat = flux_x - pltpu.roll(flux_x, 1, 1)
        flux_y = face(cond, pltpu.roll(cond, rows - 1, 0), temp, pltpu.roll(temp, rows - 1, 0))
        flux_y = jnp.where(row == rows - 1, 0.0, flux_y)
        heat = heat + flux_y - pltpu.roll(flux_y, 1, 0)
        if flux_below is not None:
            heat = heat - flux_below
        if z + 1 < layers:
            temp_up = temp_ref[z + 1]
            cond_up = conduct(kappa_ref[z + 1], slope_ref[z + 1], temp_up)
            flux_below = face(cond, cond_up, temp, temp_up)
            heat = heat + flux_below
        emit(z, temp, cond, heat)
        if z + 1 < layers:
            temp, cond = temp_up, cond_up


def pack_kernel(
    temp_hbm, kappa_hbm, slope_hbm, power_hbm, flow_hbm, wall_hbm, dir_hbm, map_hbm, link_hbm,
    core_ref, cross_ref, step_ref, map_ref, link_ref,
    temp_ref, kappa_ref, slope_ref, power_ref, top_ref, tmp_ref, row_ref, dir_ref,
    block_sem, top_sem, share_sem, small_sem,
):
    layers, rows, cols = temp_hbm.shape
    share = 2 * rows + 8
    group = lax.axis_index("grp")
    even = lax.rem(group, 2) == 0
    copies = []
    for n, (source, target) in enumerate((
        (temp_hbm, temp_ref), (kappa_hbm, kappa_ref), (slope_hbm, slope_ref), (power_hbm, power_ref),
    )):
        copies.append(pltpu.make_async_copy(source.at[:, 0:2], target.at[:, 0:2], block_sem.at[n, 0]))
        copies.append(
            pltpu.make_async_copy(source.at[:, rows - 2 : rows], target.at[:, 6:8], block_sem.at[n, 1])
        )
    tops = [
        pltpu.make_async_copy(source.at[0], top_ref.at[n], top_sem.at[n])
        for n, source in enumerate((temp_hbm, kappa_hbm, slope_hbm))
    ]
    smalls = [
        pltpu.make_async_copy(source, target, small_sem.at[n])
        for n, (source, target) in enumerate(((dir_hbm, dir_ref), (map_hbm, map_ref), (link_hbm, link_ref)))
    ]
    smalls.append(pltpu.make_async_copy(flow_hbm, cross_ref.at[0:rows], share_sem.at[0]))
    smalls.append(pltpu.make_async_copy(wall_hbm, cross_ref.at[rows : 2 * rows], share_sem.at[1]))
    for copy in copies + tops + smalls:
        copy.start()
    tmp_ref[...] = jnp.zeros_like(tmp_ref)
    row_ref[...] = jnp.zeros_like(row_ref)
    for copy in copies:
        copy.wait()

    def emit(z, temp, cond, heat):
        after = temp + heat + time_step * power_ref[z]
        for q, value in enumerate((after, temp, kappa_ref[z], slope_ref[z])):
            at = q * layers + z
            core_ref[share + at : share + at + 1, :] = jnp.where(even, value[7:8], value[0:1])
            step_ref[at : at + 1, :] = jnp.where(even, value[0:1], value[7:8])

    closed_heat(temp_ref, kappa_ref, slope_ref, emit)
    for copy in tops:
        copy.wait()
    temp = top_ref[0]
    cond = conduct(top_ref[1], top_ref[2], temp)
    lane = lax.broadcasted_iota(jnp.int32, (rows, TILE), 1)
    packed = jnp.where(lane == 0, temp[:, 0:TILE], pltpu.roll(temp[:, cols - TILE :], 2, 1))
    packed = jnp.where(lane == 3, pltpu.roll(cond[:, 0:TILE], 3, 1), packed)
    packed = jnp.where(lane == 4, pltpu.roll(cond[:, cols - TILE :], 5, 1), packed)
    tmp_ref[0:rows, :] = packed
    row_ref[0:8, 0:TILE] = tmp_ref[...].T[0:8, :]
    for copy in smalls:
        copy.wait()
    row_ref[2:3, 0:rows] = dir_ref[...].astype(F32)
    extra = pltpu.roll(row_ref[...], group * rows, 1)
    cross_ref[2 * rows : share, :] = extra
    core_ref[2 * rows : share, :] = extra
    core_ref[0 : 2 * rows, :] = cross_ref[0 : 2 * rows, :]


def open_kernel(
    temp_hbm, kappa_hbm, slope_hbm, power_hbm, after_ref,
    next_ref, temp_ref, kappa_ref, slope_ref, power_ref, block_sem,
):
    layers = temp_ref.shape[0]
    blocks = []
    for z in range(0, layers, CHUNK):
        part = pl.ds(z, CHUNK)
        blocks.append([
            pltpu.make_async_copy(source.at[part], target.at[part], block_sem.at[n, z // CHUNK])
            for n, (source, target) in enumerate((
                (temp_hbm, temp_ref), (kappa_hbm, kappa_ref), (slope_hbm, slope_ref), (power_hbm, power_ref),
            ))
        ])
    for block in blocks:
        for copy in block:
            copy.start()

    def ready(z):
        if z % CHUNK == 0:
            for copy in blocks[z // CHUNK]:
                copy.wait()

    def emit(z, temp, cond, heat):
        next_ref[z] = temp + heat + time_step * power_ref[z]

    closed_heat(temp_ref, kappa_ref, slope_ref, emit, ready)


def edge_kernel(
    first_ref, temp_ref, kappa_ref, slope_ref, core_ref, step_ref,
    next_ref, yo_ref, line_ref, strip_ref, small_ref,
):
    layers, rows, cols = temp_ref.shape
    span = 2 * rows + 8
    group, groups = lax.axis_index("grp"), lax.axis_size("grp")
    even = lax.rem(group, 2) == 0
    ya, yb = core_ref[span : span + 4 * layers, :], step_ref[...]
    low, high = jnp.where(even, yb, ya), jnp.where(even, ya, yb)
    yo_ref[0 : 4 * layers, :] = low
    yo_ref[4 * layers :, :] = high
    low_open = jnp.where(group == 0, 0.0, 1.0)
    high_open = jnp.where(group == groups - 1, 0.0, 1.0)

    row = lax.broadcasted_iota(jnp.int32, (rows, cols), 0)
    lane = lax.broadcasted_iota(jnp.int32, (rows, TILE), 1)
    small_ref[...] = jnp.zeros_like(small_ref)
    lane1 = lax.broadcasted_iota(jnp.int32, (1, TILE), 1)
    for z in range(layers):
        temp, kappa, slope = temp_ref[z], kappa_ref[z], slope_ref[z]
        after = first_ref[z]
        edges = []
        for side, base, at, opened in ((0, 0, 0, low_open), (1, 4 * layers, rows - 1, high_open)):
            temp_h = yo_ref[base + layers + z : base + layers + z + 1, :]
            cond_h = conduct(
                yo_ref[base + 2 * layers + z : base + 2 * layers + z + 1, :],
                yo_ref[base + 3 * layers + z : base + 3 * layers + z + 1, :],
                temp_h,
            )
            temp_e = temp[at : at + 1]
            cond_e = conduct(kappa[at : at + 1], slope[at : at + 1], temp_e)
            flux = opened * face(cond_e, cond_h, temp_e, temp_h)
            halo = yo_ref[base + z : base + z + 1, :] - flux
            yo_ref[base + z : base + z + 1, :] = halo
            edges.append(flux)
            corner = jnp.where(
                lane1 == 0,
                temp_h[:, 0:TILE],
                jnp.where(
                    lane1 == 1,
                    pltpu.roll(cond_h[:, 0:TILE], 1, 1),
                    jnp.where(
                        lane1 == 4,
                        pltpu.roll(temp_h[:, cols - TILE :], 5, 1),
                        pltpu.roll(cond_h[:, cols - TILE :], 6, 1),
                    ),
                ),
            )
            small_ref[16 * side + z : 16 * side + z + 1, :] = corner
        after = after + jnp.where(row == 0, edges[0], jnp.where(row == rows - 1, edges[1], 0.0))
        next_ref[z] = after
        packed = None
        for n, value in enumerate((after, temp, kappa, slope)):
            left = value[:, 0:TILE]
            right = pltpu.roll(value[:, cols - TILE :], n + 5, 1)
            left = pltpu.roll(left, n, 1) if n else left
            packed = left if packed is None else jnp.where(lane == n, left, packed)
            packed = jnp.where(lane == n + 4, right, packed)
        strip_ref[z * rows : (z + 1) * rows, :] = packed
    line_ref[0:8, :] = strip_ref[...].T[0:8, :]
    line_ref[8:16, 0:TILE] = small_ref[...].T[0:8, :]


def select_kernel(
    old_ref, halo_ref, line_ref, temp_ref, own_ref, core_ref, cross_ref, relay_ref, map_ref,
    top_ref, yo_ref, sa_ref, sb_ref, fw_ref, crow_ref, all_ref, tmp_ref,
):
    rows, cols = old_ref.shape[1:]
    layers = temp_ref.shape[0]
    span = 2 * rows + 8
    group, groups = lax.axis_index("grp"), lax.axis_size("grp")
    place_even = lax.rem(lax.axis_index("loop"), 2) == 0
    beside = group + 1 - 2 * lax.rem(group, 2)
    extra = jnp.zeros((8, cols), F32)
    for ref, owner in (
        (own_ref, group), (core_ref, beside), (cross_ref, groups - 1 - group), (relay_ref, groups - 1 - beside),
    ):
        part = pl.ds(pl.multiple_of(owner * rows, 8), rows)
        all_ref[part, 0:cols] = ref[0:rows, :]
        all_ref[part, cols : 2 * cols] = ref[rows : 2 * rows, :]
        extra = extra + ref[2 * rows : span, :]
    flow_all, wall_all = all_ref[:, 0:cols], all_ref[:, cols : 2 * cols]
    chooser = one_hot(map_ref[...], group * rows - 8, rows + 16)
    both = pick(chooser, all_ref[...], ((1,), (0,)))
    flow_y, wall_y = both[:, :cols], both[:, cols:]
    flow, wall = flow_y[8 : 8 + rows], wall_y[8 : 8 + rows]
    fw_ref[0:rows, :] = flow
    fw_ref[rows:, :] = wall
    sink = wall * (temp_ref[0] - flow)
    for base, at in ((0, 7), (4 * layers, 8 + rows)):
        temp = halo_ref[base + layers : base + layers + 1, :]
        heat = wall_y[at : at + 1] * (temp - flow_y[at : at + 1])
        yo_ref[base : base + 8, :] = halo_ref[base : base + 8, :]
        yo_ref[base : base + 1, :] = halo_ref[base : base + 1, :] - time_step * heat
    top_ref[0] = old_ref[0] - time_step * sink
    lane = lax.broadcasted_iota(jnp.int32, (rows, TILE), 1)
    tmp_ref[...] = jnp.zeros_like(tmp_ref)
    tmp_ref[0:rows, :] = jnp.where(lane == 0, sink[:, 0:TILE], pltpu.roll(sink[:, cols - TILE :], 2, 1))
    sunk = tmp_ref[...].T[0:8, :]
    lane_c = lax.broadcasted_iota(jnp.int32, (groups * rows, TILE), 1)
    right_flow = flow_all[:, cols - TILE :]
    pack = jnp.where(lane_c < 2, flow_all[:, 0:TILE], pltpu.roll(right_flow, 4, 1))
    pack = jnp.where(lane_c == 4, pltpu.roll(wall_all[:, 0:TILE], 4, 1), pack)
    pack = jnp.where(lane_c == 5, pltpu.roll(wall_all[:, cols - TILE :], 6, 1), pack)
    turned = pack.T
    flow_0, flow_1 = turned[0:1], turned[1:2]
    flow_m, flow_e = turned[2:3], turned[3:4]
    wall_0, wall_e = turned[4:5], turned[5:6]
    top = pick_rows(extra, one_hot(map_ref[...], 0, groups * rows))
    toward = extra[2:3]
    flux_0 = wall_0 * (top[0:1] - flow_0)
    flux_e = wall_e * (top[1:2] - flow_e)
    part_0 = (1.0 - courant) * flow_0 + courant * (1.0 - toward) * flow_1 + heat_gain * flux_0
    part_e = (1.0 - courant) * flow_e + courant * toward * flow_m + heat_gain * flux_e
    crow_ref[...] = jnp.zeros_like(crow_ref)
    crow_ref[0:1, :] = toward
    crow_ref[1:2, :] = flow_0
    crow_ref[2:3, :] = flow_e
    crow_ref[3:4, :] = wall_0
    crow_ref[4:5, :] = wall_e
    channels = groups * rows
    for ref, pick_right in ((sa_ref, place_even), (sb_ref, jnp.logical_not(place_even))):
        ref[...] = jnp.zeros_like(ref)
        ref[0:4, 0 : layers * rows] = jnp.where(pick_right, line_ref[4:8, :], line_ref[0:4, :])
        ref[0:1, 0:rows] = ref[0:1, 0:rows] - time_step * jnp.where(
            pick_right, sunk[1:2, 0:rows], sunk[0:1, 0:rows]
        )
        ref[4:6, 0:TILE] = jnp.where(pick_right, line_ref[12:14, 0:TILE], line_ref[8:10, 0:TILE])
        ref[4:5, channels : 2 * channels] = jnp.where(pick_right, extra[1:2], extra[0:1])
        ref[5:6, channels : 2 * channels] = jnp.where(pick_right, extra[4:5], extra[3:4])
        ref[6:7, 0:channels] = jnp.where(pick_right, flow_e, flow_0)
        ref[7:8, 0:channels] = jnp.where(pick_right, part_e, part_0)


def coolant_kernel(fw_ref, temp_ref, after_ref, crow_ref, map_ref, first_ref, second_ref):
    rows, cols = first_ref.shape
    channels = crow_ref.shape[1]
    chooser = one_hot(map_ref[...], lax.axis_index("grp") * rows, rows)
    toward = lax.dot_general(
        chooser, jnp.broadcast_to(crow_ref[0:1, :], (TILE, channels)).astype(BF16), (((1,), (1,)), ((), ())),
        preferred_element_type=F32,
    )
    toward = jnp.concatenate([toward] * (cols // TILE), 1) > 0.5
    lane = lax.broadcasted_iota(jnp.int32, (rows, cols), 1)

    def advance(flow, temp):
        before = jnp.where(lane == 0, 0.0, pltpu.roll(flow, 1, 1))
        after = jnp.where(lane == cols - 1, 0.0, pltpu.roll(flow, cols - 1, 1))
        flux = fw_ref[rows:, :] * (temp - flow)
        return flow - courant * (flow - jnp.where(toward, before, after)) + heat_gain * flux

    first = advance(fw_ref[0:rows, :], temp_ref[0])
    first_ref[...] = first
    second_ref[...] = advance(first, after_ref[0])


def close_kernel(
    temp_ref, kappa_ref, slope_ref, power_ref, yo_ref, ra_ref, rb_ref, sa_ref, sb_ref,
    flow_ref, fw_ref, crow_ref, map_ref, link_ref,
    out_hbm, tail_ref, add_ref, wide_ref, xt_ref, xc_ref, xf_ref, full_ref, out_ref, turn_ref, out_sem,
):
    layers, rows, cols = temp_ref.shape
    group, groups = lax.axis_index("grp"), lax.axis_size("grp")
    place, places = lax.axis_index("loop"), lax.axis_size("loop")
    even = lax.rem(place, 2) == 0
    channels = crow_ref.shape[1]
    low_open = jnp.where(group == 0, 0.0, 1.0)
    high_open = jnp.where(group == groups - 1, 0.0, 1.0)
    got_a, got_b, own_a, own_b = (ref[0:8, 0 : layers * rows] for ref in (ra_ref, rb_ref, sa_ref, sb_ref))
    got = (jnp.where(even, got_b, got_a), jnp.where(even, got_a, got_b))
    own = (jnp.where(even, own_b, own_a), jnp.where(even, own_a, own_b))

    def turn(first, last, ref):
        wide_ref[0:1, 0 : first.shape[1]] = first
        wide_ref[TILE - 1 : TILE, 0 : last.shape[1]] = last
        ref[...] = wide_ref[:, 0 : ref.shape[0]].T

    wide_ref[...] = jnp.zeros_like(wide_ref)
    temps, conds, fluxes = [], [], []
    for side in range(2):
        temp_n, temp_o = got[side][1:2], own[side][1:2]
        cond_n = conduct(got[side][2:3], got[side][3:4], temp_n)
        cond_o = conduct(own[side][2:3], own[side][3:4], temp_o)
        flux = face(cond_o, cond_n, temp_o, temp_n)
        after = got[side][0:1] - flux
        temps.append(after)
        conds.append(conduct(got[side][2:3], got[side][3:4], after))
        fluxes.append(flux)
    turn(temps[0], temps[1], xt_ref)
    turn(conds[0], conds[1], xc_ref)
    turn(fluxes[0], fluxes[1], xf_ref)

    wide_ref[0:1, 0:TILE] = got[0][4:5, 0:TILE]
    wide_ref[TILE - 1 : TILE, 0:TILE] = got[1][4:5, 0:TILE]
    corner_t = wide_ref[:, 0:TILE].T
    wide_ref[0:1, 0:TILE] = got[0][5:6, 0:TILE]
    wide_ref[TILE - 1 : TILE, 0:TILE] = got[1][5:6, 0:TILE]
    corner_c = wide_ref[:, 0:TILE].T
    lane_l = lax.broadcasted_iota(jnp.int32, (layers, TILE), 1)
    halo = []
    for side in range(2):
        base = 4 * layers * side
        after = yo_ref[base : base + layers, :]
        before = yo_ref[base + layers : base + 2 * layers, :]
        kappa = yo_ref[base + 2 * layers : base + 3 * layers, :]
        slope = yo_ref[base + 3 * layers : base + 4 * layers, :]
        cond = conduct(kappa, slope, before)
        c_t, c_c = corner_t[16 * side : 16 * side + layers], corner_c[16 * side : 16 * side + layers]
        tiles = []
        for start, at in ((0, 0), (cols - TILE, TILE - 1)):
            flux = face(
                cond[:, start : start + TILE], c_c, before[:, start : start + TILE], c_t
            )
            tiles.append(after[:, start : start + TILE] + jnp.where(lane_l == at, flux, 0.0))
        after = jnp.concatenate([tiles[0], after[:, TILE : cols - TILE], tiles[1]], 1) if (
            cols > 2 * TILE
        ) else jnp.concatenate(tiles, 1)
        halo.append((after, conduct(kappa, slope, after)))

    lane = lax.broadcasted_iota(jnp.int32, (rows, TILE), 1)
    for z in range(layers):
        add = xf_ref[z * rows : (z + 1) * rows, :]
        full_ref[z] = temp_ref[z]
        full_ref[z, :, 0:TILE] = temp_ref[z, :, 0:TILE] + jnp.where(lane == 0, add, 0.0)
        full_ref[z, :, cols - TILE :] = temp_ref[z, :, cols - TILE :] + jnp.where(
            lane == TILE - 1, add, 0.0
        )

    toward_c = crow_ref[0:1, :]
    first_place = place == 0
    last_place = place == places - 1
    link = one_hot(link_ref[...], 0, channels)
    stack = jnp.concatenate(
        [got[0][6:7, 0:channels], got[1][6:7, 0:channels], crow_ref[1:3, :], crow_ref[4:8, :]], 0
    )
    moved = pick_rows(stack, link)
    own_0 = jnp.where(first_place, moved[2:3], stack[2:3])
    own_e = jnp.where(last_place, moved[3:4], stack[3:4])
    late_l = got[0][7:8, 0:channels] + courant * (1.0 - toward_c) * own_0
    late_r = got[1][7:8, 0:channels] + courant * toward_c * own_e
    late = jnp.concatenate([late_l, late_r, crow_ref[2:8, :]], 0)
    late_moved = pick_rows(late, link)
    edge_rows = (
        (jnp.where(first_place, moved[0:1], stack[0:1]), jnp.where(last_place, moved[1:2], stack[1:2])),
        (jnp.where(first_place, late_moved[0:1], late_l), jnp.where(last_place, late_moved[1:2], late_r)),
    )
    shift_0 = courant * toward_c * edge_rows[0][0]
    shift_e = courant * (1.0 - toward_c) * edge_rows[0][1]
    tops = [
        face(
            own[side][5:6, channels : 2 * channels], got[side][5:6, channels : 2 * channels],
            own[side][4:5, channels : 2 * channels], got[side][4:5, channels : 2 * channels],
        )
        for side in range(2)
    ]
    every = one_hot(map_ref[...], 0, channels)
    tops = pick_rows(jnp.concatenate(tops + [crow_ref[2:8, :]], 0), every)
    wall_0, wall_e = crow_ref[3:4, :], crow_ref[4:5, :]
    add_0 = (
        courant * toward_c * edge_rows[1][0]
        + ((1.0 - courant) - heat_gain * wall_0) * shift_0
        + heat_gain * wall_0 * tops[0:1]
    )
    add_e = (
        courant * (1.0 - toward_c) * edge_rows[1][1]
        + ((1.0 - courant) - heat_gain * wall_e) * shift_e
        + heat_gain * wall_e * tops[1:2]
    )
    wide_row = lax.broadcasted_iota(jnp.int32, (TILE, channels), 0)
    chooser = one_hot(map_ref[...], group * rows, rows)
    edge_y = pick(chooser, jnp.where(wide_row == 0, shift_0, shift_e), ((1,), (1,)))
    adds = jnp.where(wide_row == 0, add_0, jnp.where(wide_row == 1, courant * toward_c * shift_0, add_e))
    adds = jnp.where(wide_row == TILE - 2, courant * (1.0 - toward_c) * shift_e, adds)
    turn_ref[0:channels, :] = adds.T
    turn_ref[channels:, :] = jnp.broadcast_to(map_ref[...].astype(F32), (TILE, channels)).T
    add_ref[0:rows, :] = turn_ref[pl.ds(pl.multiple_of(group * rows, 8), rows), :]
    add_ref[rows:, :] = turn_ref[pl.ds(pl.multiple_of(channels + group * rows, 8), rows), :]
    pad = [jnp.zeros((rows, cols - 2 * TILE), F32)] if cols > 2 * TILE else []
    flow = flow_ref[...] + jnp.concatenate(
        [jnp.where(lane == 0, edge_y, 0.0)] + pad + [jnp.where(lane == TILE - 1, edge_y, 0.0)], 1
    )
    flux = fw_ref[rows:, :] * (full_ref[0] - flow)

    row8 = lax.broadcasted_iota(jnp.int32, (8, cols), 0)

    def emit(z, temp, cond, heat):
        result = temp + heat + time_step * power_ref[z]
        if z == 0:
            result = result - time_step * flux
        halo_t = xt_ref[z * rows : (z + 1) * rows, :]
        halo_c = xc_ref[z * rows : (z + 1) * rows, :]
        sides = []
        for start, at in ((0, 0), (cols - TILE, TILE - 1)):
            part = slice(start, start + TILE)
            extra = face(cond[:, part], halo_c, temp[:, part], halo_t)
            sides.append(jnp.where(lane == at, extra, 0.0))
        middle = [jnp.zeros((rows, cols - 2 * TILE), F32)] if cols > 2 * TILE else []
        result = result + jnp.concatenate([sides[0]] + middle + [sides[1]], 1)
        early = layers - tail_ref.shape[0]
        target, at_z = (out_ref, z) if z < early else (tail_ref, z - early)
        target[at_z] = result
        for side, opened, start, at in ((0, low_open, 0, 0), (1, high_open, rows - 8, 7)):
            part = slice(start, start + 8)
            extra = opened * face(
                cond[part], halo[side][1][z : z + 1], temp[part], halo[side][0][z : z + 1]
            )
            target[at_z, part, :] = result[part] + jnp.where(row8 == at, extra, 0.0)
        if z < early:
            copies.append(pltpu.make_async_copy(out_ref.at[z], out_hbm.at[z], out_sem.at[z]))
            copies[-1].start()

    copies = []
    closed_heat(full_ref, kappa_ref, slope_ref, emit)
    for copy in copies:
        copy.wait()


def return_kernel(
    part_hbm, tail_ref, own_ref, core_ref, cross_ref, relay_ref, add_ref,
    out_hbm, flow_hbm, all_ref, out_ref, sem,
):
    rows, cols = out_ref.shape
    layers, late = out_hbm.shape[0], tail_ref.shape[0]
    tail = pltpu.make_async_copy(tail_ref, out_hbm.at[layers - late : layers], sem.at[0])
    tail.start()
    group, groups = lax.axis_index("grp"), lax.axis_size("grp")
    beside = group + 1 - 2 * lax.rem(group, 2)
    for ref, owner in (
        (own_ref, group), (core_ref, beside), (cross_ref, groups - 1 - group), (relay_ref, groups - 1 - beside),
    ):
        all_ref[pl.ds(pl.multiple_of(owner * rows, 8), rows), :] = ref[...]
    lane = lax.broadcasted_iota(jnp.int32, (rows, TILE), 1)
    adds, row = add_ref[0:rows, :], add_ref[rows:, :]
    channels = groups * rows
    chooser = jnp.concatenate(
        [jnp.where(row == (lane + start).astype(F32), 1.0, 0.0) for start in range(0, channels, TILE)], 1
    ).astype(BF16)
    flow = pick(chooser, all_ref[...], ((1,), (0,)))
    pad = [jnp.zeros((rows, cols - 2 * TILE), F32)] if cols > 2 * TILE else []
    out_ref[...] = flow + jnp.concatenate(
        [jnp.where(lane < 2, adds, 0.0)] + pad + [jnp.where(lane >= TILE - 2, adds, 0.0)], 1
    )
    back = pltpu.make_async_copy(out_ref, flow_hbm, sem.at[1])
    back.start()
    tail.wait()
    back.wait()


def pairs(count, first, closed):
    swaps = []
    for low in range(first, count, 2):
        high = low + 1
        if high == count:
            if not closed:
                continue
            high = 0
        swaps += [(low, high), (high, low)]
    return swaps


def shards(
    solid_temp, kappa, slope, power, coolant_temp, wall_coeff, channel_map, flow_dir, loop_link
):
    groups, places = lax.axis_size("grp"), lax.axis_size("loop")
    layers, rows, cols = solid_temp.shape
    channels = groups * rows
    strip = layers * rows
    params = pltpu.CompilerParams(vmem_limit_bytes=48 * 1024 * 1024)

    def shape(*dims):
        return jax.ShapeDtypeStruct(dims, F32)

    def call(body, outs, scratch, *args, far=0, outs_far=0, cost=None, alias={}):
        return pl.pallas_call(
            body,
            out_shape=outs,
            in_specs=[pl.BlockSpec(memory_space=pltpu.HBM)] * far + [pl.BlockSpec(memory_space=pltpu.VMEM)] * (len(args) - far),
            out_specs=[pl.BlockSpec(memory_space=pltpu.HBM)] * outs_far
            + [pl.BlockSpec(memory_space=pltpu.VMEM)] * (len(outs) - outs_far),
            scratch_shapes=scratch,
            compiler_params=params,
            cost_estimate=cost,
            input_output_aliases=alias,
        )(*[pltpu.with_memory_space_constraint(arg, pltpu.HBM) for arg in args[:far]], *args[far:])

    def vmem(*dims):
        return pltpu.VMEM(dims, F32)

    heavy = pl.CostEstimate(
        flops=30 * layers * rows * cols, bytes_accessed=36 * layers * rows * cols, transcendentals=0
    )
    block = shape(layers, rows, cols)
    share = shape(2 * rows + 8, cols)
    wide = shape(2 * rows + 8 + 4 * layers, cols)
    index = jax.ShapeDtypeStruct((1, channels), jnp.int32)
    core, cross, step, map_row, link_row = call(
        pack_kernel,
        (wide, share, shape(4 * layers, cols), index, index),
        [
            vmem(layers, 8, cols), vmem(layers, 8, cols), vmem(layers, 8, cols), vmem(layers, 8, cols),
            vmem(3, rows, cols), vmem(TILE, TILE), vmem(8, cols), pltpu.VMEM((1, rows), jnp.int32),
            pltpu.SemaphoreType.DMA((4, 2)), pltpu.SemaphoreType.DMA((3,)), pltpu.SemaphoreType.DMA((2,)),
            pltpu.SemaphoreType.DMA((3,)),
        ],
        solid_temp, kappa, slope, power, coolant_temp, wall_coeff, flow_dir.reshape(1, rows),
        channel_map, loop_link.reshape(1, channels),
        far=9,
    )
    beside = [(i, i + 1 - 2 * (i % 2)) for i in range(groups)]
    across = [(i, groups - 1 - i) for i in range(groups)]
    got_cross = lax.ppermute(cross, "grp", across)
    got_step = lax.ppermute(step, "grp", pairs(groups, 1, False))
    got_core = lax.ppermute(core, "grp", beside)
    first, temp, kappa, slope, power = call(
        open_kernel,
        (block, block, block, block, block),
        [pltpu.SemaphoreType.DMA((4, layers // CHUNK))],
        solid_temp, kappa, slope, power, map_row,
        far=4,
        cost=heavy,
    )
    got_cross, got_step, first = lax.optimization_barrier((got_cross, got_step, first))
    relay = lax.ppermute(got_cross, "grp", beside)
    after, yo, line = call(
        edge_kernel,
        (block, shape(8 * layers, cols), shape(16, strip)),
        [vmem(strip, TILE), vmem(TILE, TILE)],
        first, temp, kappa, slope, got_core, got_step,
        cost=heavy,
    )
    after, yo, sa, sb, fw, crow = call(
        select_kernel,
        (
            block, shape(8 * layers, cols), shape(16, strip + strip // 3), shape(16, strip + strip // 3),
            shape(2 * rows, cols), shape(8, channels),
        ),
        [vmem(channels, 2 * cols), vmem(TILE, TILE)],
        after, yo, line, temp, core, got_core, got_cross, relay, map_row,
        alias={0: 0, 1: 1},
    )
    ra = lax.ppermute(sa, "loop", pairs(places, 0, True))
    rb = lax.ppermute(sb, "loop", pairs(places, 1, True))
    flow1, flow = call(
        coolant_kernel, (shape(rows, cols), shape(rows, cols)), [], fw, temp, after, crow, map_row,
    )
    got_across = lax.ppermute(flow, "grp", across)
    got_over = lax.ppermute(flow, "grp", [(i, (i + groups // 2) % groups) for i in range(groups)])
    got_beside = lax.ppermute(flow, "grp", beside)
    late = layers // 3
    out, tail, adds = call(
        close_kernel,
        (block, shape(late, rows, cols), shape(2 * rows, TILE)),
        [
            vmem(TILE, strip), vmem(strip, TILE), vmem(strip, TILE), vmem(strip, TILE),
            vmem(layers, rows, cols), vmem(layers - late, rows, cols), vmem(2 * channels, TILE),
            pltpu.SemaphoreType.DMA((layers - late,)),
        ],
        after, kappa, slope, power, yo, ra, rb, sa, sb, flow1, fw, crow, map_row, link_row,
        outs_far=1,
        cost=heavy,
    )
    return call(
        return_kernel,
        (block, shape(rows, cols)),
        [vmem(channels, cols), vmem(rows, cols), pltpu.SemaphoreType.DMA((2,))],
        out, tail, flow, got_beside, got_across, got_over, adds,
        far=1,
        outs_far=2,
        alias={0: 0},
    )


def solution(mesh):
    block = P(None, "grp", "loop")
    plane = P("grp", "loop")
    return jax.shard_map(
        shards,
        mesh=mesh,
        in_specs=(block, block, block, block, plane, plane, P("loop", None), P("grp"), P()),
        out_specs=(block, plane),
        check_vma=False,
    )
```

```python
import jax
import jax.numpy as jnp
from jax import lax
from jax.experimental import pallas as pl
from jax.experimental.pallas import tpu as pltpu
from jax.sharding import PartitionSpec as P

time_step = 0.06
courant = 0.5
heat_gain = 0.5
TILE = 128
CHUNK = 4
F32 = jnp.float32
BF16 = jnp.bfloat16


def split3(value):
    high = value.astype(BF16)
    rest = value - high.astype(F32)
    middle = rest.astype(BF16)
    low = (rest - middle.astype(F32)).astype(BF16)
    return high, middle, low


def pick(chooser, value, dims):
    total = None
    for part in split3(value):
        term = lax.dot_general(chooser, part, (dims, ((), ())), preferred_element_type=F32)
        total = term if total is None else total + term
    return total


def pick_rows(value, chooser):
    total = None
    for part in split3(value):
        term = lax.dot_general(part, chooser, (((1,), (0,)), ((), ())), preferred_element_type=F32)
        total = term if total is None else total + term
    return total


def one_hot(index_row, first, count):
    shape = (count, index_row.shape[1])
    here = lax.broadcasted_iota(jnp.int32, shape, 0) + first
    return jnp.where(index_row == here, 1.0, 0.0).astype(BF16)


def conduct(kappa, slope, temp):
    return (0.5 * time_step) * kappa * (1.0 + slope * temp)


def face(cond_a, cond_b, temp_a, temp_b):
    return (cond_a + cond_b) * (temp_b - temp_a)


def closed_heat(temp_ref, kappa_ref, slope_ref, emit, ready=lambda z: None):
    layers, rows, cols = temp_ref.shape
    lane = lax.broadcasted_iota(jnp.int32, (rows, cols), 1)
    row = lax.broadcasted_iota(jnp.int32, (rows, cols), 0)
    ready(0)
    temp = temp_ref[0]
    cond = conduct(kappa_ref[0], slope_ref[0], temp)
    flux_below = None
    for z in range(layers):
        if z + 1 < layers:
            ready(z + 1)
        flux_x = face(cond, pltpu.roll(cond, cols - 1, 1), temp, pltpu.roll(temp, cols - 1, 1))
        flux_x = jnp.where(lane == cols - 1, 0.0, flux_x)
        heat = flux_x - pltpu.roll(flux_x, 1, 1)
        flux_y = face(cond, pltpu.roll(cond, rows - 1, 0), temp, pltpu.roll(temp, rows - 1, 0))
        flux_y = jnp.where(row == rows - 1, 0.0, flux_y)
        heat = heat + flux_y - pltpu.roll(flux_y, 1, 0)
        if flux_below is not None:
            heat = heat - flux_below
        if z + 1 < layers:
            temp_up = temp_ref[z + 1]
            cond_up = conduct(kappa_ref[z + 1], slope_ref[z + 1], temp_up)
            flux_below = face(cond, cond_up, temp, temp_up)
            heat = heat + flux_below
        emit(z, temp, cond, heat)
        if z + 1 < layers:
            temp, cond = temp_up, cond_up


def pack_kernel(
    temp_hbm, kappa_hbm, slope_hbm, power_hbm, flow_hbm, wall_hbm, dir_hbm, map_hbm, link_hbm,
    core_ref, cross_ref, step_ref, map_ref, link_ref,
    temp_ref, kappa_ref, slope_ref, power_ref, top_ref, tmp_ref, row_ref, dir_ref,
    block_sem, top_sem, share_sem, small_sem,
):
    layers, rows, cols = temp_hbm.shape
    share = 2 * rows + 8
    group = lax.axis_index("grp")
    even = lax.rem(group, 2) == 0
    copies = []
    for n, (source, target) in enumerate((
        (temp_hbm, temp_ref), (kappa_hbm, kappa_ref), (slope_hbm, slope_ref), (power_hbm, power_ref),
    )):
        copies.append(pltpu.make_async_copy(source.at[:, 0:2], target.at[:, 0:2], block_sem.at[n, 0]))
        copies.append(
            pltpu.make_async_copy(source.at[:, rows - 2 : rows], target.at[:, 6:8], block_sem.at[n, 1])
        )
    tops = [
        pltpu.make_async_copy(source.at[0], top_ref.at[n], top_sem.at[n])
        for n, source in enumerate((temp_hbm, kappa_hbm, slope_hbm))
    ]
    smalls = [
        pltpu.make_async_copy(source, target, small_sem.at[n])
        for n, (source, target) in enumerate(((dir_hbm, dir_ref), (map_hbm, map_ref), (link_hbm, link_ref)))
    ]
    smalls.append(pltpu.make_async_copy(flow_hbm, cross_ref.at[0:rows], share_sem.at[0]))
    smalls.append(pltpu.make_async_copy(wall_hbm, cross_ref.at[rows : 2 * rows], share_sem.at[1]))
    for copy in copies + tops + smalls:
        copy.start()
    tmp_ref[...] = jnp.zeros_like(tmp_ref)
    row_ref[...] = jnp.zeros_like(row_ref)
    for copy in copies:
        copy.wait()

    def emit(z, temp, cond, heat):
        after = temp + heat + time_step * power_ref[z]
        for q, value in enumerate((after, temp, kappa_ref[z], slope_ref[z])):
            at = q * layers + z
            core_ref[share + at : share + at + 1, :] = jnp.where(even, value[7:8], value[0:1])
            step_ref[at : at + 1, :] = jnp.where(even, value[0:1], value[7:8])

    closed_heat(temp_ref, kappa_ref, slope_ref, emit)
    for copy in tops:
        copy.wait()
    temp = top_ref[0]
    cond = conduct(top_ref[1], top_ref[2], temp)
    lane = lax.broadcasted_iota(jnp.int32, (rows, TILE), 1)
    packed = jnp.where(lane == 0, temp[:, 0:TILE], pltpu.roll(temp[:, cols - TILE :], 2, 1))
    packed = jnp.where(lane == 3, pltpu.roll(cond[:, 0:TILE], 3, 1), packed)
    packed = jnp.where(lane == 4, pltpu.roll(cond[:, cols - TILE :], 5, 1), packed)
    tmp_ref[0:rows, :] = packed
    row_ref[0:8, 0:TILE] = tmp_ref[...].T[0:8, :]
    for copy in smalls:
        copy.wait()
    row_ref[2:3, 0:rows] = dir_ref[...].astype(F32)
    extra = pltpu.roll(row_ref[...], group * rows, 1)
    cross_ref[2 * rows : share, :] = extra
    core_ref[2 * rows : share, :] = extra
    core_ref[0 : 2 * rows, :] = cross_ref[0 : 2 * rows, :]


def open_kernel(
    temp_hbm, kappa_hbm, slope_hbm, power_hbm, after_ref,
    next_ref, temp_ref, kappa_ref, slope_ref, power_ref, block_sem,
):
    layers = temp_ref.shape[0]
    blocks = []
    for z in range(0, layers, CHUNK):
        part = pl.ds(z, CHUNK)
        blocks.append([
            pltpu.make_async_copy(source.at[part], target.at[part], block_sem.at[n, z // CHUNK])
            for n, (source, target) in enumerate((
                (temp_hbm, temp_ref), (kappa_hbm, kappa_ref), (slope_hbm, slope_ref), (power_hbm, power_ref),
            ))
        ])
    for block in blocks:
        for copy in block:
            copy.start()

    def ready(z):
        if z % CHUNK == 0:
            for copy in blocks[z // CHUNK]:
                copy.wait()

    def emit(z, temp, cond, heat):
        next_ref[z] = temp + heat + time_step * power_ref[z]

    closed_heat(temp_ref, kappa_ref, slope_ref, emit, ready)


def edge_kernel(
    first_ref, temp_ref, kappa_ref, slope_ref, core_ref, step_ref,
    next_ref, yo_ref, line_ref, strip_ref, small_ref,
):
    layers, rows, cols = temp_ref.shape
    span = 2 * rows + 8
    group, groups = lax.axis_index("grp"), lax.axis_size("grp")
    even = lax.rem(group, 2) == 0
    ya, yb = core_ref[span : span + 4 * layers, :], step_ref[...]
    low, high = jnp.where(even, yb, ya), jnp.where(even, ya, yb)
    yo_ref[0 : 4 * layers, :] = low
    yo_ref[4 * layers :, :] = high
    low_open = jnp.where(group == 0, 0.0, 1.0)
    high_open = jnp.where(group == groups - 1, 0.0, 1.0)

    row = lax.broadcasted_iota(jnp.int32, (rows, cols), 0)
    lane = lax.broadcasted_iota(jnp.int32, (rows, TILE), 1)
    small_ref[...] = jnp.zeros_like(small_ref)
    lane1 = lax.broadcasted_iota(jnp.int32, (1, TILE), 1)
    for z in range(layers):
        temp, kappa, slope = temp_ref[z], kappa_ref[z], slope_ref[z]
        after = first_ref[z]
        edges = []
        for side, base, at, opened in ((0, 0, 0, low_open), (1, 4 * layers, rows - 1, high_open)):
            temp_h = yo_ref[base + layers + z : base + layers + z + 1, :]
            cond_h = conduct(
                yo_ref[base + 2 * layers + z : base + 2 * layers + z + 1, :],
                yo_ref[base + 3 * layers + z : base + 3 * layers + z + 1, :],
                temp_h,
            )
            temp_e = temp[at : at + 1]
            cond_e = conduct(kappa[at : at + 1], slope[at : at + 1], temp_e)
            flux = opened * face(cond_e, cond_h, temp_e, temp_h)
            halo = yo_ref[base + z : base + z + 1, :] - flux
            yo_ref[base + z : base + z + 1, :] = halo
            edges.append(flux)
            corner = jnp.where(
                lane1 == 0,
                temp_h[:, 0:TILE],
                jnp.where(
                    lane1 == 1,
                    pltpu.roll(cond_h[:, 0:TILE], 1, 1),
                    jnp.where(
                        lane1 == 4,
                        pltpu.roll(temp_h[:, cols - TILE :], 5, 1),
                        pltpu.roll(cond_h[:, cols - TILE :], 6, 1),
                    ),
                ),
            )
            small_ref[16 * side + z : 16 * side + z + 1, :] = corner
        after = after + jnp.where(row == 0, edges[0], jnp.where(row == rows - 1, edges[1], 0.0))
        next_ref[z] = after
        packed = None
        for n, value in enumerate((after, temp, kappa, slope)):
            left = value[:, 0:TILE]
            right = pltpu.roll(value[:, cols - TILE :], n + 5, 1)
            left = pltpu.roll(left, n, 1) if n else left
            packed = left if packed is None else jnp.where(lane == n, left, packed)
            packed = jnp.where(lane == n + 4, right, packed)
        strip_ref[z * rows : (z + 1) * rows, :] = packed
    line_ref[0:8, :] = strip_ref[...].T[0:8, :]
    line_ref[8:16, 0:TILE] = small_ref[...].T[0:8, :]


def select_kernel(
    old_ref, halo_ref, line_ref, temp_ref, own_ref, core_ref, cross_ref, relay_ref, map_ref,
    top_ref, yo_ref, sa_ref, sb_ref, fw_ref, crow_ref, all_ref, tmp_ref,
):
    rows, cols = old_ref.shape[1:]
    layers = temp_ref.shape[0]
    span = 2 * rows + 8
    group, groups = lax.axis_index("grp"), lax.axis_size("grp")
    place_even = lax.rem(lax.axis_index("loop"), 2) == 0
    beside = group + 1 - 2 * lax.rem(group, 2)
    extra = jnp.zeros((8, cols), F32)
    for ref, owner in (
        (own_ref, group), (core_ref, beside), (cross_ref, groups - 1 - group), (relay_ref, groups - 1 - beside),
    ):
        part = pl.ds(pl.multiple_of(owner * rows, 8), rows)
        all_ref[part, 0:cols] = ref[0:rows, :]
        all_ref[part, cols : 2 * cols] = ref[rows : 2 * rows, :]
        extra = extra + ref[2 * rows : span, :]
    flow_all, wall_all = all_ref[:, 0:cols], all_ref[:, cols : 2 * cols]
    chooser = one_hot(map_ref[...], group * rows - 8, rows + 16)
    both = pick(chooser, all_ref[...], ((1,), (0,)))
    flow_y, wall_y = both[:, :cols], both[:, cols:]
    flow, wall = flow_y[8 : 8 + rows], wall_y[8 : 8 + rows]
    fw_ref[0:rows, :] = flow
    fw_ref[rows:, :] = wall
    sink = wall * (temp_ref[0] - flow)
    for base, at in ((0, 7), (4 * layers, 8 + rows)):
        temp = halo_ref[base + layers : base + layers + 1, :]
        heat = wall_y[at : at + 1] * (temp - flow_y[at : at + 1])
        yo_ref[base : base + 8, :] = halo_ref[base : base + 8, :]
        yo_ref[base : base + 1, :] = halo_ref[base : base + 1, :] - time_step * heat
    top_ref[0] = old_ref[0] - time_step * sink
    lane = lax.broadcasted_iota(jnp.int32, (rows, TILE), 1)
    tmp_ref[...] = jnp.zeros_like(tmp_ref)
    tmp_ref[0:rows, :] = jnp.where(lane == 0, sink[:, 0:TILE], pltpu.roll(sink[:, cols - TILE :], 2, 1))
    sunk = tmp_ref[...].T[0:8, :]
    lane_c = lax.broadcasted_iota(jnp.int32, (groups * rows, TILE), 1)
    right_flow = flow_all[:, cols - TILE :]
    pack = jnp.where(lane_c < 2, flow_all[:, 0:TILE], pltpu.roll(right_flow, 4, 1))
    pack = jnp.where(lane_c == 4, pltpu.roll(wall_all[:, 0:TILE], 4, 1), pack)
    pack = jnp.where(lane_c == 5, pltpu.roll(wall_all[:, cols - TILE :], 6, 1), pack)
    turned = pack.T
    flow_0, flow_1 = turned[0:1], turned[1:2]
    flow_m, flow_e = turned[2:3], turned[3:4]
    wall_0, wall_e = turned[4:5], turned[5:6]
    top = pick_rows(extra, one_hot(map_ref[...], 0, groups * rows))
    toward = extra[2:3]
    flux_0 = wall_0 * (top[0:1] - flow_0)
    flux_e = wall_e * (top[1:2] - flow_e)
    part_0 = (1.0 - courant) * flow_0 + courant * (1.0 - toward) * flow_1 + heat_gain * flux_0
    part_e = (1.0 - courant) * flow_e + courant * toward * flow_m + heat_gain * flux_e
    crow_ref[...] = jnp.zeros_like(crow_ref)
    crow_ref[0:1, :] = toward
    crow_ref[1:2, :] = flow_0
    crow_ref[2:3, :] = flow_e
    crow_ref[3:4, :] = wall_0
    crow_ref[4:5, :] = wall_e
    channels = groups * rows
    for ref, pick_right in ((sa_ref, place_even), (sb_ref, jnp.logical_not(place_even))):
        ref[...] = jnp.zeros_like(ref)
        ref[0:4, 0 : layers * rows] = jnp.where(pick_right, line_ref[4:8, :], line_ref[0:4, :])
        ref[0:1, 0:rows] = ref[0:1, 0:rows] - time_step * jnp.where(
            pick_right, sunk[1:2, 0:rows], sunk[0:1, 0:rows]
        )
        ref[4:6, 0:TILE] = jnp.where(pick_right, line_ref[12:14, 0:TILE], line_ref[8:10, 0:TILE])
        ref[4:5, channels : 2 * channels] = jnp.where(pick_right, extra[1:2], extra[0:1])
        ref[5:6, channels : 2 * channels] = jnp.where(pick_right, extra[4:5], extra[3:4])
        ref[6:7, 0:channels] = jnp.where(pick_right, flow_e, flow_0)
        ref[7:8, 0:channels] = jnp.where(pick_right, part_e, part_0)


def coolant_kernel(fw_ref, temp_ref, after_ref, crow_ref, map_ref, first_ref, second_ref):
    rows, cols = first_ref.shape
    channels = crow_ref.shape[1]
    chooser = one_hot(map_ref[...], lax.axis_index("grp") * rows, rows)
    toward = lax.dot_general(
        chooser, jnp.broadcast_to(crow_ref[0:1, :], (TILE, channels)).astype(BF16), (((1,), (1,)), ((), ())),
        preferred_element_type=F32,
    )
    toward = jnp.concatenate([toward] * (cols // TILE), 1) > 0.5
    lane = lax.broadcasted_iota(jnp.int32, (rows, cols), 1)

    def advance(flow, temp):
        before = jnp.where(lane == 0, 0.0, pltpu.roll(flow, 1, 1))
        after = jnp.where(lane == cols - 1, 0.0, pltpu.roll(flow, cols - 1, 1))
        flux = fw_ref[rows:, :] * (temp - flow)
        return flow - courant * (flow - jnp.where(toward, before, after)) + heat_gain * flux

    first = advance(fw_ref[0:rows, :], temp_ref[0])
    first_ref[...] = first
    second_ref[...] = advance(first, after_ref[0])


def close_kernel(
    temp_ref, kappa_ref, slope_ref, power_ref, yo_ref, ra_ref, rb_ref, sa_ref, sb_ref,
    flow_ref, fw_ref, crow_ref, map_ref, link_ref,
    out_hbm, tail_ref, add_ref, wide_ref, xt_ref, xc_ref, xf_ref, full_ref, out_ref, turn_ref, out_sem,
):
    layers, rows, cols = temp_ref.shape
    group, groups = lax.axis_index("grp"), lax.axis_size("grp")
    place, places = lax.axis_index("loop"), lax.axis_size("loop")
    even = lax.rem(place, 2) == 0
    channels = crow_ref.shape[1]
    low_open = jnp.where(group == 0, 0.0, 1.0)
    high_open = jnp.where(group == groups - 1, 0.0, 1.0)
    got_a, got_b, own_a, own_b = (ref[0:8, 0 : layers * rows] for ref in (ra_ref, rb_ref, sa_ref, sb_ref))
    got = (jnp.where(even, got_b, got_a), jnp.where(even, got_a, got_b))
    own = (jnp.where(even, own_b, own_a), jnp.where(even, own_a, own_b))

    def turn(first, last, ref):
        wide_ref[0:1, 0 : first.shape[1]] = first
        wide_ref[TILE - 1 : TILE, 0 : last.shape[1]] = last
        ref[...] = wide_ref[:, 0 : ref.shape[0]].T

    wide_ref[...] = jnp.zeros_like(wide_ref)
    temps, conds, fluxes = [], [], []
    for side in range(2):
        temp_n, temp_o = got[side][1:2], own[side][1:2]
        cond_n = conduct(got[side][2:3], got[side][3:4], temp_n)
        cond_o = conduct(own[side][2:3], own[side][3:4], temp_o)
        flux = face(cond_o, cond_n, temp_o, temp_n)
        after = got[side][0:1] - flux
        temps.append(after)
        conds.append(conduct(got[side][2:3], got[side][3:4], after))
        fluxes.append(flux)
    turn(temps[0], temps[1], xt_ref)
    turn(conds[0], conds[1], xc_ref)
    turn(fluxes[0], fluxes[1], xf_ref)

    wide_ref[0:1, 0:TILE] = got[0][4:5, 0:TILE]
    wide_ref[TILE - 1 : TILE, 0:TILE] = got[1][4:5, 0:TILE]
    corner_t = wide_ref[:, 0:TILE].T
    wide_ref[0:1, 0:TILE] = got[0][5:6, 0:TILE]
    wide_ref[TILE - 1 : TILE, 0:TILE] = got[1][5:6, 0:TILE]
    corner_c = wide_ref[:, 0:TILE].T
    lane_l = lax.broadcasted_iota(jnp.int32, (layers, TILE), 1)
    halo = []
    for side in range(2):
        base = 4 * layers * side
        after = yo_ref[base : base + layers, :]
        before = yo_ref[base + layers : base + 2 * layers, :]
        kappa = yo_ref[base + 2 * layers : base + 3 * layers, :]
        slope = yo_ref[base + 3 * layers : base + 4 * layers, :]
        cond = conduct(kappa, slope, before)
        c_t, c_c = corner_t[16 * side : 16 * side + layers], corner_c[16 * side : 16 * side + layers]
        tiles = []
        for start, at in ((0, 0), (cols - TILE, TILE - 1)):
            flux = face(
                cond[:, start : start + TILE], c_c, before[:, start : start + TILE], c_t
            )
            tiles.append(after[:, start : start + TILE] + jnp.where(lane_l == at, flux, 0.0))
        after = jnp.concatenate([tiles[0], after[:, TILE : cols - TILE], tiles[1]], 1) if (
            cols > 2 * TILE
        ) else jnp.concatenate(tiles, 1)
        halo.append((after, conduct(kappa, slope, after)))

    lane = lax.broadcasted_iota(jnp.int32, (rows, TILE), 1)
    for z in range(layers):
        add = xf_ref[z * rows : (z + 1) * rows, :]
        full_ref[z] = temp_ref[z]
        full_ref[z, :, 0:TILE] = temp_ref[z, :, 0:TILE] + jnp.where(lane == 0, add, 0.0)
        full_ref[z, :, cols - TILE :] = temp_ref[z, :, cols - TILE :] + jnp.where(
            lane == TILE - 1, add, 0.0
        )

    toward_c = crow_ref[0:1, :]
    first_place = place == 0
    last_place = place == places - 1
    link = one_hot(link_ref[...], 0, channels)
    stack = jnp.concatenate(
        [got[0][6:7, 0:channels], got[1][6:7, 0:channels], crow_ref[1:3, :], crow_ref[4:8, :]], 0
    )
    moved = pick_rows(stack, link)
    own_0 = jnp.where(first_place, moved[2:3], stack[2:3])
    own_e = jnp.where(last_place, moved[3:4], stack[3:4])
    late_l = got[0][7:8, 0:channels] + courant * (1.0 - toward_c) * own_0
    late_r = got[1][7:8, 0:channels] + courant * toward_c * own_e
    late = jnp.concatenate([late_l, late_r, crow_ref[2:8, :]], 0)
    late_moved = pick_rows(late, link)
    edge_rows = (
        (jnp.where(first_place, moved[0:1], stack[0:1]), jnp.where(last_place, moved[1:2], stack[1:2])),
        (jnp.where(first_place, late_moved[0:1], late_l), jnp.where(last_place, late_moved[1:2], late_r)),
    )
    shift_0 = courant * toward_c * edge_rows[0][0]
    shift_e = courant * (1.0 - toward_c) * edge_rows[0][1]
    tops = [
        face(
            own[side][5:6, channels : 2 * channels], got[side][5:6, channels : 2 * channels],
            own[side][4:5, channels : 2 * channels], got[side][4:5, channels : 2 * channels],
        )
        for side in range(2)
    ]
    every = one_hot(map_ref[...], 0, channels)
    tops = pick_rows(jnp.concatenate(tops + [crow_ref[2:8, :]], 0), every)
    wall_0, wall_e = crow_ref[3:4, :], crow_ref[4:5, :]
    add_0 = (
        courant * toward_c * edge_rows[1][0]
        + ((1.0 - courant) - heat_gain * wall_0) * shift_0
        + heat_gain * wall_0 * tops[0:1]
    )
    add_e = (
        courant * (1.0 - toward_c) * edge_rows[1][1]
        + ((1.0 - courant) - heat_gain * wall_e) * shift_e
        + heat_gain * wall_e * tops[1:2]
    )
    wide_row = lax.broadcasted_iota(jnp.int32, (TILE, channels), 0)
    chooser = one_hot(map_ref[...], group * rows, rows)
    edge_y = pick(chooser, jnp.where(wide_row == 0, shift_0, shift_e), ((1,), (1,)))
    adds = jnp.where(wide_row == 0, add_0, jnp.where(wide_row == 1, courant * toward_c * shift_0, add_e))
    adds = jnp.where(wide_row == TILE - 2, courant * (1.0 - toward_c) * shift_e, adds)
    turn_ref[0:channels, :] = adds.T
    turn_ref[channels:, :] = jnp.broadcast_to(map_ref[...].astype(F32), (TILE, channels)).T
    add_ref[0:rows, :] = turn_ref[pl.ds(pl.multiple_of(group * rows, 8), rows), :]
    add_ref[rows:, :] = turn_ref[pl.ds(pl.multiple_of(channels + group * rows, 8), rows), :]
    pad = [jnp.zeros((rows, cols - 2 * TILE), F32)] if cols > 2 * TILE else []
    flow = flow_ref[...] + jnp.concatenate(
        [jnp.where(lane == 0, edge_y, 0.0)] + pad + [jnp.where(lane == TILE - 1, edge_y, 0.0)], 1
    )
    flux = fw_ref[rows:, :] * (full_ref[0] - flow)

    row8 = lax.broadcasted_iota(jnp.int32, (8, cols), 0)

    def emit(z, temp, cond, heat):
        result = temp + heat + time_step * power_ref[z]
        if z == 0:
            result = result - time_step * flux
        halo_t = xt_ref[z * rows : (z + 1) * rows, :]
        halo_c = xc_ref[z * rows : (z + 1) * rows, :]
        sides = []
        for start, at in ((0, 0), (cols - TILE, TILE - 1)):
            part = slice(start, start + TILE)
            extra = face(cond[:, part], halo_c, temp[:, part], halo_t)
            sides.append(jnp.where(lane == at, extra, 0.0))
        middle = [jnp.zeros((rows, cols - 2 * TILE), F32)] if cols > 2 * TILE else []
        result = result + jnp.concatenate([sides[0]] + middle + [sides[1]], 1)
        early = layers - tail_ref.shape[0]
        target, at_z = (out_ref, z) if z < early else (tail_ref, z - early)
        target[at_z] = result
        for side, opened, start, at in ((0, low_open, 0, 0), (1, high_open, rows - 8, 7)):
            part = slice(start, start + 8)
            extra = opened * face(
                cond[part], halo[side][1][z : z + 1], temp[part], halo[side][0][z : z + 1]
            )
            target[at_z, part, :] = result[part] + jnp.where(row8 == at, extra, 0.0)
        if z < early:
            copies.append(pltpu.make_async_copy(out_ref.at[z], out_hbm.at[z], out_sem.at[z]))
            copies[-1].start()

    copies = []
    closed_heat(full_ref, kappa_ref, slope_ref, emit)
    for copy in copies:
        copy.wait()


def return_kernel(
    part_hbm, tail_ref, own_ref, cross_ref, core_ref, relay_ref, add_ref,
    out_hbm, flow_hbm, all_ref, out_ref, sem,
):
    rows, cols = out_ref.shape
    layers, late = out_hbm.shape[0], tail_ref.shape[0]
    tail = pltpu.make_async_copy(tail_ref, out_hbm.at[layers - late : layers], sem.at[0])
    tail.start()
    group, groups = lax.axis_index("grp"), lax.axis_size("grp")
    beside = group + 1 - 2 * lax.rem(group, 2)
    for ref, owner in (
        (own_ref, group), (core_ref, beside), (cross_ref, groups - 1 - group), (relay_ref, groups - 1 - beside),
    ):
        all_ref[pl.ds(pl.multiple_of(owner * rows, 8), rows), :] = ref[...]
    lane = lax.broadcasted_iota(jnp.int32, (rows, TILE), 1)
    adds, row = add_ref[0:rows, :], add_ref[rows:, :]
    channels = groups * rows
    chooser = jnp.concatenate(
        [jnp.where(row == (lane + start).astype(F32), 1.0, 0.0) for start in range(0, channels, TILE)], 1
    ).astype(BF16)
    flow = pick(chooser, all_ref[...], ((1,), (0,)))
    pad = [jnp.zeros((rows, cols - 2 * TILE), F32)] if cols > 2 * TILE else []
    out_ref[...] = flow + jnp.concatenate(
        [jnp.where(lane < 2, adds, 0.0)] + pad + [jnp.where(lane >= TILE - 2, adds, 0.0)], 1
    )
    back = pltpu.make_async_copy(out_ref, flow_hbm, sem.at[1])
    back.start()
    tail.wait()
    back.wait()


def pairs(count, first, closed):
    swaps = []
    for low in range(first, count, 2):
        high = low + 1
        if high == count:
            if not closed:
                continue
            high = 0
        swaps += [(low, high), (high, low)]
    return swaps


def shards(
    solid_temp, kappa, slope, power, coolant_temp, wall_coeff, channel_map, flow_dir, loop_link
):
    groups, places = lax.axis_size("grp"), lax.axis_size("loop")
    layers, rows, cols = solid_temp.shape
    channels = groups * rows
    strip = layers * rows
    params = pltpu.CompilerParams(vmem_limit_bytes=48 * 1024 * 1024)

    def shape(*dims):
        return jax.ShapeDtypeStruct(dims, F32)

    def call(body, outs, scratch, *args, far=0, outs_far=0, cost=None, alias={}):
        return pl.pallas_call(
            body,
            out_shape=outs,
            in_specs=[pl.BlockSpec(memory_space=pltpu.HBM)] * far + [pl.BlockSpec(memory_space=pltpu.VMEM)] * (len(args) - far),
            out_specs=[pl.BlockSpec(memory_space=pltpu.HBM)] * outs_far
            + [pl.BlockSpec(memory_space=pltpu.VMEM)] * (len(outs) - outs_far),
            scratch_shapes=scratch,
            compiler_params=params,
            cost_estimate=cost,
            input_output_aliases=alias,
        )(*[pltpu.with_memory_space_constraint(arg, pltpu.HBM) for arg in args[:far]], *args[far:])

    def vmem(*dims):
        return pltpu.VMEM(dims, F32)

    heavy = pl.CostEstimate(
        flops=30 * layers * rows * cols, bytes_accessed=36 * layers * rows * cols, transcendentals=0
    )
    block = shape(layers, rows, cols)
    share = shape(2 * rows + 8, cols)
    wide = shape(2 * rows + 8 + 4 * layers, cols)
    index = jax.ShapeDtypeStruct((1, channels), jnp.int32)
    core, cross, step, map_row, link_row = call(
        pack_kernel,
        (wide, share, shape(4 * layers, cols), index, index),
        [
            vmem(layers, 8, cols), vmem(layers, 8, cols), vmem(layers, 8, cols), vmem(layers, 8, cols),
            vmem(3, rows, cols), vmem(TILE, TILE), vmem(8, cols), pltpu.VMEM((1, rows), jnp.int32),
            pltpu.SemaphoreType.DMA((4, 2)), pltpu.SemaphoreType.DMA((3,)), pltpu.SemaphoreType.DMA((2,)),
            pltpu.SemaphoreType.DMA((3,)),
        ],
        solid_temp, kappa, slope, power, coolant_temp, wall_coeff, flow_dir.reshape(1, rows),
        channel_map, loop_link.reshape(1, channels),
        far=9,
    )
    beside = [(i, i + 1 - 2 * (i % 2)) for i in range(groups)]
    across = [(i, groups - 1 - i) for i in range(groups)]
    got_cross = lax.ppermute(cross, "grp", across)
    got_step = lax.ppermute(step, "grp", pairs(groups, 1, False))
    got_core = lax.ppermute(core, "grp", beside)
    first, temp, kappa, slope, power = call(
        open_kernel,
        (block, block, block, block, block),
        [pltpu.SemaphoreType.DMA((4, layers // CHUNK))],
        solid_temp, kappa, slope, power, map_row,
        far=4,
        cost=heavy,
    )
    got_cross, got_step, first = lax.optimization_barrier((got_cross, got_step, first))
    relay = lax.ppermute(got_cross, "grp", beside)
    after, yo, line = call(
        edge_kernel,
        (block, shape(8 * layers, cols), shape(16, strip)),
        [vmem(strip, TILE), vmem(TILE, TILE)],
        first, temp, kappa, slope, got_core, got_step,
        cost=heavy,
    )
    after, yo, sa, sb, fw, crow = call(
        select_kernel,
        (
            block, shape(8 * layers, cols), shape(16, strip + strip // 3), shape(16, strip + strip // 3),
            shape(2 * rows, cols), shape(8, channels),
        ),
        [vmem(channels, 2 * cols), vmem(TILE, TILE)],
        after, yo, line, temp, core, got_core, got_cross, relay, map_row,
        alias={0: 0, 1: 1},
    )
    ra = lax.ppermute(sa, "loop", pairs(places, 0, True))
    rb = lax.ppermute(sb, "loop", pairs(places, 1, True))
    flow1, flow = call(
        coolant_kernel, (shape(rows, cols), shape(rows, cols)), [], fw, temp, after, crow, map_row,
    )
    got_across = lax.ppermute(flow, "grp", across)
    got_over = lax.ppermute(flow, "grp", [(i, (i + groups // 2) % groups) for i in range(groups)])
    got_beside = lax.ppermute(flow, "grp", beside)
    late = layers // 3
    out, tail, adds = call(
        close_kernel,
        (block, shape(late, rows, cols), shape(2 * rows, TILE)),
        [
            vmem(TILE, strip), vmem(strip, TILE), vmem(strip, TILE), vmem(strip, TILE),
            vmem(layers, rows, cols), vmem(layers - late, rows, cols), vmem(2 * channels, TILE),
            pltpu.SemaphoreType.DMA((layers - late,)),
        ],
        after, kappa, slope, power, yo, ra, rb, sa, sb, flow1, fw, crow, map_row, link_row,
        outs_far=1,
        cost=heavy,
    )
    return call(
        return_kernel,
        (block, shape(rows, cols)),
        [vmem(channels, cols), vmem(rows, cols), pltpu.SemaphoreType.DMA((2,))],
        out, tail, flow, got_across, got_beside, got_over, adds,
        far=1,
        outs_far=2,
        alias={0: 0},
    )


def solution(mesh):
    block = P(None, "grp", "loop")
    plane = P("grp", "loop")
    return jax.shard_map(
        shards,
        mesh=mesh,
        in_specs=(block, block, block, block, plane, plane, P("loop", None), P("grp"), P()),
        out_specs=(block, plane),
        check_vma=False,
    )
```

```python
import jax
import jax.numpy as jnp
from jax import lax
from jax.experimental import pallas as pl
from jax.experimental.pallas import tpu as pltpu
from jax.sharding import PartitionSpec as P

time_step = 0.06
courant = 0.5
heat_gain = 0.5
TILE = 128
CHUNK = 4
F32 = jnp.float32
BF16 = jnp.bfloat16


def split3(value):
    high = value.astype(BF16)
    rest = value - high.astype(F32)
    middle = rest.astype(BF16)
    low = (rest - middle.astype(F32)).astype(BF16)
    return high, middle, low


def pick(chooser, value, dims):
    total = None
    for part in split3(value):
        term = lax.dot_general(chooser, part, (dims, ((), ())), preferred_element_type=F32)
        total = term if total is None else total + term
    return total


def pick_rows(value, chooser):
    total = None
    for part in split3(value):
        term = lax.dot_general(part, chooser, (((1,), (0,)), ((), ())), preferred_element_type=F32)
        total = term if total is None else total + term
    return total


def one_hot(index_row, first, count):
    shape = (count, index_row.shape[1])
    here = lax.broadcasted_iota(jnp.int32, shape, 0) + first
    return jnp.where(index_row == here, 1.0, 0.0).astype(BF16)


def conduct(kappa, slope, temp):
    return (0.5 * time_step) * kappa * (1.0 + slope * temp)


def face(cond_a, cond_b, temp_a, temp_b):
    return (cond_a + cond_b) * (temp_b - temp_a)


def closed_heat(temp_ref, kappa_ref, slope_ref, emit, ready=lambda z: None):
    layers, rows, cols = temp_ref.shape
    lane = lax.broadcasted_iota(jnp.int32, (rows, cols), 1)
    row = lax.broadcasted_iota(jnp.int32, (rows, cols), 0)
    ready(0)
    temp = temp_ref[0]
    cond = conduct(kappa_ref[0], slope_ref[0], temp)
    flux_below = None
    for z in range(layers):
        if z + 1 < layers:
            ready(z + 1)
        flux_x = face(cond, pltpu.roll(cond, cols - 1, 1), temp, pltpu.roll(temp, cols - 1, 1))
        flux_x = jnp.where(lane == cols - 1, 0.0, flux_x)
        heat = flux_x - pltpu.roll(flux_x, 1, 1)
        flux_y = face(cond, pltpu.roll(cond, rows - 1, 0), temp, pltpu.roll(temp, rows - 1, 0))
        flux_y = jnp.where(row == rows - 1, 0.0, flux_y)
        heat = heat + flux_y - pltpu.roll(flux_y, 1, 0)
        if flux_below is not None:
            heat = heat - flux_below
        if z + 1 < layers:
            temp_up = temp_ref[z + 1]
            cond_up = conduct(kappa_ref[z + 1], slope_ref[z + 1], temp_up)
            flux_below = face(cond, cond_up, temp, temp_up)
            heat = heat + flux_below
        emit(z, temp, cond, heat)
        if z + 1 < layers:
            temp, cond = temp_up, cond_up


def pack_kernel(
    temp_hbm, kappa_hbm, slope_hbm, power_hbm, flow_hbm, wall_hbm, dir_hbm, map_hbm, link_hbm,
    core_ref, cross_ref, step_ref, map_ref, link_ref,
    temp_ref, kappa_ref, slope_ref, power_ref, top_ref, tmp_ref, row_ref, dir_ref,
    block_sem, top_sem, share_sem, small_sem,
):
    layers, rows, cols = temp_hbm.shape
    share = 2 * rows + 8
    group = lax.axis_index("grp")
    even = lax.rem(group, 2) == 0
    copies = []
    for n, (source, target) in enumerate((
        (temp_hbm, temp_ref), (kappa_hbm, kappa_ref), (slope_hbm, slope_ref), (power_hbm, power_ref),
    )):
        copies.append(pltpu.make_async_copy(source.at[:, 0:2], target.at[:, 0:2], block_sem.at[n, 0]))
        copies.append(
            pltpu.make_async_copy(source.at[:, rows - 2 : rows], target.at[:, 6:8], block_sem.at[n, 1])
        )
    tops = [
        pltpu.make_async_copy(source.at[0], top_ref.at[n], top_sem.at[n])
        for n, source in enumerate((temp_hbm, kappa_hbm, slope_hbm))
    ]
    smalls = [
        pltpu.make_async_copy(source, target, small_sem.at[n])
        for n, (source, target) in enumerate(((dir_hbm, dir_ref), (map_hbm, map_ref), (link_hbm, link_ref)))
    ]
    smalls.append(pltpu.make_async_copy(flow_hbm, cross_ref.at[0:rows], share_sem.at[0]))
    smalls.append(pltpu.make_async_copy(wall_hbm, cross_ref.at[rows : 2 * rows], share_sem.at[1]))
    for copy in copies + tops + smalls:
        copy.start()
    tmp_ref[...] = jnp.zeros_like(tmp_ref)
    row_ref[...] = jnp.zeros_like(row_ref)
    for copy in copies:
        copy.wait()

    def emit(z, temp, cond, heat):
        after = temp + heat + time_step * power_ref[z]
        for q, value in enumerate((after, temp, kappa_ref[z], slope_ref[z])):
            at = q * layers + z
            core_ref[share + at : share + at + 1, :] = jnp.where(even, value[7:8], value[0:1])
            step_ref[at : at + 1, :] = jnp.where(even, value[0:1], value[7:8])

    closed_heat(temp_ref, kappa_ref, slope_ref, emit)
    for copy in tops:
        copy.wait()
    temp = top_ref[0]
    cond = conduct(top_ref[1], top_ref[2], temp)
    lane = lax.broadcasted_iota(jnp.int32, (rows, TILE), 1)
    packed = jnp.where(lane == 0, temp[:, 0:TILE], pltpu.roll(temp[:, cols - TILE :], 2, 1))
    packed = jnp.where(lane == 3, pltpu.roll(cond[:, 0:TILE], 3, 1), packed)
    packed = jnp.where(lane == 4, pltpu.roll(cond[:, cols - TILE :], 5, 1), packed)
    tmp_ref[0:rows, :] = packed
    row_ref[0:8, 0:TILE] = tmp_ref[...].T[0:8, :]
    for copy in smalls:
        copy.wait()
    row_ref[2:3, 0:rows] = dir_ref[...].astype(F32)
    extra = pltpu.roll(row_ref[...], group * rows, 1)
    cross_ref[2 * rows : share, :] = extra
    core_ref[2 * rows : share, :] = extra
    core_ref[0 : 2 * rows, :] = cross_ref[0 : 2 * rows, :]


def open_kernel(
    temp_hbm, kappa_hbm, slope_hbm, power_hbm, after_ref,
    next_ref, temp_ref, kappa_ref, slope_ref, power_ref, block_sem,
):
    layers = temp_ref.shape[0]
    blocks = []
    for z in range(0, layers, CHUNK):
        part = pl.ds(z, CHUNK)
        blocks.append([
            pltpu.make_async_copy(source.at[part], target.at[part], block_sem.at[n, z // CHUNK])
            for n, (source, target) in enumerate((
                (temp_hbm, temp_ref), (kappa_hbm, kappa_ref), (slope_hbm, slope_ref), (power_hbm, power_ref),
            ))
        ])
    for block in blocks:
        for copy in block:
            copy.start()

    def ready(z):
        if z % CHUNK == 0:
            for copy in blocks[z // CHUNK]:
                copy.wait()

    def emit(z, temp, cond, heat):
        next_ref[z] = temp + heat + time_step * power_ref[z]

    closed_heat(temp_ref, kappa_ref, slope_ref, emit, ready)


def edge_kernel(
    first_ref, temp_ref, kappa_ref, slope_ref, core_ref, step_ref,
    next_ref, yo_ref, line_ref, strip_ref, small_ref,
):
    layers, rows, cols = temp_ref.shape
    span = 2 * rows + 8
    group, groups = lax.axis_index("grp"), lax.axis_size("grp")
    even = lax.rem(group, 2) == 0
    ya, yb = core_ref[span : span + 4 * layers, :], step_ref[...]
    low, high = jnp.where(even, yb, ya), jnp.where(even, ya, yb)
    yo_ref[0 : 4 * layers, :] = low
    yo_ref[4 * layers :, :] = high
    low_open = jnp.where(group == 0, 0.0, 1.0)
    high_open = jnp.where(group == groups - 1, 0.0, 1.0)

    row = lax.broadcasted_iota(jnp.int32, (rows, cols), 0)
    lane = lax.broadcasted_iota(jnp.int32, (rows, TILE), 1)
    small_ref[...] = jnp.zeros_like(small_ref)
    lane1 = lax.broadcasted_iota(jnp.int32, (1, TILE), 1)
    for z in range(layers):
        temp, kappa, slope = temp_ref[z], kappa_ref[z], slope_ref[z]
        after = first_ref[z]
        edges = []
        for side, base, at, opened in ((0, 0, 0, low_open), (1, 4 * layers, rows - 1, high_open)):
            temp_h = yo_ref[base + layers + z : base + layers + z + 1, :]
            cond_h = conduct(
                yo_ref[base + 2 * layers + z : base + 2 * layers + z + 1, :],
                yo_ref[base + 3 * layers + z : base + 3 * layers + z + 1, :],
                temp_h,
            )
            temp_e = temp[at : at + 1]
            cond_e = conduct(kappa[at : at + 1], slope[at : at + 1], temp_e)
            flux = opened * face(cond_e, cond_h, temp_e, temp_h)
            halo = yo_ref[base + z : base + z + 1, :] - flux
            yo_ref[base + z : base + z + 1, :] = halo
            edges.append(flux)
            corner = jnp.where(
                lane1 == 0,
                temp_h[:, 0:TILE],
                jnp.where(
                    lane1 == 1,
                    pltpu.roll(cond_h[:, 0:TILE], 1, 1),
                    jnp.where(
                        lane1 == 4,
                        pltpu.roll(temp_h[:, cols - TILE :], 5, 1),
                        pltpu.roll(cond_h[:, cols - TILE :], 6, 1),
                    ),
                ),
            )
            small_ref[16 * side + z : 16 * side + z + 1, :] = corner
        after = after + jnp.where(row == 0, edges[0], jnp.where(row == rows - 1, edges[1], 0.0))
        next_ref[z] = after
        packed = None
        for n, value in enumerate((after, temp, kappa, slope)):
            left = value[:, 0:TILE]
            right = pltpu.roll(value[:, cols - TILE :], n + 5, 1)
            left = pltpu.roll(left, n, 1) if n else left
            packed = left if packed is None else jnp.where(lane == n, left, packed)
            packed = jnp.where(lane == n + 4, right, packed)
        strip_ref[z * rows : (z + 1) * rows, :] = packed
    line_ref[0:8, :] = strip_ref[...].T[0:8, :]
    line_ref[8:16, 0:TILE] = small_ref[...].T[0:8, :]


def select_kernel(
    old_ref, halo_ref, line_ref, temp_ref, own_ref, core_ref, cross_ref, relay_ref, map_ref,
    top_ref, yo_ref, sa_ref, sb_ref, fw_ref, crow_ref, all_ref, tmp_ref,
):
    rows, cols = old_ref.shape[1:]
    layers = temp_ref.shape[0]
    span = 2 * rows + 8
    group, groups = lax.axis_index("grp"), lax.axis_size("grp")
    place_even = lax.rem(lax.axis_index("loop"), 2) == 0
    beside = group + 1 - 2 * lax.rem(group, 2)
    extra = jnp.zeros((8, cols), F32)
    for ref, owner in (
        (own_ref, group), (core_ref, beside), (cross_ref, groups - 1 - group), (relay_ref, groups - 1 - beside),
    ):
        part = pl.ds(pl.multiple_of(owner * rows, 8), rows)
        all_ref[part, 0:cols] = ref[0:rows, :]
        all_ref[part, cols : 2 * cols] = ref[rows : 2 * rows, :]
        extra = extra + ref[2 * rows : span, :]
    flow_all, wall_all = all_ref[:, 0:cols], all_ref[:, cols : 2 * cols]
    chooser = one_hot(map_ref[...], group * rows - 8, rows + 16)
    both = pick(chooser, all_ref[...], ((1,), (0,)))
    flow_y, wall_y = both[:, :cols], both[:, cols:]
    flow, wall = flow_y[8 : 8 + rows], wall_y[8 : 8 + rows]
    fw_ref[0:rows, :] = flow
    fw_ref[rows:, :] = wall
    sink = wall * (temp_ref[0] - flow)
    for base, at in ((0, 7), (4 * layers, 8 + rows)):
        temp = halo_ref[base + layers : base + layers + 1, :]
        heat = wall_y[at : at + 1] * (temp - flow_y[at : at + 1])
        yo_ref[base : base + 8, :] = halo_ref[base : base + 8, :]
        yo_ref[base : base + 1, :] = halo_ref[base : base + 1, :] - time_step * heat
    top_ref[0] = old_ref[0] - time_step * sink
    lane = lax.broadcasted_iota(jnp.int32, (rows, TILE), 1)
    tmp_ref[...] = jnp.zeros_like(tmp_ref)
    tmp_ref[0:rows, :] = jnp.where(lane == 0, sink[:, 0:TILE], pltpu.roll(sink[:, cols - TILE :], 2, 1))
    sunk = tmp_ref[...].T[0:8, :]
    lane_c = lax.broadcasted_iota(jnp.int32, (groups * rows, TILE), 1)
    right_flow = flow_all[:, cols - TILE :]
    pack = jnp.where(lane_c < 2, flow_all[:, 0:TILE], pltpu.roll(right_flow, 4, 1))
    pack = jnp.where(lane_c == 4, pltpu.roll(wall_all[:, 0:TILE], 4, 1), pack)
    pack = jnp.where(lane_c == 5, pltpu.roll(wall_all[:, cols - TILE :], 6, 1), pack)
    turned = pack.T
    flow_0, flow_1 = turned[0:1], turned[1:2]
    flow_m, flow_e = turned[2:3], turned[3:4]
    wall_0, wall_e = turned[4:5], turned[5:6]
    top = pick_rows(extra, one_hot(map_ref[...], 0, groups * rows))
    toward = extra[2:3]
    flux_0 = wall_0 * (top[0:1] - flow_0)
    flux_e = wall_e * (top[1:2] - flow_e)
    part_0 = (1.0 - courant) * flow_0 + courant * (1.0 - toward) * flow_1 + heat_gain * flux_0
    part_e = (1.0 - courant) * flow_e + courant * toward * flow_m + heat_gain * flux_e
    crow_ref[...] = jnp.zeros_like(crow_ref)
    crow_ref[0:1, :] = toward
    crow_ref[1:2, :] = flow_0
    crow_ref[2:3, :] = flow_e
    crow_ref[3:4, :] = wall_0
    crow_ref[4:5, :] = wall_e
    channels = groups * rows
    for ref, pick_right in ((sa_ref, place_even), (sb_ref, jnp.logical_not(place_even))):
        ref[...] = jnp.zeros_like(ref)
        ref[0:4, 0 : layers * rows] = jnp.where(pick_right, line_ref[4:8, :], line_ref[0:4, :])
        ref[0:1, 0:rows] = ref[0:1, 0:rows] - time_step * jnp.where(
            pick_right, sunk[1:2, 0:rows], sunk[0:1, 0:rows]
        )
        ref[4:6, 0:TILE] = jnp.where(pick_right, line_ref[12:14, 0:TILE], line_ref[8:10, 0:TILE])
        ref[4:5, channels : 2 * channels] = jnp.where(pick_right, extra[1:2], extra[0:1])
        ref[5:6, channels : 2 * channels] = jnp.where(pick_right, extra[4:5], extra[3:4])
        ref[6:7, 0:channels] = jnp.where(pick_right, flow_e, flow_0)
        ref[7:8, 0:channels] = jnp.where(pick_right, part_e, part_0)


def coolant_kernel(fw_ref, temp_ref, after_ref, crow_ref, map_ref, first_ref, second_ref):
    rows, cols = first_ref.shape
    channels = crow_ref.shape[1]
    chooser = one_hot(map_ref[...], lax.axis_index("grp") * rows, rows)
    toward = lax.dot_general(
        chooser, jnp.broadcast_to(crow_ref[0:1, :], (TILE, channels)).astype(BF16), (((1,), (1,)), ((), ())),
        preferred_element_type=F32,
    )
    toward = jnp.concatenate([toward] * (cols // TILE), 1) > 0.5
    lane = lax.broadcasted_iota(jnp.int32, (rows, cols), 1)

    def advance(flow, temp):
        before = jnp.where(lane == 0, 0.0, pltpu.roll(flow, 1, 1))
        after = jnp.where(lane == cols - 1, 0.0, pltpu.roll(flow, cols - 1, 1))
        flux = fw_ref[rows:, :] * (temp - flow)
        return flow - courant * (flow - jnp.where(toward, before, after)) + heat_gain * flux

    first = advance(fw_ref[0:rows, :], temp_ref[0])
    first_ref[...] = first
    second_ref[...] = advance(first, after_ref[0])


def close_kernel(
    temp_ref, kappa_ref, slope_ref, power_ref, yo_ref, ra_ref, rb_ref, sa_ref, sb_ref,
    flow_ref, fw_ref, crow_ref, map_ref, link_ref,
    out_hbm, tail_ref, add_ref, wide_ref, xt_ref, xc_ref, xf_ref, full_ref, out_ref, turn_ref, out_sem,
):
    layers, rows, cols = temp_ref.shape
    group, groups = lax.axis_index("grp"), lax.axis_size("grp")
    place, places = lax.axis_index("loop"), lax.axis_size("loop")
    even = lax.rem(place, 2) == 0
    channels = crow_ref.shape[1]
    low_open = jnp.where(group == 0, 0.0, 1.0)
    high_open = jnp.where(group == groups - 1, 0.0, 1.0)
    got_a, got_b, own_a, own_b = (ref[0:8, 0 : layers * rows] for ref in (ra_ref, rb_ref, sa_ref, sb_ref))
    got = (jnp.where(even, got_b, got_a), jnp.where(even, got_a, got_b))
    own = (jnp.where(even, own_b, own_a), jnp.where(even, own_a, own_b))

    def turn(first, last, ref):
        wide_ref[0:1, 0 : first.shape[1]] = first
        wide_ref[TILE - 1 : TILE, 0 : last.shape[1]] = last
        ref[...] = wide_ref[:, 0 : ref.shape[0]].T

    wide_ref[...] = jnp.zeros_like(wide_ref)
    temps, conds, fluxes = [], [], []
    for side in range(2):
        temp_n, temp_o = got[side][1:2], own[side][1:2]
        cond_n = conduct(got[side][2:3], got[side][3:4], temp_n)
        cond_o = conduct(own[side][2:3], own[side][3:4], temp_o)
        flux = face(cond_o, cond_n, temp_o, temp_n)
        after = got[side][0:1] - flux
        temps.append(after)
        conds.append(conduct(got[side][2:3], got[side][3:4], after))
        fluxes.append(flux)
    turn(temps[0], temps[1], xt_ref)
    turn(conds[0], conds[1], xc_ref)
    turn(fluxes[0], fluxes[1], xf_ref)

    wide_ref[0:1, 0:TILE] = got[0][4:5, 0:TILE]
    wide_ref[TILE - 1 : TILE, 0:TILE] = got[1][4:5, 0:TILE]
    corner_t = wide_ref[:, 0:TILE].T
    wide_ref[0:1, 0:TILE] = got[0][5:6, 0:TILE]
    wide_ref[TILE - 1 : TILE, 0:TILE] = got[1][5:6, 0:TILE]
    corner_c = wide_ref[:, 0:TILE].T
    lane_l = lax.broadcasted_iota(jnp.int32, (layers, TILE), 1)
    halo = []
    for side in range(2):
        base = 4 * layers * side
        after = yo_ref[base : base + layers, :]
        before = yo_ref[base + layers : base + 2 * layers, :]
        kappa = yo_ref[base + 2 * layers : base + 3 * layers, :]
        slope = yo_ref[base + 3 * layers : base + 4 * layers, :]
        cond = conduct(kappa, slope, before)
        c_t, c_c = corner_t[16 * side : 16 * side + layers], corner_c[16 * side : 16 * side + layers]
        tiles = []
        for start, at in ((0, 0), (cols - TILE, TILE - 1)):
            flux = face(
                cond[:, start : start + TILE], c_c, before[:, start : start + TILE], c_t
            )
            tiles.append(after[:, start : start + TILE] + jnp.where(lane_l == at, flux, 0.0))
        after = jnp.concatenate([tiles[0], after[:, TILE : cols - TILE], tiles[1]], 1) if (
            cols > 2 * TILE
        ) else jnp.concatenate(tiles, 1)
        halo.append((after, conduct(kappa, slope, after)))

    lane = lax.broadcasted_iota(jnp.int32, (rows, TILE), 1)
    for z in range(layers):
        add = xf_ref[z * rows : (z + 1) * rows, :]
        full_ref[z] = temp_ref[z]
        full_ref[z, :, 0:TILE] = temp_ref[z, :, 0:TILE] + jnp.where(lane == 0, add, 0.0)
        full_ref[z, :, cols - TILE :] = temp_ref[z, :, cols - TILE :] + jnp.where(
            lane == TILE - 1, add, 0.0
        )

    toward_c = crow_ref[0:1, :]
    first_place = place == 0
    last_place = place == places - 1
    link = one_hot(link_ref[...], 0, channels)
    stack = jnp.concatenate(
        [got[0][6:7, 0:channels], got[1][6:7, 0:channels], crow_ref[1:3, :], crow_ref[4:8, :]], 0
    )
    moved = pick_rows(stack, link)
    own_0 = jnp.where(first_place, moved[2:3], stack[2:3])
    own_e = jnp.where(last_place, moved[3:4], stack[3:4])
    late_l = got[0][7:8, 0:channels] + courant * (1.0 - toward_c) * own_0
    late_r = got[1][7:8, 0:channels] + courant * toward_c * own_e
    late = jnp.concatenate([late_l, late_r, crow_ref[2:8, :]], 0)
    late_moved = pick_rows(late, link)
    edge_rows = (
        (jnp.where(first_place, moved[0:1], stack[0:1]), jnp.where(last_place, moved[1:2], stack[1:2])),
        (jnp.where(first_place, late_moved[0:1], late_l), jnp.where(last_place, late_moved[1:2], late_r)),
    )
    shift_0 = courant * toward_c * edge_rows[0][0]
    shift_e = courant * (1.0 - toward_c) * edge_rows[0][1]
    tops = [
        face(
            own[side][5:6, channels : 2 * channels], got[side][5:6, channels : 2 * channels],
            own[side][4:5, channels : 2 * channels], got[side][4:5, channels : 2 * channels],
        )
        for side in range(2)
    ]
    every = one_hot(map_ref[...], 0, channels)
    tops = pick_rows(jnp.concatenate(tops + [crow_ref[2:8, :]], 0), every)
    wall_0, wall_e = crow_ref[3:4, :], crow_ref[4:5, :]
    add_0 = (
        courant * toward_c * edge_rows[1][0]
        + ((1.0 - courant) - heat_gain * wall_0) * shift_0
        + heat_gain * wall_0 * tops[0:1]
    )
    add_e = (
        courant * (1.0 - toward_c) * edge_rows[1][1]
        + ((1.0 - courant) - heat_gain * wall_e) * shift_e
        + heat_gain * wall_e * tops[1:2]
    )
    wide_row = lax.broadcasted_iota(jnp.int32, (TILE, channels), 0)
    chooser = one_hot(map_ref[...], group * rows, rows)
    edge_y = pick(chooser, jnp.where(wide_row == 0, shift_0, shift_e), ((1,), (1,)))
    adds = jnp.where(wide_row == 0, add_0, jnp.where(wide_row == 1, courant * toward_c * shift_0, add_e))
    adds = jnp.where(wide_row == TILE - 2, courant * (1.0 - toward_c) * shift_e, adds)
    turn_ref[0:channels, :] = adds.T
    turn_ref[channels:, :] = jnp.broadcast_to(map_ref[...].astype(F32), (TILE, channels)).T
    add_ref[0:rows, :] = turn_ref[pl.ds(pl.multiple_of(group * rows, 8), rows), :]
    add_ref[rows:, :] = turn_ref[pl.ds(pl.multiple_of(channels + group * rows, 8), rows), :]
    pad = [jnp.zeros((rows, cols - 2 * TILE), F32)] if cols > 2 * TILE else []
    flow = flow_ref[...] + jnp.concatenate(
        [jnp.where(lane == 0, edge_y, 0.0)] + pad + [jnp.where(lane == TILE - 1, edge_y, 0.0)], 1
    )
    flux = fw_ref[rows:, :] * (full_ref[0] - flow)

    row8 = lax.broadcasted_iota(jnp.int32, (8, cols), 0)

    def emit(z, temp, cond, heat):
        result = temp + heat + time_step * power_ref[z]
        if z == 0:
            result = result - time_step * flux
        halo_t = xt_ref[z * rows : (z + 1) * rows, :]
        halo_c = xc_ref[z * rows : (z + 1) * rows, :]
        sides = []
        for start, at in ((0, 0), (cols - TILE, TILE - 1)):
            part = slice(start, start + TILE)
            extra = face(cond[:, part], halo_c, temp[:, part], halo_t)
            sides.append(jnp.where(lane == at, extra, 0.0))
        middle = [jnp.zeros((rows, cols - 2 * TILE), F32)] if cols > 2 * TILE else []
        result = result + jnp.concatenate([sides[0]] + middle + [sides[1]], 1)
        early = layers - tail_ref.shape[0]
        target, at_z = (out_ref, z) if z < early else (tail_ref, z - early)
        target[at_z] = result
        for side, opened, start, at in ((0, low_open, 0, 0), (1, high_open, rows - 8, 7)):
            part = slice(start, start + 8)
            extra = opened * face(
                cond[part], halo[side][1][z : z + 1], temp[part], halo[side][0][z : z + 1]
            )
            target[at_z, part, :] = result[part] + jnp.where(row8 == at, extra, 0.0)
        if z < early:
            copies.append(pltpu.make_async_copy(out_ref.at[z], out_hbm.at[z], out_sem.at[z]))
            copies[-1].start()

    copies = []
    closed_heat(full_ref, kappa_ref, slope_ref, emit)
    for copy in copies:
        copy.wait()


def return_kernel(
    part_hbm, tail_ref, own_ref, cross_ref, core_ref, relay_ref, add_ref,
    out_hbm, flow_hbm, all_ref, out_ref, sem,
):
    rows, cols = out_ref.shape
    layers, late = out_hbm.shape[0], tail_ref.shape[0]
    tail = pltpu.make_async_copy(tail_ref, out_hbm.at[layers - late : layers], sem.at[0])
    tail.start()
    group, groups = lax.axis_index("grp"), lax.axis_size("grp")
    beside = group + 1 - 2 * lax.rem(group, 2)
    for ref, owner in (
        (own_ref, group), (core_ref, beside), (cross_ref, groups - 1 - group), (relay_ref, groups - 1 - beside),
    ):
        all_ref[pl.ds(pl.multiple_of(owner * rows, 8), rows), :] = ref[...]
    lane = lax.broadcasted_iota(jnp.int32, (rows, TILE), 1)
    adds, row = add_ref[0:rows, :], add_ref[rows:, :]
    channels = groups * rows
    chooser = jnp.concatenate(
        [jnp.where(row == (lane + start).astype(F32), 1.0, 0.0) for start in range(0, channels, TILE)], 1
    ).astype(BF16)
    flow = pick(chooser, all_ref[...], ((1,), (0,)))
    pad = [jnp.zeros((rows, cols - 2 * TILE), F32)] if cols > 2 * TILE else []
    out_ref[...] = flow + jnp.concatenate(
        [jnp.where(lane < 2, adds, 0.0)] + pad + [jnp.where(lane >= TILE - 2, adds, 0.0)], 1
    )
    back = pltpu.make_async_copy(out_ref, flow_hbm, sem.at[1])
    back.start()
    tail.wait()
    back.wait()


def pairs(count, first, closed):
    swaps = []
    for low in range(first, count, 2):
        high = low + 1
        if high == count:
            if not closed:
                continue
            high = 0
        swaps += [(low, high), (high, low)]
    return swaps


def shards(
    solid_temp, kappa, slope, power, coolant_temp, wall_coeff, channel_map, flow_dir, loop_link
):
    groups, places = lax.axis_size("grp"), lax.axis_size("loop")
    layers, rows, cols = solid_temp.shape
    channels = groups * rows
    strip = layers * rows
    params = pltpu.CompilerParams(vmem_limit_bytes=48 * 1024 * 1024)

    def shape(*dims):
        return jax.ShapeDtypeStruct(dims, F32)

    def call(body, outs, scratch, *args, far=0, outs_far=0, cost=None, alias={}):
        return pl.pallas_call(
            body,
            out_shape=outs,
            in_specs=[pl.BlockSpec(memory_space=pltpu.HBM)] * far + [pl.BlockSpec(memory_space=pltpu.VMEM)] * (len(args) - far),
            out_specs=[pl.BlockSpec(memory_space=pltpu.HBM)] * outs_far
            + [pl.BlockSpec(memory_space=pltpu.VMEM)] * (len(outs) - outs_far),
            scratch_shapes=scratch,
            compiler_params=params,
            cost_estimate=cost,
            input_output_aliases=alias,
        )(*[pltpu.with_memory_space_constraint(arg, pltpu.HBM) for arg in args[:far]], *args[far:])

    def vmem(*dims):
        return pltpu.VMEM(dims, F32)

    heavy = pl.CostEstimate(
        flops=30 * layers * rows * cols, bytes_accessed=36 * layers * rows * cols, transcendentals=0
    )
    block = shape(layers, rows, cols)
    share = shape(2 * rows + 8, cols)
    wide = shape(2 * rows + 8 + 4 * layers, cols)
    index = jax.ShapeDtypeStruct((1, channels), jnp.int32)
    core, cross, step, map_row, link_row = call(
        pack_kernel,
        (wide, share, shape(4 * layers, cols), index, index),
        [
            vmem(layers, 8, cols), vmem(layers, 8, cols), vmem(layers, 8, cols), vmem(layers, 8, cols),
            vmem(3, rows, cols), vmem(TILE, TILE), vmem(8, cols), pltpu.VMEM((1, rows), jnp.int32),
            pltpu.SemaphoreType.DMA((4, 2)), pltpu.SemaphoreType.DMA((3,)), pltpu.SemaphoreType.DMA((2,)),
            pltpu.SemaphoreType.DMA((3,)),
        ],
        solid_temp, kappa, slope, power, coolant_temp, wall_coeff, flow_dir.reshape(1, rows),
        channel_map, loop_link.reshape(1, channels),
        far=9,
    )
    beside = [(i, i + 1 - 2 * (i % 2)) for i in range(groups)]
    across = [(i, groups - 1 - i) for i in range(groups)]
    got_cross = lax.ppermute(cross, "grp", across)
    got_step = lax.ppermute(step, "grp", pairs(groups, 1, False))
    got_core = lax.ppermute(core, "grp", beside)
    first, temp, kappa, slope, power = call(
        open_kernel,
        (block, block, block, block, block),
        [pltpu.SemaphoreType.DMA((4, layers // CHUNK))],
        solid_temp, kappa, slope, power, map_row,
        far=4,
        cost=heavy,
    )
    got_cross, got_step, first = lax.optimization_barrier((got_cross, got_step, first))
    relay = lax.ppermute(got_cross, "grp", beside)
    after, yo, line = call(
        edge_kernel,
        (block, shape(8 * layers, cols), shape(16, strip)),
        [vmem(strip, TILE), vmem(TILE, TILE)],
        first, temp, kappa, slope, got_core, got_step,
        cost=heavy,
    )
    after, yo, sa, sb, fw, crow = call(
        select_kernel,
        (
            block, shape(8 * layers, cols), shape(16, strip + strip // 3), shape(16, strip + strip // 3),
            shape(2 * rows, cols), shape(8, channels),
        ),
        [vmem(channels, 2 * cols), vmem(TILE, TILE)],
        after, yo, line, temp, core, got_core, got_cross, relay, map_row,
        alias={0: 0, 1: 1},
    )
    ra = lax.ppermute(sa, "loop", pairs(places, 0, True))
    rb = lax.ppermute(sb, "loop", pairs(places, 1, True))
    flow1, flow = call(
        coolant_kernel, (shape(rows, cols), shape(rows, cols)), [], fw, temp, after, crow, map_row,
    )
    got_across = lax.ppermute(flow, "grp", across)
    got_over = lax.ppermute(flow, "grp", [(i, (i + groups // 2) % groups) for i in range(groups)])
    got_beside = lax.ppermute(flow, "grp", beside)
    late = layers // 2
    out, tail, adds = call(
        close_kernel,
        (block, shape(late, rows, cols), shape(2 * rows, TILE)),
        [
            vmem(TILE, strip), vmem(strip, TILE), vmem(strip, TILE), vmem(strip, TILE),
            vmem(layers, rows, cols), vmem(layers - late, rows, cols), vmem(2 * channels, TILE),
            pltpu.SemaphoreType.DMA((layers - late,)),
        ],
        after, kappa, slope, power, yo, ra, rb, sa, sb, flow1, fw, crow, map_row, link_row,
        outs_far=1,
        cost=heavy,
    )
    return call(
        return_kernel,
        (block, shape(rows, cols)),
        [vmem(channels, cols), vmem(rows, cols), pltpu.SemaphoreType.DMA((2,))],
        out, tail, flow, got_across, got_beside, got_over, adds,
        far=1,
        outs_far=2,
        alias={0: 0},
    )


def solution(mesh):
    block = P(None, "grp", "loop")
    plane = P("grp", "loop")
    return jax.shard_map(
        shards,
        mesh=mesh,
        in_specs=(block, block, block, block, plane, plane, P("loop", None), P("grp"), P()),
        out_specs=(block, plane),
        check_vma=False,
    )
```

```python
import jax
import jax.numpy as jnp
from jax import lax
from jax.experimental import pallas as pl
from jax.experimental.pallas import tpu as pltpu
from jax.sharding import PartitionSpec as P

time_step = 0.06
courant = 0.5
heat_gain = 0.5
TILE = 128
CHUNK = 3
F32 = jnp.float32
BF16 = jnp.bfloat16


def split3(value):
    high = value.astype(BF16)
    rest = value - high.astype(F32)
    middle = rest.astype(BF16)
    low = (rest - middle.astype(F32)).astype(BF16)
    return high, middle, low


def pick(chooser, value, dims):
    total = None
    for part in split3(value):
        term = lax.dot_general(chooser, part, (dims, ((), ())), preferred_element_type=F32)
        total = term if total is None else total + term
    return total


def pick_rows(value, chooser):
    total = None
    for part in split3(value):
        term = lax.dot_general(part, chooser, (((1,), (0,)), ((), ())), preferred_element_type=F32)
        total = term if total is None else total + term
    return total


def one_hot(index_row, first, count):
    shape = (count, index_row.shape[1])
    here = lax.broadcasted_iota(jnp.int32, shape, 0) + first
    return jnp.where(index_row == here, 1.0, 0.0).astype(BF16)


def conduct(kappa, slope, temp):
    return (0.5 * time_step) * kappa * (1.0 + slope * temp)


def face(cond_a, cond_b, temp_a, temp_b):
    return (cond_a + cond_b) * (temp_b - temp_a)


def closed_heat(temp_ref, kappa_ref, slope_ref, emit, ready=lambda z: None):
    layers, rows, cols = temp_ref.shape
    lane = lax.broadcasted_iota(jnp.int32, (rows, cols), 1)
    row = lax.broadcasted_iota(jnp.int32, (rows, cols), 0)
    ready(0)
    temp = temp_ref[0]
    cond = conduct(kappa_ref[0], slope_ref[0], temp)
    flux_below = None
    for z in range(layers):
        if z + 1 < layers:
            ready(z + 1)
        flux_x = face(cond, pltpu.roll(cond, cols - 1, 1), temp, pltpu.roll(temp, cols - 1, 1))
        flux_x = jnp.where(lane == cols - 1, 0.0, flux_x)
        heat = flux_x - pltpu.roll(flux_x, 1, 1)
        flux_y = face(cond, pltpu.roll(cond, rows - 1, 0), temp, pltpu.roll(temp, rows - 1, 0))
        flux_y = jnp.where(row == rows - 1, 0.0, flux_y)
        heat = heat + flux_y - pltpu.roll(flux_y, 1, 0)
        if flux_below is not None:
            heat = heat - flux_below
        if z + 1 < layers:
            temp_up = temp_ref[z + 1]
            cond_up = conduct(kappa_ref[z + 1], slope_ref[z + 1], temp_up)
            flux_below = face(cond, cond_up, temp, temp_up)
            heat = heat + flux_below
        emit(z, temp, cond, heat)
        if z + 1 < layers:
            temp, cond = temp_up, cond_up


def pack_kernel(
    temp_hbm, kappa_hbm, slope_hbm, power_hbm, flow_hbm, wall_hbm, dir_hbm, map_hbm, link_hbm,
    core_ref, cross_ref, step_ref, map_ref, link_ref,
    temp_ref, kappa_ref, slope_ref, power_ref, top_ref, tmp_ref, row_ref, dir_ref,
    block_sem, top_sem, share_sem, small_sem,
):
    layers, rows, cols = temp_hbm.shape
    share = 2 * rows + 8
    group = lax.axis_index("grp")
    even = lax.rem(group, 2) == 0
    copies = []
    for n, (source, target) in enumerate((
        (temp_hbm, temp_ref), (kappa_hbm, kappa_ref), (slope_hbm, slope_ref), (power_hbm, power_ref),
    )):
        copies.append(pltpu.make_async_copy(source.at[:, 0:2], target.at[:, 0:2], block_sem.at[n, 0]))
        copies.append(
            pltpu.make_async_copy(source.at[:, rows - 2 : rows], target.at[:, 6:8], block_sem.at[n, 1])
        )
    tops = [
        pltpu.make_async_copy(source.at[0], top_ref.at[n], top_sem.at[n])
        for n, source in enumerate((temp_hbm, kappa_hbm, slope_hbm))
    ]
    smalls = [
        pltpu.make_async_copy(source, target, small_sem.at[n])
        for n, (source, target) in enumerate(((dir_hbm, dir_ref), (map_hbm, map_ref), (link_hbm, link_ref)))
    ]
    smalls.append(pltpu.make_async_copy(flow_hbm, cross_ref.at[0:rows], share_sem.at[0]))
    smalls.append(pltpu.make_async_copy(wall_hbm, cross_ref.at[rows : 2 * rows], share_sem.at[1]))
    for copy in copies + tops + smalls:
        copy.start()
    tmp_ref[...] = jnp.zeros_like(tmp_ref)
    row_ref[...] = jnp.zeros_like(row_ref)
    for copy in copies:
        copy.wait()

    def emit(z, temp, cond, heat):
        after = temp + heat + time_step * power_ref[z]
        for q, value in enumerate((after, temp, kappa_ref[z], slope_ref[z])):
            at = q * layers + z
            core_ref[share + at : share + at + 1, :] = jnp.where(even, value[7:8], value[0:1])
            step_ref[at : at + 1, :] = jnp.where(even, value[0:1], value[7:8])

    closed_heat(temp_ref, kappa_ref, slope_ref, emit)
    for copy in tops:
        copy.wait()
    temp = top_ref[0]
    cond = conduct(top_ref[1], top_ref[2], temp)
    lane = lax.broadcasted_iota(jnp.int32, (rows, TILE), 1)
    packed = jnp.where(lane == 0, temp[:, 0:TILE], pltpu.roll(temp[:, cols - TILE :], 2, 1))
    packed = jnp.where(lane == 3, pltpu.roll(cond[:, 0:TILE], 3, 1), packed)
    packed = jnp.where(lane == 4, pltpu.roll(cond[:, cols - TILE :], 5, 1), packed)
    tmp_ref[0:rows, :] = packed
    row_ref[0:8, 0:TILE] = tmp_ref[...].T[0:8, :]
    for copy in smalls:
        copy.wait()
    row_ref[2:3, 0:rows] = dir_ref[...].astype(F32)
    extra = pltpu.roll(row_ref[...], group * rows, 1)
    cross_ref[2 * rows : share, :] = extra
    core_ref[2 * rows : share, :] = extra
    core_ref[0 : 2 * rows, :] = cross_ref[0 : 2 * rows, :]


def open_kernel(
    temp_hbm, kappa_hbm, slope_hbm, power_hbm, after_ref,
    next_ref, temp_ref, kappa_ref, slope_ref, power_ref, block_sem,
):
    layers = temp_ref.shape[0]
    blocks = []
    for z in range(0, layers, CHUNK):
        part = pl.ds(z, CHUNK)
        blocks.append([
            pltpu.make_async_copy(source.at[part], target.at[part], block_sem.at[n, z // CHUNK])
            for n, (source, target) in enumerate((
                (temp_hbm, temp_ref), (kappa_hbm, kappa_ref), (slope_hbm, slope_ref), (power_hbm, power_ref),
            ))
        ])
    for block in blocks:
        for copy in block:
            copy.start()

    def ready(z):
        if z % CHUNK == 0:
            for copy in blocks[z // CHUNK]:
                copy.wait()

    def emit(z, temp, cond, heat):
        next_ref[z] = temp + heat + time_step * power_ref[z]

    closed_heat(temp_ref, kappa_ref, slope_ref, emit, ready)


def edge_kernel(
    first_ref, temp_ref, kappa_ref, slope_ref, core_ref, step_ref,
    next_ref, yo_ref, line_ref, strip_ref, small_ref,
):
    layers, rows, cols = temp_ref.shape
    span = 2 * rows + 8
    group, groups = lax.axis_index("grp"), lax.axis_size("grp")
    even = lax.rem(group, 2) == 0
    ya, yb = core_ref[span : span + 4 * layers, :], step_ref[...]
    low, high = jnp.where(even, yb, ya), jnp.where(even, ya, yb)
    yo_ref[0 : 4 * layers, :] = low
    yo_ref[4 * layers :, :] = high
    low_open = jnp.where(group == 0, 0.0, 1.0)
    high_open = jnp.where(group == groups - 1, 0.0, 1.0)

    row = lax.broadcasted_iota(jnp.int32, (rows, cols), 0)
    lane = lax.broadcasted_iota(jnp.int32, (rows, TILE), 1)
    small_ref[...] = jnp.zeros_like(small_ref)
    lane1 = lax.broadcasted_iota(jnp.int32, (1, TILE), 1)
    for z in range(layers):
        temp, kappa, slope = temp_ref[z], kappa_ref[z], slope_ref[z]
        after = first_ref[z]
        edges = []
        for side, base, at, opened in ((0, 0, 0, low_open), (1, 4 * layers, rows - 1, high_open)):
            temp_h = yo_ref[base + layers + z : base + layers + z + 1, :]
            cond_h = conduct(
                yo_ref[base + 2 * layers + z : base + 2 * layers + z + 1, :],
                yo_ref[base + 3 * layers + z : base + 3 * layers + z + 1, :],
                temp_h,
            )
            temp_e = temp[at : at + 1]
            cond_e = conduct(kappa[at : at + 1], slope[at : at + 1], temp_e)
            flux = opened * face(cond_e, cond_h, temp_e, temp_h)
            halo = yo_ref[base + z : base + z + 1, :] - flux
            yo_ref[base + z : base + z + 1, :] = halo
            edges.append(flux)
            corner = jnp.where(
                lane1 == 0,
                temp_h[:, 0:TILE],
                jnp.where(
                    lane1 == 1,
                    pltpu.roll(cond_h[:, 0:TILE], 1, 1),
                    jnp.where(
                        lane1 == 4,
                        pltpu.roll(temp_h[:, cols - TILE :], 5, 1),
                        pltpu.roll(cond_h[:, cols - TILE :], 6, 1),
                    ),
                ),
            )
            small_ref[16 * side + z : 16 * side + z + 1, :] = corner
        after = after + jnp.where(row == 0, edges[0], jnp.where(row == rows - 1, edges[1], 0.0))
        next_ref[z] = after
        packed = None
        for n, value in enumerate((after, temp, kappa, slope)):
            left = value[:, 0:TILE]
            right = pltpu.roll(value[:, cols - TILE :], n + 5, 1)
            left = pltpu.roll(left, n, 1) if n else left
            packed = left if packed is None else jnp.where(lane == n, left, packed)
            packed = jnp.where(lane == n + 4, right, packed)
        strip_ref[z * rows : (z + 1) * rows, :] = packed
    line_ref[0:8, :] = strip_ref[...].T[0:8, :]
    line_ref[8:16, 0:TILE] = small_ref[...].T[0:8, :]


def select_kernel(
    old_ref, halo_ref, line_ref, temp_ref, own_ref, core_ref, cross_ref, relay_ref, map_ref,
    top_ref, yo_ref, sa_ref, sb_ref, fw_ref, crow_ref, all_ref, tmp_ref,
):
    rows, cols = old_ref.shape[1:]
    layers = temp_ref.shape[0]
    span = 2 * rows + 8
    group, groups = lax.axis_index("grp"), lax.axis_size("grp")
    place_even = lax.rem(lax.axis_index("loop"), 2) == 0
    beside = group + 1 - 2 * lax.rem(group, 2)
    extra = jnp.zeros((8, cols), F32)
    for ref, owner in (
        (own_ref, group), (core_ref, beside), (cross_ref, groups - 1 - group), (relay_ref, groups - 1 - beside),
    ):
        part = pl.ds(pl.multiple_of(owner * rows, 8), rows)
        all_ref[part, 0:cols] = ref[0:rows, :]
        all_ref[part, cols : 2 * cols] = ref[rows : 2 * rows, :]
        extra = extra + ref[2 * rows : span, :]
    flow_all, wall_all = all_ref[:, 0:cols], all_ref[:, cols : 2 * cols]
    chooser = one_hot(map_ref[...], group * rows - 8, rows + 16)
    both = pick(chooser, all_ref[...], ((1,), (0,)))
    flow_y, wall_y = both[:, :cols], both[:, cols:]
    flow, wall = flow_y[8 : 8 + rows], wall_y[8 : 8 + rows]
    fw_ref[0:rows, :] = flow
    fw_ref[rows:, :] = wall
    sink = wall * (temp_ref[0] - flow)
    for base, at in ((0, 7), (4 * layers, 8 + rows)):
        temp = halo_ref[base + layers : base + layers + 1, :]
        heat = wall_y[at : at + 1] * (temp - flow_y[at : at + 1])
        yo_ref[base : base + 8, :] = halo_ref[base : base + 8, :]
        yo_ref[base : base + 1, :] = halo_ref[base : base + 1, :] - time_step * heat
    top_ref[0] = old_ref[0] - time_step * sink
    lane = lax.broadcasted_iota(jnp.int32, (rows, TILE), 1)
    tmp_ref[...] = jnp.zeros_like(tmp_ref)
    tmp_ref[0:rows, :] = jnp.where(lane == 0, sink[:, 0:TILE], pltpu.roll(sink[:, cols - TILE :], 2, 1))
    sunk = tmp_ref[...].T[0:8, :]
    lane_c = lax.broadcasted_iota(jnp.int32, (groups * rows, TILE), 1)
    right_flow = flow_all[:, cols - TILE :]
    pack = jnp.where(lane_c < 2, flow_all[:, 0:TILE], pltpu.roll(right_flow, 4, 1))
    pack = jnp.where(lane_c == 4, pltpu.roll(wall_all[:, 0:TILE], 4, 1), pack)
    pack = jnp.where(lane_c == 5, pltpu.roll(wall_all[:, cols - TILE :], 6, 1), pack)
    turned = pack.T
    flow_0, flow_1 = turned[0:1], turned[1:2]
    flow_m, flow_e = turned[2:3], turned[3:4]
    wall_0, wall_e = turned[4:5], turned[5:6]
    top = pick_rows(extra, one_hot(map_ref[...], 0, groups * rows))
    toward = extra[2:3]
    flux_0 = wall_0 * (top[0:1] - flow_0)
    flux_e = wall_e * (top[1:2] - flow_e)
    part_0 = (1.0 - courant) * flow_0 + courant * (1.0 - toward) * flow_1 + heat_gain * flux_0
    part_e = (1.0 - courant) * flow_e + courant * toward * flow_m + heat_gain * flux_e
    crow_ref[...] = jnp.zeros_like(crow_ref)
    crow_ref[0:1, :] = toward
    crow_ref[1:2, :] = flow_0
    crow_ref[2:3, :] = flow_e
    crow_ref[3:4, :] = wall_0
    crow_ref[4:5, :] = wall_e
    channels = groups * rows
    for ref, pick_right in ((sa_ref, place_even), (sb_ref, jnp.logical_not(place_even))):
        ref[...] = jnp.zeros_like(ref)
        ref[0:4, 0 : layers * rows] = jnp.where(pick_right, line_ref[4:8, :], line_ref[0:4, :])
        ref[0:1, 0:rows] = ref[0:1, 0:rows] - time_step * jnp.where(
            pick_right, sunk[1:2, 0:rows], sunk[0:1, 0:rows]
        )
        ref[4:6, 0:TILE] = jnp.where(pick_right, line_ref[12:14, 0:TILE], line_ref[8:10, 0:TILE])
        ref[4:5, channels : 2 * channels] = jnp.where(pick_right, extra[1:2], extra[0:1])
        ref[5:6, channels : 2 * channels] = jnp.where(pick_right, extra[4:5], extra[3:4])
        ref[6:7, 0:channels] = jnp.where(pick_right, flow_e, flow_0)
        ref[7:8, 0:channels] = jnp.where(pick_right, part_e, part_0)


def coolant_kernel(fw_ref, temp_ref, after_ref, crow_ref, map_ref, first_ref, second_ref):
    rows, cols = first_ref.shape
    channels = crow_ref.shape[1]
    chooser = one_hot(map_ref[...], lax.axis_index("grp") * rows, rows)
    toward = lax.dot_general(
        chooser, jnp.broadcast_to(crow_ref[0:1, :], (TILE, channels)).astype(BF16), (((1,), (1,)), ((), ())),
        preferred_element_type=F32,
    )
    toward = jnp.concatenate([toward] * (cols // TILE), 1) > 0.5
    lane = lax.broadcasted_iota(jnp.int32, (rows, cols), 1)

    def advance(flow, temp):
        before = jnp.where(lane == 0, 0.0, pltpu.roll(flow, 1, 1))
        after = jnp.where(lane == cols - 1, 0.0, pltpu.roll(flow, cols - 1, 1))
        flux = fw_ref[rows:, :] * (temp - flow)
        return flow - courant * (flow - jnp.where(toward, before, after)) + heat_gain * flux

    first = advance(fw_ref[0:rows, :], temp_ref[0])
    first_ref[...] = first
    second_ref[...] = advance(first, after_ref[0])


def close_kernel(
    temp_ref, kappa_ref, slope_ref, power_ref, yo_ref, ra_ref, rb_ref, sa_ref, sb_ref,
    flow_ref, fw_ref, crow_ref, map_ref, link_ref,
    out_hbm, tail_ref, add_ref, wide_ref, xt_ref, xc_ref, xf_ref, full_ref, out_ref, turn_ref, out_sem,
):
    layers, rows, cols = temp_ref.shape
    group, groups = lax.axis_index("grp"), lax.axis_size("grp")
    place, places = lax.axis_index("loop"), lax.axis_size("loop")
    even = lax.rem(place, 2) == 0
    channels = crow_ref.shape[1]
    low_open = jnp.where(group == 0, 0.0, 1.0)
    high_open = jnp.where(group == groups - 1, 0.0, 1.0)
    got_a, got_b, own_a, own_b = (ref[0:8, 0 : layers * rows] for ref in (ra_ref, rb_ref, sa_ref, sb_ref))
    got = (jnp.where(even, got_b, got_a), jnp.where(even, got_a, got_b))
    own = (jnp.where(even, own_b, own_a), jnp.where(even, own_a, own_b))

    def turn(first, last, ref):
        wide_ref[0:1, 0 : first.shape[1]] = first
        wide_ref[TILE - 1 : TILE, 0 : last.shape[1]] = last
        ref[...] = wide_ref[:, 0 : ref.shape[0]].T

    wide_ref[...] = jnp.zeros_like(wide_ref)
    temps, conds, fluxes = [], [], []
    for side in range(2):
        temp_n, temp_o = got[side][1:2], own[side][1:2]
        cond_n = conduct(got[side][2:3], got[side][3:4], temp_n)
        cond_o = conduct(own[side][2:3], own[side][3:4], temp_o)
        flux = face(cond_o, cond_n, temp_o, temp_n)
        after = got[side][0:1] - flux
        temps.append(after)
        conds.append(conduct(got[side][2:3], got[side][3:4], after))
        fluxes.append(flux)
    turn(temps[0], temps[1], xt_ref)
    turn(conds[0], conds[1], xc_ref)
    turn(fluxes[0], fluxes[1], xf_ref)

    wide_ref[0:1, 0:TILE] = got[0][4:5, 0:TILE]
    wide_ref[TILE - 1 : TILE, 0:TILE] = got[1][4:5, 0:TILE]
    corner_t = wide_ref[:, 0:TILE].T
    wide_ref[0:1, 0:TILE] = got[0][5:6, 0:TILE]
    wide_ref[TILE - 1 : TILE, 0:TILE] = got[1][5:6, 0:TILE]
    corner_c = wide_ref[:, 0:TILE].T
    lane_l = lax.broadcasted_iota(jnp.int32, (layers, TILE), 1)
    halo = []
    for side in range(2):
        base = 4 * layers * side
        after = yo_ref[base : base + layers, :]
        before = yo_ref[base + layers : base + 2 * layers, :]
        kappa = yo_ref[base + 2 * layers : base + 3 * layers, :]
        slope = yo_ref[base + 3 * layers : base + 4 * layers, :]
        cond = conduct(kappa, slope, before)
        c_t, c_c = corner_t[16 * side : 16 * side + layers], corner_c[16 * side : 16 * side + layers]
        tiles = []
        for start, at in ((0, 0), (cols - TILE, TILE - 1)):
            flux = face(
                cond[:, start : start + TILE], c_c, before[:, start : start + TILE], c_t
            )
            tiles.append(after[:, start : start + TILE] + jnp.where(lane_l == at, flux, 0.0))
        after = jnp.concatenate([tiles[0], after[:, TILE : cols - TILE], tiles[1]], 1) if (
            cols > 2 * TILE
        ) else jnp.concatenate(tiles, 1)
        halo.append((after, conduct(kappa, slope, after)))

    lane = lax.broadcasted_iota(jnp.int32, (rows, TILE), 1)
    for z in range(layers):
        add = xf_ref[z * rows : (z + 1) * rows, :]
        full_ref[z] = temp_ref[z]
        full_ref[z, :, 0:TILE] = temp_ref[z, :, 0:TILE] + jnp.where(lane == 0, add, 0.0)
        full_ref[z, :, cols - TILE :] = temp_ref[z, :, cols - TILE :] + jnp.where(
            lane == TILE - 1, add, 0.0
        )

    toward_c = crow_ref[0:1, :]
    first_place = place == 0
    last_place = place == places - 1
    link = one_hot(link_ref[...], 0, channels)
    stack = jnp.concatenate(
        [got[0][6:7, 0:channels], got[1][6:7, 0:channels], crow_ref[1:3, :], crow_ref[4:8, :]], 0
    )
    moved = pick_rows(stack, link)
    own_0 = jnp.where(first_place, moved[2:3], stack[2:3])
    own_e = jnp.where(last_place, moved[3:4], stack[3:4])
    late_l = got[0][7:8, 0:channels] + courant * (1.0 - toward_c) * own_0
    late_r = got[1][7:8, 0:channels] + courant * toward_c * own_e
    late = jnp.concatenate([late_l, late_r, crow_ref[2:8, :]], 0)
    late_moved = pick_rows(late, link)
    edge_rows = (
        (jnp.where(first_place, moved[0:1], stack[0:1]), jnp.where(last_place, moved[1:2], stack[1:2])),
        (jnp.where(first_place, late_moved[0:1], late_l), jnp.where(last_place, late_moved[1:2], late_r)),
    )
    shift_0 = courant * toward_c * edge_rows[0][0]
    shift_e = courant * (1.0 - toward_c) * edge_rows[0][1]
    tops = [
        face(
            own[side][5:6, channels : 2 * channels], got[side][5:6, channels : 2 * channels],
            own[side][4:5, channels : 2 * channels], got[side][4:5, channels : 2 * channels],
        )
        for side in range(2)
    ]
    every = one_hot(map_ref[...], 0, channels)
    tops = pick_rows(jnp.concatenate(tops + [crow_ref[2:8, :]], 0), every)
    wall_0, wall_e = crow_ref[3:4, :], crow_ref[4:5, :]
    add_0 = (
        courant * toward_c * edge_rows[1][0]
        + ((1.0 - courant) - heat_gain * wall_0) * shift_0
        + heat_gain * wall_0 * tops[0:1]
    )
    add_e = (
        courant * (1.0 - toward_c) * edge_rows[1][1]
        + ((1.0 - courant) - heat_gain * wall_e) * shift_e
        + heat_gain * wall_e * tops[1:2]
    )
    wide_row = lax.broadcasted_iota(jnp.int32, (TILE, channels), 0)
    chooser = one_hot(map_ref[...], group * rows, rows)
    edge_y = pick(chooser, jnp.where(wide_row == 0, shift_0, shift_e), ((1,), (1,)))
    adds = jnp.where(wide_row == 0, add_0, jnp.where(wide_row == 1, courant * toward_c * shift_0, add_e))
    adds = jnp.where(wide_row == TILE - 2, courant * (1.0 - toward_c) * shift_e, adds)
    turn_ref[0:channels, :] = adds.T
    turn_ref[channels:, :] = jnp.broadcast_to(map_ref[...].astype(F32), (TILE, channels)).T
    add_ref[0:rows, :] = turn_ref[pl.ds(pl.multiple_of(group * rows, 8), rows), :]
    add_ref[rows:, :] = turn_ref[pl.ds(pl.multiple_of(channels + group * rows, 8), rows), :]
    pad = [jnp.zeros((rows, cols - 2 * TILE), F32)] if cols > 2 * TILE else []
    flow = flow_ref[...] + jnp.concatenate(
        [jnp.where(lane == 0, edge_y, 0.0)] + pad + [jnp.where(lane == TILE - 1, edge_y, 0.0)], 1
    )
    flux = fw_ref[rows:, :] * (full_ref[0] - flow)

    row8 = lax.broadcasted_iota(jnp.int32, (8, cols), 0)

    def emit(z, temp, cond, heat):
        result = temp + heat + time_step * power_ref[z]
        if z == 0:
            result = result - time_step * flux
        halo_t = xt_ref[z * rows : (z + 1) * rows, :]
        halo_c = xc_ref[z * rows : (z + 1) * rows, :]
        sides = []
        for start, at in ((0, 0), (cols - TILE, TILE - 1)):
            part = slice(start, start + TILE)
            extra = face(cond[:, part], halo_c, temp[:, part], halo_t)
            sides.append(jnp.where(lane == at, extra, 0.0))
        middle = [jnp.zeros((rows, cols - 2 * TILE), F32)] if cols > 2 * TILE else []
        result = result + jnp.concatenate([sides[0]] + middle + [sides[1]], 1)
        early = layers - tail_ref.shape[0]
        target, at_z = (out_ref, z) if z < early else (tail_ref, z - early)
        target[at_z] = result
        for side, opened, start, at in ((0, low_open, 0, 0), (1, high_open, rows - 8, 7)):
            part = slice(start, start + 8)
            extra = opened * face(
                cond[part], halo[side][1][z : z + 1], temp[part], halo[side][0][z : z + 1]
            )
            target[at_z, part, :] = result[part] + jnp.where(row8 == at, extra, 0.0)
        if z < early:
            copies.append(pltpu.make_async_copy(out_ref.at[z], out_hbm.at[z], out_sem.at[z]))
            copies[-1].start()

    copies = []
    closed_heat(full_ref, kappa_ref, slope_ref, emit)
    for copy in copies:
        copy.wait()


def return_kernel(
    part_hbm, tail_ref, own_ref, cross_ref, core_ref, relay_ref, add_ref,
    out_hbm, flow_hbm, all_ref, out_ref, sem,
):
    rows, cols = out_ref.shape
    layers, late = out_hbm.shape[0], tail_ref.shape[0]
    tail = pltpu.make_async_copy(tail_ref, out_hbm.at[layers - late : layers], sem.at[0])
    tail.start()
    group, groups = lax.axis_index("grp"), lax.axis_size("grp")
    beside = group + 1 - 2 * lax.rem(group, 2)
    for ref, owner in (
        (own_ref, group), (core_ref, beside), (cross_ref, groups - 1 - group), (relay_ref, groups - 1 - beside),
    ):
        all_ref[pl.ds(pl.multiple_of(owner * rows, 8), rows), :] = ref[...]
    lane = lax.broadcasted_iota(jnp.int32, (rows, TILE), 1)
    adds, row = add_ref[0:rows, :], add_ref[rows:, :]
    channels = groups * rows
    chooser = jnp.concatenate(
        [jnp.where(row == (lane + start).astype(F32), 1.0, 0.0) for start in range(0, channels, TILE)], 1
    ).astype(BF16)
    flow = pick(chooser, all_ref[...], ((1,), (0,)))
    pad = [jnp.zeros((rows, cols - 2 * TILE), F32)] if cols > 2 * TILE else []
    out_ref[...] = flow + jnp.concatenate(
        [jnp.where(lane < 2, adds, 0.0)] + pad + [jnp.where(lane >= TILE - 2, adds, 0.0)], 1
    )
    back = pltpu.make_async_copy(out_ref, flow_hbm, sem.at[1])
    back.start()
    tail.wait()
    back.wait()


def pairs(count, first, closed):
    swaps = []
    for low in range(first, count, 2):
        high = low + 1
        if high == count:
            if not closed:
                continue
            high = 0
        swaps += [(low, high), (high, low)]
    return swaps


def shards(
    solid_temp, kappa, slope, power, coolant_temp, wall_coeff, channel_map, flow_dir, loop_link
):
    groups, places = lax.axis_size("grp"), lax.axis_size("loop")
    layers, rows, cols = solid_temp.shape
    channels = groups * rows
    strip = layers * rows
    params = pltpu.CompilerParams(vmem_limit_bytes=48 * 1024 * 1024)

    def shape(*dims):
        return jax.ShapeDtypeStruct(dims, F32)

    def call(body, outs, scratch, *args, far=0, outs_far=0, cost=None, alias={}):
        return pl.pallas_call(
            body,
            out_shape=outs,
            in_specs=[pl.BlockSpec(memory_space=pltpu.HBM)] * far + [pl.BlockSpec(memory_space=pltpu.VMEM)] * (len(args) - far),
            out_specs=[pl.BlockSpec(memory_space=pltpu.HBM)] * outs_far
            + [pl.BlockSpec(memory_space=pltpu.VMEM)] * (len(outs) - outs_far),
            scratch_shapes=scratch,
            compiler_params=params,
            cost_estimate=cost,
            input_output_aliases=alias,
        )(*[pltpu.with_memory_space_constraint(arg, pltpu.HBM) for arg in args[:far]], *args[far:])

    def vmem(*dims):
        return pltpu.VMEM(dims, F32)

    heavy = pl.CostEstimate(
        flops=30 * layers * rows * cols, bytes_accessed=36 * layers * rows * cols, transcendentals=0
    )
    block = shape(layers, rows, cols)
    share = shape(2 * rows + 8, cols)
    wide = shape(2 * rows + 8 + 4 * layers, cols)
    index = jax.ShapeDtypeStruct((1, channels), jnp.int32)
    core, cross, step, map_row, link_row = call(
        pack_kernel,
        (wide, share, shape(4 * layers, cols), index, index),
        [
            vmem(layers, 8, cols), vmem(layers, 8, cols), vmem(layers, 8, cols), vmem(layers, 8, cols),
            vmem(3, rows, cols), vmem(TILE, TILE), vmem(8, cols), pltpu.VMEM((1, rows), jnp.int32),
            pltpu.SemaphoreType.DMA((4, 2)), pltpu.SemaphoreType.DMA((3,)), pltpu.SemaphoreType.DMA((2,)),
            pltpu.SemaphoreType.DMA((3,)),
        ],
        solid_temp, kappa, slope, power, coolant_temp, wall_coeff, flow_dir.reshape(1, rows),
        channel_map, loop_link.reshape(1, channels),
        far=9,
    )
    beside = [(i, i + 1 - 2 * (i % 2)) for i in range(groups)]
    across = [(i, groups - 1 - i) for i in range(groups)]
    got_cross = lax.ppermute(cross, "grp", across)
    got_step = lax.ppermute(step, "grp", pairs(groups, 1, False))
    got_core = lax.ppermute(core, "grp", beside)
    first, temp, kappa, slope, power = call(
        open_kernel,
        (block, block, block, block, block),
        [pltpu.SemaphoreType.DMA((4, layers // CHUNK))],
        solid_temp, kappa, slope, power, map_row,
        far=4,
        cost=heavy,
    )
    got_cross, got_step, first = lax.optimization_barrier((got_cross, got_step, first))
    relay = lax.ppermute(got_cross, "grp", beside)
    after, yo, line = call(
        edge_kernel,
        (block, shape(8 * layers, cols), shape(16, strip)),
        [vmem(strip, TILE), vmem(TILE, TILE)],
        first, temp, kappa, slope, got_core, got_step,
        cost=heavy,
    )
    after, yo, sa, sb, fw, crow = call(
        select_kernel,
        (
            block, shape(8 * layers, cols), shape(16, strip + strip // 3), shape(16, strip + strip // 3),
            shape(2 * rows, cols), shape(8, channels),
        ),
        [vmem(channels, 2 * cols), vmem(TILE, TILE)],
        after, yo, line, temp, core, got_core, got_cross, relay, map_row,
        alias={0: 0, 1: 1},
    )
    ra = lax.ppermute(sa, "loop", pairs(places, 0, True))
    rb = lax.ppermute(sb, "loop", pairs(places, 1, True))
    flow1, flow = call(
        coolant_kernel, (shape(rows, cols), shape(rows, cols)), [], fw, temp, after, crow, map_row,
    )
    got_across = lax.ppermute(flow, "grp", across)
    got_over = lax.ppermute(flow, "grp", [(i, (i + groups // 2) % groups) for i in range(groups)])
    got_beside = lax.ppermute(flow, "grp", beside)
    late = layers // 2
    out, tail, adds = call(
        close_kernel,
        (block, shape(late, rows, cols), shape(2 * rows, TILE)),
        [
            vmem(TILE, strip), vmem(strip, TILE), vmem(strip, TILE), vmem(strip, TILE),
            vmem(layers, rows, cols), vmem(layers - late, rows, cols), vmem(2 * channels, TILE),
            pltpu.SemaphoreType.DMA((layers - late,)),
        ],
        after, kappa, slope, power, yo, ra, rb, sa, sb, flow1, fw, crow, map_row, link_row,
        outs_far=1,
        cost=heavy,
    )
    return call(
        return_kernel,
        (block, shape(rows, cols)),
        [vmem(channels, cols), vmem(rows, cols), pltpu.SemaphoreType.DMA((2,))],
        out, tail, flow, got_across, got_beside, got_over, adds,
        far=1,
        outs_far=2,
        alias={0: 0},
    )


def solution(mesh):
    block = P(None, "grp", "loop")
    plane = P("grp", "loop")
    return jax.shard_map(
        shards,
        mesh=mesh,
        in_specs=(block, block, block, block, plane, plane, P("loop", None), P("grp"), P()),
        out_specs=(block, plane),
        check_vma=False,
    )
```

```python
import jax
import jax.numpy as jnp
from jax import lax
from jax.experimental import pallas as pl
from jax.experimental.pallas import tpu as pltpu
from jax.sharding import PartitionSpec as P

time_step = 0.06
courant = 0.5
heat_gain = 0.5
TILE = 128
CHUNK = 4
F32 = jnp.float32
BF16 = jnp.bfloat16


def split3(value):
    high = value.astype(BF16)
    rest = value - high.astype(F32)
    middle = rest.astype(BF16)
    low = (rest - middle.astype(F32)).astype(BF16)
    return high, middle, low


def pick(chooser, value, dims):
    total = None
    for part in split3(value):
        term = lax.dot_general(chooser, part, (dims, ((), ())), preferred_element_type=F32)
        total = term if total is None else total + term
    return total


def pick_rows(value, chooser):
    total = None
    for part in split3(value):
        term = lax.dot_general(part, chooser, (((1,), (0,)), ((), ())), preferred_element_type=F32)
        total = term if total is None else total + term
    return total


def one_hot(index_row, first, count):
    shape = (count, index_row.shape[1])
    here = lax.broadcasted_iota(jnp.int32, shape, 0) + first
    return jnp.where(index_row == here, 1.0, 0.0).astype(BF16)


def conduct(kappa, slope, temp):
    return (0.5 * time_step) * kappa * (1.0 + slope * temp)


def face(cond_a, cond_b, temp_a, temp_b):
    return (cond_a + cond_b) * (temp_b - temp_a)


def closed_heat(temp_ref, kappa_ref, slope_ref, emit, ready=lambda z: None):
    layers, rows, cols = temp_ref.shape
    lane = lax.broadcasted_iota(jnp.int32, (rows, cols), 1)
    row = lax.broadcasted_iota(jnp.int32, (rows, cols), 0)
    ready(0)
    temp = temp_ref[0]
    cond = conduct(kappa_ref[0], slope_ref[0], temp)
    flux_below = None
    for z in range(layers):
        if z + 1 < layers:
            ready(z + 1)
        flux_x = face(cond, pltpu.roll(cond, cols - 1, 1), temp, pltpu.roll(temp, cols - 1, 1))
        flux_x = jnp.where(lane == cols - 1, 0.0, flux_x)
        heat = flux_x - pltpu.roll(flux_x, 1, 1)
        flux_y = face(cond, pltpu.roll(cond, rows - 1, 0), temp, pltpu.roll(temp, rows - 1, 0))
        flux_y = jnp.where(row == rows - 1, 0.0, flux_y)
        heat = heat + flux_y - pltpu.roll(flux_y, 1, 0)
        if flux_below is not None:
            heat = heat - flux_below
        if z + 1 < layers:
            temp_up = temp_ref[z + 1]
            cond_up = conduct(kappa_ref[z + 1], slope_ref[z + 1], temp_up)
            flux_below = face(cond, cond_up, temp, temp_up)
            heat = heat + flux_below
        emit(z, temp, cond, heat)
        if z + 1 < layers:
            temp, cond = temp_up, cond_up


def pack_kernel(
    temp_hbm, kappa_hbm, slope_hbm, power_hbm, flow_hbm, wall_hbm, dir_hbm, map_hbm, link_hbm,
    core_ref, cross_ref, step_ref, map_ref, link_ref,
    temp_ref, kappa_ref, slope_ref, power_ref, top_ref, tmp_ref, row_ref, dir_ref,
    block_sem, top_sem, share_sem, small_sem,
):
    layers, rows, cols = temp_hbm.shape
    share = 2 * rows + 8
    group = lax.axis_index("grp")
    even = lax.rem(group, 2) == 0
    copies = []
    for n, (source, target) in enumerate((
        (temp_hbm, temp_ref), (kappa_hbm, kappa_ref), (slope_hbm, slope_ref), (power_hbm, power_ref),
    )):
        copies.append(pltpu.make_async_copy(source.at[:, 0:2], target.at[:, 0:2], block_sem.at[n, 0]))
        copies.append(
            pltpu.make_async_copy(source.at[:, rows - 2 : rows], target.at[:, 6:8], block_sem.at[n, 1])
        )
    tops = [
        pltpu.make_async_copy(source.at[0], top_ref.at[n], top_sem.at[n])
        for n, source in enumerate((temp_hbm, kappa_hbm, slope_hbm))
    ]
    smalls = [
        pltpu.make_async_copy(source, target, small_sem.at[n])
        for n, (source, target) in enumerate(((dir_hbm, dir_ref), (map_hbm, map_ref), (link_hbm, link_ref)))
    ]
    smalls.append(pltpu.make_async_copy(flow_hbm, cross_ref.at[0:rows], share_sem.at[0]))
    smalls.append(pltpu.make_async_copy(wall_hbm, cross_ref.at[rows : 2 * rows], share_sem.at[1]))
    for copy in copies + tops + smalls:
        copy.start()
    tmp_ref[...] = jnp.zeros_like(tmp_ref)
    row_ref[...] = jnp.zeros_like(row_ref)
    for copy in copies:
        copy.wait()

    def emit(z, temp, cond, heat):
        after = temp + heat + time_step * power_ref[z]
        for q, value in enumerate((after, temp, kappa_ref[z], slope_ref[z])):
            at = q * layers + z
            core_ref[share + at : share + at + 1, :] = jnp.where(even, value[7:8], value[0:1])
            step_ref[at : at + 1, :] = jnp.where(even, value[0:1], value[7:8])

    closed_heat(temp_ref, kappa_ref, slope_ref, emit)
    for copy in tops:
        copy.wait()
    temp = top_ref[0]
    cond = conduct(top_ref[1], top_ref[2], temp)
    lane = lax.broadcasted_iota(jnp.int32, (rows, TILE), 1)
    packed = jnp.where(lane == 0, temp[:, 0:TILE], pltpu.roll(temp[:, cols - TILE :], 2, 1))
    packed = jnp.where(lane == 3, pltpu.roll(cond[:, 0:TILE], 3, 1), packed)
    packed = jnp.where(lane == 4, pltpu.roll(cond[:, cols - TILE :], 5, 1), packed)
    tmp_ref[0:rows, :] = packed
    row_ref[0:8, 0:TILE] = tmp_ref[...].T[0:8, :]
    for copy in smalls:
        copy.wait()
    row_ref[2:3, 0:rows] = dir_ref[...].astype(F32)
    extra = pltpu.roll(row_ref[...], group * rows, 1)
    cross_ref[2 * rows : share, :] = extra
    core_ref[2 * rows : share, :] = extra
    core_ref[0 : 2 * rows, :] = cross_ref[0 : 2 * rows, :]


def open_kernel(
    temp_hbm, kappa_hbm, slope_hbm, power_hbm, after_ref,
    next_ref, temp_ref, kappa_ref, slope_ref, power_ref, block_sem,
):
    layers = temp_ref.shape[0]
    blocks = []
    for z in range(0, layers, CHUNK):
        part = pl.ds(z, CHUNK)
        blocks.append([
            pltpu.make_async_copy(source.at[part], target.at[part], block_sem.at[n, z // CHUNK])
            for n, (source, target) in enumerate((
                (temp_hbm, temp_ref), (kappa_hbm, kappa_ref), (slope_hbm, slope_ref), (power_hbm, power_ref),
            ))
        ])
    for block in blocks:
        for copy in block:
            copy.start()

    def ready(z):
        if z % CHUNK == 0:
            for copy in blocks[z // CHUNK]:
                copy.wait()

    def emit(z, temp, cond, heat):
        next_ref[z] = temp + heat + time_step * power_ref[z]

    closed_heat(temp_ref, kappa_ref, slope_ref, emit, ready)


def edge_kernel(
    first_ref, temp_ref, kappa_ref, slope_ref, core_ref, step_ref,
    next_ref, yo_ref, line_ref, strip_ref, small_ref,
):
    layers, rows, cols = temp_ref.shape
    span = 2 * rows + 8
    group, groups = lax.axis_index("grp"), lax.axis_size("grp")
    even = lax.rem(group, 2) == 0
    ya, yb = core_ref[span : span + 4 * layers, :], step_ref[...]
    low, high = jnp.where(even, yb, ya), jnp.where(even, ya, yb)
    yo_ref[0 : 4 * layers, :] = low
    yo_ref[4 * layers :, :] = high
    low_open = jnp.where(group == 0, 0.0, 1.0)
    high_open = jnp.where(group == groups - 1, 0.0, 1.0)

    row = lax.broadcasted_iota(jnp.int32, (rows, cols), 0)
    lane = lax.broadcasted_iota(jnp.int32, (rows, TILE), 1)
    small_ref[...] = jnp.zeros_like(small_ref)
    lane1 = lax.broadcasted_iota(jnp.int32, (1, TILE), 1)
    for z in range(layers):
        temp, kappa, slope = temp_ref[z], kappa_ref[z], slope_ref[z]
        after = first_ref[z]
        edges = []
        for side, base, at, opened in ((0, 0, 0, low_open), (1, 4 * layers, rows - 1, high_open)):
            temp_h = yo_ref[base + layers + z : base + layers + z + 1, :]
            cond_h = conduct(
                yo_ref[base + 2 * layers + z : base + 2 * layers + z + 1, :],
                yo_ref[base + 3 * layers + z : base + 3 * layers + z + 1, :],
                temp_h,
            )
            temp_e = temp[at : at + 1]
            cond_e = conduct(kappa[at : at + 1], slope[at : at + 1], temp_e)
            flux = opened * face(cond_e, cond_h, temp_e, temp_h)
            halo = yo_ref[base + z : base + z + 1, :] - flux
            yo_ref[base + z : base + z + 1, :] = halo
            edges.append(flux)
            corner = jnp.where(
                lane1 == 0,
                temp_h[:, 0:TILE],
                jnp.where(
                    lane1 == 1,
                    pltpu.roll(cond_h[:, 0:TILE], 1, 1),
                    jnp.where(
                        lane1 == 4,
                        pltpu.roll(temp_h[:, cols - TILE :], 5, 1),
                        pltpu.roll(cond_h[:, cols - TILE :], 6, 1),
                    ),
                ),
            )
            small_ref[16 * side + z : 16 * side + z + 1, :] = corner
        after = after + jnp.where(row == 0, edges[0], jnp.where(row == rows - 1, edges[1], 0.0))
        next_ref[z] = after
        packed = None
        for n, value in enumerate((after, temp, kappa, slope)):
            left = value[:, 0:TILE]
            right = pltpu.roll(value[:, cols - TILE :], n + 5, 1)
            left = pltpu.roll(left, n, 1) if n else left
            packed = left if packed is None else jnp.where(lane == n, left, packed)
            packed = jnp.where(lane == n + 4, right, packed)
        strip_ref[z * rows : (z + 1) * rows, :] = packed
    line_ref[0:8, :] = strip_ref[...].T[0:8, :]
    line_ref[8:16, 0:TILE] = small_ref[...].T[0:8, :]


def select_kernel(
    old_ref, halo_ref, line_ref, temp_ref, own_ref, core_ref, cross_ref, relay_ref, map_ref,
    top_ref, yo_ref, sa_ref, sb_ref, fw_ref, crow_ref, all_ref, tmp_ref,
):
    rows, cols = old_ref.shape[1:]
    layers = temp_ref.shape[0]
    span = 2 * rows + 8
    group, groups = lax.axis_index("grp"), lax.axis_size("grp")
    place_even = lax.rem(lax.axis_index("loop"), 2) == 0
    beside = group + 1 - 2 * lax.rem(group, 2)
    extra = jnp.zeros((8, cols), F32)
    for ref, owner in (
        (own_ref, group), (core_ref, beside), (cross_ref, groups - 1 - group), (relay_ref, groups - 1 - beside),
    ):
        part = pl.ds(pl.multiple_of(owner * rows, 8), rows)
        all_ref[part, 0:cols] = ref[0:rows, :]
        all_ref[part, cols : 2 * cols] = ref[rows : 2 * rows, :]
        extra = extra + ref[2 * rows : span, :]
    flow_all, wall_all = all_ref[:, 0:cols], all_ref[:, cols : 2 * cols]
    chooser = one_hot(map_ref[...], group * rows - 8, rows + 16)
    both = pick(chooser, all_ref[...], ((1,), (0,)))
    flow_y, wall_y = both[:, :cols], both[:, cols:]
    flow, wall = flow_y[8 : 8 + rows], wall_y[8 : 8 + rows]
    fw_ref[0:rows, :] = flow
    fw_ref[rows:, :] = wall
    sink = wall * (temp_ref[0] - flow)
    for base, at in ((0, 7), (4 * layers, 8 + rows)):
        temp = halo_ref[base + layers : base + layers + 1, :]
        heat = wall_y[at : at + 1] * (temp - flow_y[at : at + 1])
        yo_ref[base : base + 8, :] = halo_ref[base : base + 8, :]
        yo_ref[base : base + 1, :] = halo_ref[base : base + 1, :] - time_step * heat
    top_ref[0] = old_ref[0] - time_step * sink
    lane = lax.broadcasted_iota(jnp.int32, (rows, TILE), 1)
    tmp_ref[...] = jnp.zeros_like(tmp_ref)
    tmp_ref[0:rows, :] = jnp.where(lane == 0, sink[:, 0:TILE], pltpu.roll(sink[:, cols - TILE :], 2, 1))
    sunk = tmp_ref[...].T[0:8, :]
    lane_c = lax.broadcasted_iota(jnp.int32, (groups * rows, TILE), 1)
    right_flow = flow_all[:, cols - TILE :]
    pack = jnp.where(lane_c < 2, flow_all[:, 0:TILE], pltpu.roll(right_flow, 4, 1))
    pack = jnp.where(lane_c == 4, pltpu.roll(wall_all[:, 0:TILE], 4, 1), pack)
    pack = jnp.where(lane_c == 5, pltpu.roll(wall_all[:, cols - TILE :], 6, 1), pack)
    turned = pack.T
    flow_0, flow_1 = turned[0:1], turned[1:2]
    flow_m, flow_e = turned[2:3], turned[3:4]
    wall_0, wall_e = turned[4:5], turned[5:6]
    top = pick_rows(extra, one_hot(map_ref[...], 0, groups * rows))
    toward = extra[2:3]
    flux_0 = wall_0 * (top[0:1] - flow_0)
    flux_e = wall_e * (top[1:2] - flow_e)
    part_0 = (1.0 - courant) * flow_0 + courant * (1.0 - toward) * flow_1 + heat_gain * flux_0
    part_e = (1.0 - courant) * flow_e + courant * toward * flow_m + heat_gain * flux_e
    crow_ref[...] = jnp.zeros_like(crow_ref)
    crow_ref[0:1, :] = toward
    crow_ref[1:2, :] = flow_0
    crow_ref[2:3, :] = flow_e
    crow_ref[3:4, :] = wall_0
    crow_ref[4:5, :] = wall_e
    channels = groups * rows
    for ref, pick_right in ((sa_ref, place_even), (sb_ref, jnp.logical_not(place_even))):
        ref[...] = jnp.zeros_like(ref)
        ref[0:4, 0 : layers * rows] = jnp.where(pick_right, line_ref[4:8, :], line_ref[0:4, :])
        ref[0:1, 0:rows] = ref[0:1, 0:rows] - time_step * jnp.where(
            pick_right, sunk[1:2, 0:rows], sunk[0:1, 0:rows]
        )
        ref[4:6, 0:TILE] = jnp.where(pick_right, line_ref[12:14, 0:TILE], line_ref[8:10, 0:TILE])
        ref[4:5, channels : 2 * channels] = jnp.where(pick_right, extra[1:2], extra[0:1])
        ref[5:6, channels : 2 * channels] = jnp.where(pick_right, extra[4:5], extra[3:4])
        ref[6:7, 0:channels] = jnp.where(pick_right, flow_e, flow_0)
        ref[7:8, 0:channels] = jnp.where(pick_right, part_e, part_0)


def coolant_kernel(fw_ref, temp_ref, after_ref, crow_ref, map_ref, first_ref, second_ref):
    rows, cols = first_ref.shape
    channels = crow_ref.shape[1]
    chooser = one_hot(map_ref[...], lax.axis_index("grp") * rows, rows)
    toward = lax.dot_general(
        chooser, jnp.broadcast_to(crow_ref[0:1, :], (TILE, channels)).astype(BF16), (((1,), (1,)), ((), ())),
        preferred_element_type=F32,
    )
    toward = jnp.concatenate([toward] * (cols // TILE), 1) > 0.5
    lane = lax.broadcasted_iota(jnp.int32, (rows, cols), 1)

    def advance(flow, temp):
        before = jnp.where(lane == 0, 0.0, pltpu.roll(flow, 1, 1))
        after = jnp.where(lane == cols - 1, 0.0, pltpu.roll(flow, cols - 1, 1))
        flux = fw_ref[rows:, :] * (temp - flow)
        return flow - courant * (flow - jnp.where(toward, before, after)) + heat_gain * flux

    first = advance(fw_ref[0:rows, :], temp_ref[0])
    first_ref[...] = first
    second_ref[...] = advance(first, after_ref[0])


def close_kernel(
    temp_ref, kappa_ref, slope_ref, power_ref, yo_ref, ra_ref, rb_ref, sa_ref, sb_ref,
    flow_ref, fw_ref, crow_ref, map_ref, link_ref,
    out_hbm, tail_ref, add_ref, wide_ref, xt_ref, xc_ref, xf_ref, full_ref, out_ref, turn_ref, out_sem,
):
    layers, rows, cols = temp_ref.shape
    group, groups = lax.axis_index("grp"), lax.axis_size("grp")
    place, places = lax.axis_index("loop"), lax.axis_size("loop")
    even = lax.rem(place, 2) == 0
    channels = crow_ref.shape[1]
    low_open = jnp.where(group == 0, 0.0, 1.0)
    high_open = jnp.where(group == groups - 1, 0.0, 1.0)
    got_a, got_b, own_a, own_b = (ref[0:8, 0 : layers * rows] for ref in (ra_ref, rb_ref, sa_ref, sb_ref))
    got = (jnp.where(even, got_b, got_a), jnp.where(even, got_a, got_b))
    own = (jnp.where(even, own_b, own_a), jnp.where(even, own_a, own_b))

    def turn(first, last, ref):
        wide_ref[0:1, 0 : first.shape[1]] = first
        wide_ref[TILE - 1 : TILE, 0 : last.shape[1]] = last
        ref[...] = wide_ref[:, 0 : ref.shape[0]].T

    wide_ref[...] = jnp.zeros_like(wide_ref)
    temps, conds, fluxes = [], [], []
    for side in range(2):
        temp_n, temp_o = got[side][1:2], own[side][1:2]
        cond_n = conduct(got[side][2:3], got[side][3:4], temp_n)
        cond_o = conduct(own[side][2:3], own[side][3:4], temp_o)
        flux = face(cond_o, cond_n, temp_o, temp_n)
        after = got[side][0:1] - flux
        temps.append(after)
        conds.append(conduct(got[side][2:3], got[side][3:4], after))
        fluxes.append(flux)
    turn(temps[0], temps[1], xt_ref)
    turn(conds[0], conds[1], xc_ref)
    turn(fluxes[0], fluxes[1], xf_ref)

    wide_ref[0:1, 0:TILE] = got[0][4:5, 0:TILE]
    wide_ref[TILE - 1 : TILE, 0:TILE] = got[1][4:5, 0:TILE]
    corner_t = wide_ref[:, 0:TILE].T
    wide_ref[0:1, 0:TILE] = got[0][5:6, 0:TILE]
    wide_ref[TILE - 1 : TILE, 0:TILE] = got[1][5:6, 0:TILE]
    corner_c = wide_ref[:, 0:TILE].T
    lane_l = lax.broadcasted_iota(jnp.int32, (layers, TILE), 1)
    halo = []
    for side in range(2):
        base = 4 * layers * side
        after = yo_ref[base : base + layers, :]
        before = yo_ref[base + layers : base + 2 * layers, :]
        kappa = yo_ref[base + 2 * layers : base + 3 * layers, :]
        slope = yo_ref[base + 3 * layers : base + 4 * layers, :]
        cond = conduct(kappa, slope, before)
        c_t, c_c = corner_t[16 * side : 16 * side + layers], corner_c[16 * side : 16 * side + layers]
        tiles = []
        for start, at in ((0, 0), (cols - TILE, TILE - 1)):
            flux = face(
                cond[:, start : start + TILE], c_c, before[:, start : start + TILE], c_t
            )
            tiles.append(after[:, start : start + TILE] + jnp.where(lane_l == at, flux, 0.0))
        after = jnp.concatenate([tiles[0], after[:, TILE : cols - TILE], tiles[1]], 1) if (
            cols > 2 * TILE
        ) else jnp.concatenate(tiles, 1)
        halo.append((after, conduct(kappa, slope, after)))

    lane = lax.broadcasted_iota(jnp.int32, (rows, TILE), 1)
    for z in range(layers):
        add = xf_ref[z * rows : (z + 1) * rows, :]
        full_ref[z] = temp_ref[z]
        full_ref[z, :, 0:TILE] = temp_ref[z, :, 0:TILE] + jnp.where(lane == 0, add, 0.0)
        full_ref[z, :, cols - TILE :] = temp_ref[z, :, cols - TILE :] + jnp.where(
            lane == TILE - 1, add, 0.0
        )

    toward_c = crow_ref[0:1, :]
    first_place = place == 0
    last_place = place == places - 1
    link = one_hot(link_ref[...], 0, channels)
    stack = jnp.concatenate(
        [got[0][6:7, 0:channels], got[1][6:7, 0:channels], crow_ref[1:3, :], crow_ref[4:8, :]], 0
    )
    moved = pick_rows(stack, link)
    own_0 = jnp.where(first_place, moved[2:3], stack[2:3])
    own_e = jnp.where(last_place, moved[3:4], stack[3:4])
    late_l = got[0][7:8, 0:channels] + courant * (1.0 - toward_c) * own_0
    late_r = got[1][7:8, 0:channels] + courant * toward_c * own_e
    late = jnp.concatenate([late_l, late_r, crow_ref[2:8, :]], 0)
    late_moved = pick_rows(late, link)
    edge_rows = (
        (jnp.where(first_place, moved[0:1], stack[0:1]), jnp.where(last_place, moved[1:2], stack[1:2])),
        (jnp.where(first_place, late_moved[0:1], late_l), jnp.where(last_place, late_moved[1:2], late_r)),
    )
    shift_0 = courant * toward_c * edge_rows[0][0]
    shift_e = courant * (1.0 - toward_c) * edge_rows[0][1]
    tops = [
        face(
            own[side][5:6, channels : 2 * channels], got[side][5:6, channels : 2 * channels],
            own[side][4:5, channels : 2 * channels], got[side][4:5, channels : 2 * channels],
        )
        for side in range(2)
    ]
    every = one_hot(map_ref[...], 0, channels)
    tops = pick_rows(jnp.concatenate(tops + [crow_ref[2:8, :]], 0), every)
    wall_0, wall_e = crow_ref[3:4, :], crow_ref[4:5, :]
    add_0 = (
        courant * toward_c * edge_rows[1][0]
        + ((1.0 - courant) - heat_gain * wall_0) * shift_0
        + heat_gain * wall_0 * tops[0:1]
    )
    add_e = (
        courant * (1.0 - toward_c) * edge_rows[1][1]
        + ((1.0 - courant) - heat_gain * wall_e) * shift_e
        + heat_gain * wall_e * tops[1:2]
    )
    wide_row = lax.broadcasted_iota(jnp.int32, (TILE, channels), 0)
    chooser = one_hot(map_ref[...], group * rows, rows)
    edge_y = pick(chooser, jnp.where(wide_row == 0, shift_0, shift_e), ((1,), (1,)))
    adds = jnp.where(wide_row == 0, add_0, jnp.where(wide_row == 1, courant * toward_c * shift_0, add_e))
    adds = jnp.where(wide_row == TILE - 2, courant * (1.0 - toward_c) * shift_e, adds)
    turn_ref[0:channels, :] = adds.T
    turn_ref[channels:, :] = jnp.broadcast_to(map_ref[...].astype(F32), (TILE, channels)).T
    add_ref[0:rows, :] = turn_ref[pl.ds(pl.multiple_of(group * rows, 8), rows), :]
    add_ref[rows:, :] = turn_ref[pl.ds(pl.multiple_of(channels + group * rows, 8), rows), :]
    pad = [jnp.zeros((rows, cols - 2 * TILE), F32)] if cols > 2 * TILE else []
    flow = flow_ref[...] + jnp.concatenate(
        [jnp.where(lane == 0, edge_y, 0.0)] + pad + [jnp.where(lane == TILE - 1, edge_y, 0.0)], 1
    )
    flux = fw_ref[rows:, :] * (full_ref[0] - flow)

    row8 = lax.broadcasted_iota(jnp.int32, (8, cols), 0)

    def emit(z, temp, cond, heat):
        result = temp + heat + time_step * power_ref[z]
        if z == 0:
            result = result - time_step * flux
        halo_t = xt_ref[z * rows : (z + 1) * rows, :]
        halo_c = xc_ref[z * rows : (z + 1) * rows, :]
        sides = []
        for start, at in ((0, 0), (cols - TILE, TILE - 1)):
            part = slice(start, start + TILE)
            extra = face(cond[:, part], halo_c, temp[:, part], halo_t)
            sides.append(jnp.where(lane == at, extra, 0.0))
        middle = [jnp.zeros((rows, cols - 2 * TILE), F32)] if cols > 2 * TILE else []
        result = result + jnp.concatenate([sides[0]] + middle + [sides[1]], 1)
        early = layers - tail_ref.shape[0]
        target, at_z = (out_ref, z) if z < early else (tail_ref, z - early)
        target[at_z] = result
        for side, opened, start, at in ((0, low_open, 0, 0), (1, high_open, rows - 8, 7)):
            part = slice(start, start + 8)
            extra = opened * face(
                cond[part], halo[side][1][z : z + 1], temp[part], halo[side][0][z : z + 1]
            )
            target[at_z, part, :] = result[part] + jnp.where(row8 == at, extra, 0.0)
        if z < early:
            copies.append(pltpu.make_async_copy(out_ref.at[z], out_hbm.at[z], out_sem.at[z]))
            copies[-1].start()

    copies = []
    closed_heat(full_ref, kappa_ref, slope_ref, emit)
    for copy in copies:
        copy.wait()


def return_kernel(
    part_hbm, tail_ref, own_ref, cross_ref, core_ref, relay_ref, add_ref,
    out_hbm, flow_hbm, all_ref, out_ref, sem,
):
    rows, cols = out_ref.shape
    layers, late = out_hbm.shape[0], tail_ref.shape[0]
    tail = pltpu.make_async_copy(tail_ref, out_hbm.at[layers - late : layers], sem.at[0])
    tail.start()
    group, groups = lax.axis_index("grp"), lax.axis_size("grp")
    beside = group + 1 - 2 * lax.rem(group, 2)
    for ref, owner in (
        (own_ref, group), (core_ref, beside), (cross_ref, groups - 1 - group), (relay_ref, groups - 1 - beside),
    ):
        all_ref[pl.ds(pl.multiple_of(owner * rows, 8), rows), :] = ref[...]
    lane = lax.broadcasted_iota(jnp.int32, (rows, TILE), 1)
    adds, row = add_ref[0:rows, :], add_ref[rows:, :]
    channels = groups * rows
    chooser = jnp.concatenate(
        [jnp.where(row == (lane + start).astype(F32), 1.0, 0.0) for start in range(0, channels, TILE)], 1
    ).astype(BF16)
    flow = pick(chooser, all_ref[...], ((1,), (0,)))
    pad = [jnp.zeros((rows, cols - 2 * TILE), F32)] if cols > 2 * TILE else []
    out_ref[...] = flow + jnp.concatenate(
        [jnp.where(lane < 2, adds, 0.0)] + pad + [jnp.where(lane >= TILE - 2, adds, 0.0)], 1
    )
    back = pltpu.make_async_copy(out_ref, flow_hbm, sem.at[1])
    back.start()
    tail.wait()
    back.wait()


def pairs(count, first, closed):
    swaps = []
    for low in range(first, count, 2):
        high = low + 1
        if high == count:
            if not closed:
                continue
            high = 0
        swaps += [(low, high), (high, low)]
    return swaps


def shards(
    solid_temp, kappa, slope, power, coolant_temp, wall_coeff, channel_map, flow_dir, loop_link
):
    groups, places = lax.axis_size("grp"), lax.axis_size("loop")
    layers, rows, cols = solid_temp.shape
    channels = groups * rows
    strip = layers * rows
    params = pltpu.CompilerParams(vmem_limit_bytes=48 * 1024 * 1024)

    def shape(*dims):
        return jax.ShapeDtypeStruct(dims, F32)

    def call(body, outs, scratch, *args, far=0, outs_far=0, cost=None, alias={}):
        return pl.pallas_call(
            body,
            out_shape=outs,
            in_specs=[pl.BlockSpec(memory_space=pltpu.HBM)] * far + [pl.BlockSpec(memory_space=pltpu.VMEM)] * (len(args) - far),
            out_specs=[pl.BlockSpec(memory_space=pltpu.HBM)] * outs_far
            + [pl.BlockSpec(memory_space=pltpu.VMEM)] * (len(outs) - outs_far),
            scratch_shapes=scratch,
            compiler_params=params,
            cost_estimate=cost,
            input_output_aliases=alias,
        )(*[pltpu.with_memory_space_constraint(arg, pltpu.HBM) for arg in args[:far]], *args[far:])

    def vmem(*dims):
        return pltpu.VMEM(dims, F32)

    heavy = pl.CostEstimate(
        flops=30 * layers * rows * cols, bytes_accessed=36 * layers * rows * cols, transcendentals=0
    )
    block = shape(layers, rows, cols)
    share = shape(2 * rows + 8, cols)
    wide = shape(2 * rows + 8 + 4 * layers, cols)
    index = jax.ShapeDtypeStruct((1, channels), jnp.int32)
    core, cross, step, map_row, link_row = call(
        pack_kernel,
        (wide, share, shape(4 * layers, cols), index, index),
        [
            vmem(layers, 8, cols), vmem(layers, 8, cols), vmem(layers, 8, cols), vmem(layers, 8, cols),
            vmem(3, rows, cols), vmem(TILE, TILE), vmem(8, cols), pltpu.VMEM((1, rows), jnp.int32),
            pltpu.SemaphoreType.DMA((4, 2)), pltpu.SemaphoreType.DMA((3,)), pltpu.SemaphoreType.DMA((2,)),
            pltpu.SemaphoreType.DMA((3,)),
        ],
        solid_temp, kappa, slope, power, coolant_temp, wall_coeff, flow_dir.reshape(1, rows),
        channel_map, loop_link.reshape(1, channels),
        far=9,
    )
    beside = [(i, i + 1 - 2 * (i % 2)) for i in range(groups)]
    across = [(i, groups - 1 - i) for i in range(groups)]
    got_cross = lax.ppermute(cross, "grp", across)
    got_step = lax.ppermute(step, "grp", pairs(groups, 1, False))
    got_core = lax.ppermute(core, "grp", beside)
    first, temp, kappa, slope, power = call(
        open_kernel,
        (block, block, block, block, block),
        [pltpu.SemaphoreType.DMA((4, layers // CHUNK))],
        solid_temp, kappa, slope, power, map_row,
        far=4,
        cost=heavy,
    )
    got_cross, got_step, first = lax.optimization_barrier((got_cross, got_step, first))
    relay = lax.ppermute(got_cross, "grp", beside)
    after, yo, line = call(
        edge_kernel,
        (block, shape(8 * layers, cols), shape(16, strip)),
        [vmem(strip, TILE), vmem(TILE, TILE)],
        first, temp, kappa, slope, got_core, got_step,
        cost=heavy,
    )
    after, yo, sa, sb, fw, crow = call(
        select_kernel,
        (
            block, shape(8 * layers, cols), shape(16, strip + strip // 3), shape(16, strip + strip // 3),
            shape(2 * rows, cols), shape(8, channels),
        ),
        [vmem(channels, 2 * cols), vmem(TILE, TILE)],
        after, yo, line, temp, core, got_core, got_cross, relay, map_row,
        alias={0: 0, 1: 1},
    )
    ra = lax.ppermute(sa, "loop", pairs(places, 0, True))
    rb = lax.ppermute(sb, "loop", pairs(places, 1, True))
    flow1, flow = call(
        coolant_kernel, (shape(rows, cols), shape(rows, cols)), [], fw, temp, after, crow, map_row,
    )
    got_across = lax.ppermute(flow, "grp", across)
    got_over = lax.ppermute(flow, "grp", [(i, (i + groups // 2) % groups) for i in range(groups)])
    got_beside = lax.ppermute(flow, "grp", beside)
    late = 2 * layers // 3
    out, tail, adds = call(
        close_kernel,
        (block, shape(late, rows, cols), shape(2 * rows, TILE)),
        [
            vmem(TILE, strip), vmem(strip, TILE), vmem(strip, TILE), vmem(strip, TILE),
            vmem(layers, rows, cols), vmem(layers - late, rows, cols), vmem(2 * channels, TILE),
            pltpu.SemaphoreType.DMA((layers - late,)),
        ],
        after, kappa, slope, power, yo, ra, rb, sa, sb, flow1, fw, crow, map_row, link_row,
        outs_far=1,
        cost=heavy,
    )
    return call(
        return_kernel,
        (block, shape(rows, cols)),
        [vmem(channels, cols), vmem(rows, cols), pltpu.SemaphoreType.DMA((2,))],
        out, tail, flow, got_across, got_beside, got_over, adds,
        far=1,
        outs_far=2,
        alias={0: 0},
    )


def solution(mesh):
    block = P(None, "grp", "loop")
    plane = P("grp", "loop")
    return jax.shard_map(
        shards,
        mesh=mesh,
        in_specs=(block, block, block, block, plane, plane, P("loop", None), P("grp"), P()),
        out_specs=(block, plane),
        check_vma=False,
    )
```
